32 devices in a mesh: ctx: 8 (over z, x), head: 4 (over y, core).
Axes of the slice: x: 2, y: 2, z: 4, core: 2. Of those that a mesh axis runs over, the one named last changes fastest.
Arguments:
- feat_in: bfloat16 [2048, 8192], P('ctx', 'head'), may hold values from -6 to 6
- gate_in: bfloat16 [2048, 8192], P('ctx', 'head'), may hold values from -6 to 6
- state_proj: bfloat16 [2048, 256], P('ctx'), may hold values from -1.5 to 1.5
- step_raw: float32 [64, 2048], P('head', 'ctx'), may hold values from -6 to 6
- doc_offset: int32 [2048], P('ctx'), may hold values from 0 to 511, as said below
- feat_taps: float32 [4, 8192], P(None, 'head'), may hold values from -3 to 3
- feat_bias: float32 [8192], P('head'), may hold values from -1.5 to 1.5
- proj_taps: float32 [4, 256], replicated, may hold values from -3 to 3
- proj_bias: float32 [256], replicated, may hold values from -0.6 to 0.6
- step_bias: float32 [64], P('head'), may hold values from -4 to -1
- decay_log: float32 [64], P('head'), may hold values from -13 to -0.7
- skip_gain: float32 [64], P('head'), may hold values from 0.5 to 1.5
- norm_gain: float32 [8192], P('head'), may hold values from 0.1 to 1.9
Outputs:
- mixer_out: bfloat16 [2048, 8192], P('ctx', 'head')
The draws below stay inside these ranges and needn't reach their ends.
Inputs may be any that keep to these rules, and one draw needn't show every extreme that they name: `doc_offset`: the position of each token within its document: 0 at a document's first token, rising by one per token inside it. A document holds at most 512 tokens, and every document but the window's last holds more than 64.
All inputs are finite; a program needn't handle non-finite values.
Results may differ from the reference program's by a relative error of at most 0.006.
Values may be sent and summed in bfloat16 or wider, within the bound.
A program may use at most 64 MiB of HBM per device.

```python
import jax
import jax.numpy as jnp
from jax import lax

HEADS = 64
HEAD_DIM = 128
STATE = 128
CONV = 4
BLK = 256
TOKENS = 2048
DOCMAX = 512


def draw_doc_offset(key, part):
    base_key = jax.random.fold_in(key, 17)
    key_lengths, key_choice = jax.random.split(base_key)
    doc_count = 8 * TOKENS // DOCMAX + 4
    lengths = jax.random.randint(key_lengths, (doc_count,), DOCMAX // 8 + 1, DOCMAX + 1, dtype=jnp.int32)
    chosen = jax.random.randint(key_choice, (), 0, 4, dtype=jnp.int32)
    doc_index = jnp.arange(doc_count, dtype=jnp.int32)
    lengths = jnp.where(doc_index == chosen, DOCMAX, lengths)
    starts = (jnp.cumsum(lengths) - lengths).astype(jnp.int32)
    places = jnp.arange(TOKENS, dtype=jnp.int32)
    owners = (jnp.searchsorted(starts, places, side='right') - 1).astype(jnp.int32)
    return (places - starts[owners]).astype(jnp.int32)


def block_levels(stream_key, shape, cuts, smallest, top_value):
    def one(dim, blocks):
        heights = jax.random.uniform(jax.random.fold_in(jax.random.fold_in(stream_key, 6), dim), (blocks,), jnp.float32, smallest / len(cuts), top_value / len(cuts))
        return jnp.repeat(jnp.exp(heights), shape[dim] // blocks).reshape((-1,) + (1,) * (len(shape) - dim - 1))

    level = one(*cuts[0])
    for cut in cuts[1:]:
        level = level * one(*cut)
    return level


def bell_draw(rng, dims, scale, limit, cuts=(), kind=jnp.bfloat16):
    result = scale * jax.random.normal(rng, dims, jnp.float32)
    if cuts:
        result = result * block_levels(rng, dims, cuts, -0.22, 0.18)
    return jnp.clip(result, -limit, limit).astype(kind)


def setup_inputs(seed: int = 0) -> dict:
    arg_keys = jax.random.split(jax.random.key(seed), 14)
    return {
        "feat_in": bell_draw(arg_keys[0], (TOKENS, HEADS * HEAD_DIM), 1.0, 6.0, ((0, 8), (1, 4))),
        "gate_in": bell_draw(arg_keys[1], (TOKENS, HEADS * HEAD_DIM), 1.0, 6.0, ((0, 8), (1, 4))),
        "state_proj": bell_draw(arg_keys[2], (TOKENS, 2 * STATE), 0.25, 1.5, ((0, 8),)),
        "step_raw": bell_draw(arg_keys[3], (HEADS, TOKENS), 1.0, 6.0, ((0, 4), (1, 8)), jnp.float32),
        "doc_offset": draw_doc_offset(jax.random.fold_in(arg_keys[13], 71), 0),
        "feat_taps": bell_draw(arg_keys[5], (CONV, HEADS * HEAD_DIM), 0.5, 3.0, ((1, 4),), jnp.float32),
        "feat_bias": bell_draw(arg_keys[6], (HEADS * HEAD_DIM,), 0.25, 1.5, ((0, 4),), jnp.float32),
        "proj_taps": bell_draw(arg_keys[7], (CONV, 2 * STATE), 0.5, 3.0, (), jnp.float32),
        "proj_bias": bell_draw(arg_keys[8], (2 * STATE,), 0.1, 0.6, (), jnp.float32),
        "step_bias": jnp.clip(-4.0 + 3.0 * jax.random.uniform(arg_keys[9], (HEADS,), jnp.float32) ** block_levels(arg_keys[9], (HEADS,), ((0, 4),), -0.2, 0.2), -4.0, -1.0),
        "decay_log": jnp.clip(-13.0 + 12.3 * jax.random.uniform(arg_keys[10], (HEADS,), jnp.float32) ** block_levels(arg_keys[10], (HEADS,), ((0, 4),), -0.2, 0.2), -13.0, -0.7),
        "skip_gain": jnp.clip(0.5 + 1.0 * jax.random.uniform(arg_keys[11], (HEADS,), jnp.float32) ** block_levels(arg_keys[11], (HEADS,), ((0, 4),), -0.2, 0.2), 0.5, 1.5),
        "norm_gain": jnp.clip(1.0 + 0.18 * jax.random.normal(arg_keys[12], (HEADS * HEAD_DIM,), jnp.float32), 0.1, 1.9),
    }


def conv_silu(values, kernel_taps, kernel_bias, offsets):
    row_count = values.shape[0]
    tap_count = kernel_taps.shape[0]
    widened = values.astype(jnp.float32)
    summed = jnp.broadcast_to(kernel_bias[None, :], values.shape).astype(jnp.float32)
    for tap_index in range(tap_count):
        tap_lag = tap_count - 1 - tap_index
        shifted = jnp.pad(widened, ((tap_lag, 0), (0, 0)))[:row_count]
        summed = summed + jnp.where((offsets >= tap_lag)[:, None], kernel_taps[tap_index][None, :] * shifted, 0.0)
    return jax.nn.silu(summed).astype(jnp.bfloat16)

def reference(feat_in, gate_in, state_proj, step_raw, doc_offset, feat_taps, feat_bias, proj_taps, proj_bias, step_bias, decay_log, skip_gain, norm_gain):
    conv_proj = conv_silu(state_proj, proj_taps, proj_bias, doc_offset)
    blocks = TOKENS // BLK
    in_proj = conv_proj[:, :STATE].reshape(blocks, BLK, STATE)
    out_proj = conv_proj[:, STATE:].reshape(blocks, BLK, STATE)
    offsets = doc_offset.reshape(blocks, BLK)
    position = jnp.arange(BLK, dtype=jnp.int32)
    causal = position[None, :] <= position[:, None]
    final_row = BLK - 1

    def gated_head(head_index):
        column = (head_index * HEAD_DIM).astype(jnp.int32)
        feat_cols = lax.dynamic_slice_in_dim(feat_in, column, HEAD_DIM, 1)
        taps_cols = lax.dynamic_slice_in_dim(feat_taps, column, HEAD_DIM, 1)
        bias_cols = lax.dynamic_slice_in_dim(feat_bias, column, HEAD_DIM, 0)
        conv_feat = conv_silu(feat_cols, taps_cols, bias_cols, doc_offset)
        raw_row = lax.dynamic_index_in_dim(step_raw, head_index, 0, keepdims=False)
        step_row = jax.nn.softplus(raw_row + step_bias[head_index])
        rate_row = step_row * -jnp.exp(decay_log[head_index])
        skip_value = skip_gain[head_index]

        def one_block(state_in, pieces):
            feat_block, in_block, out_block, rate_block, step_block, offset_block = pieces
            cumulative = jnp.cumsum(rate_block)
            same_doc = causal & (offset_block[:, None] >= position[:, None] - position[None, :])
            scores = jnp.dot(out_block, in_block.T, preferred_element_type=jnp.float32)
            exponent_gap = jnp.where(same_doc, cumulative[:, None] - cumulative[None, :], -jnp.inf)
            weights = (scores * jnp.exp(exponent_gap) * step_block[None, :]).astype(jnp.bfloat16)
            inner_out = jnp.dot(weights, feat_block, preferred_element_type=jnp.float32)
            reaches = offset_block >= position + 1
            lift_factor = jnp.where(reaches, jnp.exp(cumulative), 0.0)
            from_state = jnp.dot(out_block.astype(jnp.float32), state_in.T, precision=lax.Precision.HIGHEST) * lift_factor[:, None]
            ssm_out = inner_out + from_state + skip_value * feat_block.astype(jnp.float32)
            tail_mask = offset_block[final_row] >= final_row - position
            tail_coef = jnp.where(tail_mask, jnp.exp(cumulative[final_row] - cumulative) * step_block, 0.0)
            scaled = (in_block.astype(jnp.float32) * tail_coef[:, None]).astype(jnp.bfloat16)
            contrib = jnp.dot(feat_block.T, scaled, preferred_element_type=jnp.float32)
            keep_factor = jnp.where(reaches[final_row], jnp.exp(cumulative[final_row]), 0.0)
            return (keep_factor * state_in + contrib, ssm_out)
        pieces = (conv_feat.reshape(blocks, BLK, HEAD_DIM), in_proj, out_proj, rate_row.reshape(blocks, BLK), step_row.reshape(blocks, BLK), offsets)
        scanned = lax.scan(one_block, jnp.zeros((HEAD_DIM, STATE), jnp.float32), pieces)
        gate_cols = lax.dynamic_slice_in_dim(gate_in, column, HEAD_DIM, 1).astype(jnp.float32)
        return scanned[1].reshape(TOKENS, HEAD_DIM) * jax.nn.silu(gate_cols)

    def add_squares(carried, head_index):
        gated = gated_head(head_index)
        return (carried + lax.optimization_barrier(jnp.sum(gated * gated, axis=1)), None)
    summed = lax.scan(add_squares, jnp.zeros((TOKENS,), jnp.float32), jnp.arange(HEADS, dtype=jnp.int32))
    scale = lax.rsqrt(summed[0] / (HEADS * HEAD_DIM) + 1e-05)

    def finish(head_index):
        gated = gated_head(head_index)
        gain_cols = lax.dynamic_slice_in_dim(norm_gain, (head_index * HEAD_DIM).astype(jnp.int32), HEAD_DIM, 0)
        return (gated * scale[:, None] * gain_cols[None, :]).astype(jnp.bfloat16)
    normed = lax.map(finish, jnp.arange(HEADS, dtype=jnp.int32))
    return jnp.transpose(normed, (1, 0, 2)).reshape(TOKENS, HEADS * HEAD_DIM)
```

```python
import functools

import jax
import jax.numpy as jnp
from jax import lax
from jax.experimental import pallas as pl
from jax.experimental.pallas import tpu as pltpu
from jax.sharding import PartitionSpec as P


def passed_along(block, axis, distance):
    devices = range(lax.axis_size(axis))
    route = [(i - distance, i) for i in devices if i - distance in devices]
    return lax.ppermute(block, axis, route)


def causal_taps(values, rim_rows, kernel_taps, kernel_bias, offsets):
    row_count = values.shape[0]
    tap_count = kernel_taps.shape[0]
    joined = jnp.concatenate([rim_rows, values], axis=0).astype(jnp.float32)
    summed = jnp.broadcast_to(kernel_bias[None, :], values.shape)
    for tap_index in range(tap_count):
        tap_lag = tap_count - 1 - tap_index
        window_rows = lax.slice_in_dim(joined, tap_index, tap_index + row_count, axis=0)
        summed = summed + jnp.where(
            (offsets >= tap_lag)[:, None], kernel_taps[tap_index][None, :] * window_rows, 0.0
        )
    return jax.nn.silu(summed).astype(jnp.bfloat16)


def combine_states(earlier_part, later_part):
    return (
        earlier_part[0] * later_part[0],
        later_part[0][:, None, None] * earlier_part[1] + later_part[1],
    )


def body(
    feat_in,
    gate_in,
    state_proj,
    step_raw,
    doc_offset,
    feat_taps,
    feat_bias,
    proj_taps,
    proj_bias,
    step_bias,
    decay_log,
    skip_gain,
    norm_gain,
):
    head_count = step_raw.shape[0]
    row_count = feat_in.shape[0]
    head_dim = feat_in.shape[1] // head_count
    state_size = state_proj.shape[1] // 2
    tap_count = feat_taps.shape[0]
    rim_feat, rim_proj = passed_along(
        (feat_in[row_count - tap_count + 1 :], state_proj[row_count - tap_count + 1 :]), "ctx", 1
    )
    conv_feat = causal_taps(feat_in, rim_feat, feat_taps, feat_bias, doc_offset)
    conv_proj = causal_taps(state_proj, rim_proj, proj_taps, proj_bias, doc_offset)
    step_all = jax.nn.softplus(step_raw + step_bias[:, None])
    rate_all = step_all * (-jnp.exp(decay_log))[:, None]
    block_rows = min(512, row_count)
    position = jnp.arange(block_rows, dtype=jnp.int32)
    causal = position[None, :] <= position[:, None]
    final_row = block_rows - 1
    element_decay = jnp.ones((head_count,), jnp.float32)
    element_state = jnp.zeros((head_count, head_dim, state_size), jnp.float32)
    block_index = 0
    start = block_index * block_rows
    feat_block = conv_feat.reshape(block_rows, head_count, head_dim)
    in_block = conv_proj[start : start + block_rows, :state_size]
    out_block = conv_proj[start : start + block_rows, state_size:]
    cumulative = jnp.cumsum(rate_all, axis=1)
    same_doc = causal & (doc_offset[:, None] >= position[:, None] - position[None, :])
    scores = jnp.dot(out_block, in_block.T, preferred_element_type=jnp.float32)
    exponent_gap = jnp.where(
        same_doc[None], cumulative[:, :, None] - cumulative[:, None, :], -jnp.inf
    )
    weights = (scores[None] * jnp.exp(exponent_gap) * step_all[:, None, :]).astype(jnp.bfloat16)
    inner_out = jnp.einsum("hts,shp->thp", weights, feat_block, preferred_element_type=jnp.float32)
    reaches = doc_offset >= position + 1
    tail_mask = doc_offset[final_row] >= final_row - position
    tail_coef = jnp.where(
        tail_mask[None, :],
        jnp.exp(cumulative[:, final_row : final_row + 1] - cumulative) * step_all,
        0.0,
    )
    scaled = (in_block.astype(jnp.float32)[None] * tail_coef[:, :, None]).astype(jnp.bfloat16)
    contrib = jnp.einsum("shp,hsn->hpn", feat_block, scaled, preferred_element_type=jnp.float32)
    keep_factor = jnp.where(reaches[final_row], jnp.exp(cumulative[:, final_row]), 0.0)
    saved_blocks = [(feat_block, out_block, cumulative, reaches, inner_out, contrib, keep_factor)]
    element_state = keep_factor[:, None, None] * element_state + contrib
    element_decay = element_decay * keep_factor
    longest_doc = row_count * lax.axis_size("ctx") // 4
    span_back = (longest_doc + row_count - 2) // row_count
    distances = [1]
    window_size = 1
    while window_size < span_back:
        distances.append(window_size)
        window_size = window_size * 2
    current = (element_decay, element_state)
    for turn_index, distance in enumerate(distances):
        moved = passed_along((current[0], current[1]), "ctx", distance)
        if turn_index == 0:
            current = moved
        else:
            current = combine_states(moved, current)
    start_state = current[1]
    pieces_out = []
    for block_index, saved in enumerate(saved_blocks):
        feat_block, out_block, cumulative, reaches, inner_out, contrib, keep_factor = saved
        lift_factor = jnp.where(reaches[None, :], jnp.exp(cumulative), 0.0)
        from_state = (
            jnp.einsum(
                "tn,hpn->thp",
                out_block.astype(jnp.float32),
                start_state,
                precision=lax.Precision.HIGHEST,
            )
            * lift_factor.T[:, :, None]
        )
        pieces_out.append(
            inner_out + from_state + skip_gain[None, :, None] * feat_block.astype(jnp.float32)
        )
    mixed = pieces_out[0].reshape(row_count, head_count * head_dim)
    gated = mixed * jax.nn.silu(gate_in.astype(jnp.float32))
    squares = jnp.sum(gated * gated, axis=1)
    total_squares = lax.psum(squares, "head")
    scale = lax.rsqrt(total_squares / (head_count * head_dim * lax.axis_size("head")) + 1e-05)
    return (gated * scale[:, None] * norm_gain[None, :]).astype(jnp.bfloat16)


PAIR = 2
LAG = 2
EARLY = 8
GATED = jnp.bfloat16

LOG2E = 1.4426950408889634
F32 = jnp.float32
BF16 = jnp.bfloat16
EXACT = lax.Precision.HIGHEST


def to_column(row, size):
    rows = lax.broadcasted_iota(jnp.int32, (size, size), 0)
    cols = lax.broadcasted_iota(jnp.int32, (size, size), 1)
    return jnp.sum(jnp.where(rows == cols, row, 0.0), axis=1, keepdims=True)


def tap_sum(window_of, taps, bias, offsets, tap_count):
    summed = bias
    for tap_index in range(tap_count):
        tap_lag = tap_count - 1 - tap_index
        term = taps[tap_index : tap_index + 1, :] * window_of(tap_lag)
        if tap_lag:
            term = jnp.where(offsets >= float(tap_lag), term, 0.0)
        summed = summed + term
    return summed * (1.0 / (1.0 + jnp.exp(-summed)))


def mixer_kernel(
    ctx_size, head_size, pair,
    feat_hbm, gate_hbm, proj_hbm, step_ref, offset_ref, offset_smem, taps_ref, bias_ref,
    ptaps_ref, pbias_ref, sbias_ref, dlog_ref, skip_smem,
    gated_hbm, scale_ref,
    feat, gate, proj, xs, xp, rim, prim, conv, in_t, bc, out_b, masked, cb, a_rows, coef,
    offs, own, send, arecv, srecv, sout, lsend, lrecv, kown, kin, yv, g2, gated, part, sq, sqr,
    feat_sems, gate_sems, out_sems, proj_sem, halo_send, halo_recv, keep_sems,
    asend, arecv_sem, ssend, srecv_sem, fsend, lrecv_sem, sqsend, sqrecv,
):
    d = lax.axis_index("ctx")
    hd = lax.axis_index("head")
    rows, cols = feat.shape
    heads = step_ref.shape[0]
    hdim = cols // heads
    state = in_t.shape[0]
    taps_n = taps_ref.shape[0]
    width = pair * hdim
    chunks = heads // pair
    half = rows // 2
    odd = d % 2 == 1
    even = d % 2 == 0
    parity = d % 2
    mate = d + 1 - 2 * parity
    part_chunks = heads // pair // 2
    mine = parity * part_chunks
    theirs = part_chunks - mine
    sends_early = even | (d + 1 < ctx_size)
    gets_early = odd | (d + 2 < ctx_size)
    sends_late = even | (d >= 2)
    gets_late = odd | (d >= 2)

    def chunk_cols(c):
        return pl.ds(pl.multiple_of(c * width, width), width)

    def feat_copy(c):
        return pltpu.make_async_copy(feat_hbm.at[:, chunk_cols(c)], feat.at[:, chunk_cols(c)], feat_sems.at[c])

    def gate_copy(c):
        return pltpu.make_async_copy(gate_hbm.at[:, chunk_cols(c)], gate.at[:, chunk_cols(c)], gate_sems.at[c])

    def out_copy(c):
        return pltpu.make_async_copy(gated.at[:, chunk_cols(c)], gated_hbm.at[:, chunk_cols(c)], out_sems.at[c])

    def remote(src, dst, ssem, rsem, where):
        return pltpu.make_async_remote_copy(
            src_ref=src, dst_ref=dst, send_sem=ssem, recv_sem=rsem,
            device_id=where, device_id_type=pl.DeviceIdType.MESH,
        )

    barrier = pltpu.get_barrier_semaphore()
    for shift in (-2, -1, 1, 2):
        @pl.when((d + shift >= 0) & (d + shift < ctx_size))
        def _():
            pl.semaphore_signal(barrier, inc=1, device_id=(d + shift, hd), device_id_type=pl.DeviceIdType.MESH)
    for k in range(1, head_size):
        pl.semaphore_signal(
            barrier, inc=1, device_id=(d, lax.rem(hd + k, head_size)), device_id_type=pl.DeviceIdType.MESH
        )

    proj_copy = pltpu.make_async_copy(proj_hbm, proj, proj_sem)
    proj_copy.start()
    for c in range(chunks):
        feat_copy(c).start()
    for c in range(chunks):
        gate_copy(c).start()

    off_col = to_column(offset_ref[...].astype(F32), rows)
    offs[...] = jnp.broadcast_to(off_col, offs.shape)
    step = jax.nn.softplus(step_ref[...] + to_column(sbias_ref[...], heads))
    rate = step * (-jnp.exp(to_column(dlog_ref[...], heads)) * LOG2E)
    near = jnp.minimum(d, 2) + jnp.minimum(ctx_size - 1 - d, 2) + head_size - 1
    pl.semaphore_wait(barrier, near)
    halo_f = remote(feat_hbm.at[pl.ds(rows - 8, 8), :], rim, halo_send.at[0], halo_recv.at[0], (d + 1, hd))
    halo_p = remote(proj_hbm.at[pl.ds(rows - 8, 8), :], prim, halo_send.at[1], halo_recv.at[1], (d + 1, hd))

    @pl.when(d + 1 < ctx_size)
    def _():
        halo_p.start()
        halo_f.start()

    @pl.when(d == 0)
    def _():
        rim[...] = jnp.zeros_like(rim)
        prim[...] = jnp.zeros_like(prim)

    @pl.when(d < 2)
    def _():
        srecv[...] = jnp.zeros_like(srecv)

    @pl.when(d == 0)
    def _():
        lrecv[...] = jnp.zeros_like(lrecv)

    upper = (
        lax.broadcasted_iota(jnp.int32, (rows, rows), 0) <= lax.broadcasted_iota(jnp.int32, (rows, rows), 1)
    ).astype(F32)
    cum = jnp.dot(rate, upper, precision=EXACT, preferred_element_type=F32)
    shifted = cum - jnp.log(step) * LOG2E
    a_rows[...] = shifted
    last = offset_smem[rows - 1]
    place = lax.broadcasted_iota(jnp.int32, (heads, rows), 1)
    coef[...] = jnp.where(last >= rows - 1 - place, jnp.exp2(cum[:, rows - 1 : rows] - shifted), 0.0)
    keep = jnp.where(last >= rows, jnp.exp2(cum[:, rows - 1 : rows]), 0.0)
    cum_t = cum.T
    for h in range(heads):
        cb[h] = jnp.broadcast_to(cum_t[:, h : h + 1], (rows, hdim))
        kown[:, h * hdim : (h + 1) * hdim] = jnp.broadcast_to(keep[h : h + 1, :], (1, hdim))

    keep_msg = remote(kown, kin, keep_sems.at[0], keep_sems.at[1], (mate, hd))
    keep_msg.start()

    def conv_main(c):
        feat_copy(c).wait()
        sl = chunk_cols(c)
        xs[8:, sl] = feat[:, sl].astype(F32)
        conv[16:, sl] = tap_sum(
            lambda lag: xs[24 - lag : 8 + rows - lag, sl], taps_ref[:, sl], bias_ref[:, sl], offs[16:, :1], taps_n
        ).astype(BF16)

    def conv_top(c):
        sl = chunk_cols(c)
        xs[:8, sl] = rim[:, sl].astype(F32)
        conv[:16, sl] = tap_sum(
            lambda lag: xs[8 - lag : 24 - lag, sl], taps_ref[:, sl], bias_ref[:, sl], offs[:16, :1], taps_n
        ).astype(BF16)

    def ordered(i):
        return lax.rem(mine + i, chunks)

    def early_body(c, _):
        conv_main(ordered(c))
        return 0

    proj_copy.wait()
    xp[8:, :] = proj[...].astype(F32)
    cp = tap_sum(
        lambda lag: xp[24 - lag : 8 + rows - lag, :], ptaps_ref[...], pbias_ref[...], offs[16:, :1], taps_n
    ).astype(BF16)
    bc[16:, :] = cp
    lax.fori_loop(0, min(EARLY // pair, chunks), early_body, 0)

    @pl.when(d > 0)
    def _():
        halo_p.wait_recv()
        halo_f.wait_recv()

    xp[:8, :] = prim[...].astype(F32)
    bc[:16, :] = tap_sum(
        lambda lag: xp[8 - lag : 24 - lag, :], ptaps_ref[...], pbias_ref[...], offs[:16, :1], taps_n
    ).astype(BF16)
    in_b = bc[:, :state]
    in_t[...] = in_b.astype(F32).T
    out_b[...] = bc[:, state:]

    def contrib(c):
        conv_top(c)
        for k in range(pair):
            h = c * pair + k
            scaled = (in_t[...] * coef[pl.ds(h, 1), :]).astype(BF16)
            fcols = pl.ds(pl.multiple_of(h * hdim, hdim), hdim)
            got = jnp.dot(scaled, conv[:, fcols], preferred_element_type=F32)
            own[c, :, k * hdim : (k + 1) * hdim] = got
            send[c, :, k * hdim : (k + 1) * hdim] = got.astype(BF16)

        @pl.when(sends_early & (c >= mine) & (c < mine + part_chunks))
        def _():
            a_copy(c - mine).start()

    def contrib_body(i, _):
        contrib(ordered(i))
        return 0

    def late_body(i, _):
        conv_main(ordered(i))
        contrib(ordered(i))
        return 0

    def a_copy(r):
        return remote(send.at[mine + r], arecv.at[r], asend.at[r], arecv_sem.at[r], (mate, hd))

    def s_copy(r):
        return remote(sout.at[r], srecv.at[r], ssend.at[r], srecv_sem.at[r], (d + 2, hd))

    def f_copy(r):
        return remote(lsend.at[r], lrecv.at[r], fsend.at[r], lrecv_sem.at[r], (mate, hd))

    def g_copy(r):
        return remote(srecv.at[r], lrecv.at[r], fsend.at[r], lrecv_sem.at[r], (mate, hd))

    lax.fori_loop(0, min(EARLY // pair, chunks), contrib_body, 0)
    lax.fori_loop(min(EARLY // pair, chunks), chunks, late_body, 0)
    scores = lax.dot_general(out_b[...], in_b, (((1,), (1,)), ((), ())), preferred_element_type=F32)
    ti = lax.broadcasted_iota(jnp.int32, (rows, rows), 0)
    si = lax.broadcasted_iota(jnp.int32, (rows, rows), 1)
    gap = ti - si
    masked[...] = jnp.where((gap >= 0) & (offs[:, :1] >= gap.astype(F32)), scores, 0.0)
    part[...] = jnp.zeros_like(part)

    def local_part(c):
        gate_copy(c).wait()
        for k in range(pair):
            h = c * pair + k
            fcols = pl.ds(pl.multiple_of(h * hdim, hdim), hdim)
            arow = a_rows[pl.ds(h, 1), :]
            cbv = cb[h]
            w0 = (jnp.exp2(jnp.minimum(cbv - arow[:, :half], 126.0)) * masked[:, :half]).astype(BF16)
            w1 = (jnp.exp2(jnp.minimum(cbv[half:] - arow[:, half:], 126.0)) * masked[half:, half:]).astype(BF16)
            fv = conv[:, fcols]
            first = jnp.dot(w0, fv[:half], preferred_element_type=F32)
            second = jnp.dot(w1, fv[half:], preferred_element_type=F32)
            inner = jnp.concatenate([first[:half], first[half:] + second], axis=0)
            gv = gate[:, fcols].astype(F32)
            sg = gv * (1.0 / (1.0 + jnp.exp(-gv)))
            yv[:, fcols] = (inner + skip_smem[h] * fv.astype(F32)) * sg
            tpos = lax.broadcasted_iota(jnp.int32, (rows, hdim), 0)
            lift = jnp.where(offs[...] >= (tpos + 1).astype(F32), jnp.exp2(cbv), 0.0)
            g2[:, fcols] = lift * sg

    def relay(r):
        c = theirs + r
        sl = chunk_cols(c)

        @pl.when(gets_early)
        def _():
            a_copy(r).wait_recv()

        @pl.when((d + 2 < ctx_size) & even)
        def _():
            sout[r] = (arecv[r].astype(F32) + kin[:, sl] * own[c]).astype(BF16)
            s_copy(r).start()

        @pl.when((d + 2 < ctx_size) & odd)
        def _():
            sout[r] = (own[c] + kown[:, sl] * arecv[r].astype(F32)).astype(BF16)
            s_copy(r).start()

    def finish(c, st):
        sl = chunk_cols(c)
        fs = jnp.dot(out_b[...], st, preferred_element_type=F32)
        gt = yv[:, sl] + fs * g2[:, sl]
        gated[:, sl] = gt.astype(gated.dtype)
        squares = gt * gt
        total = squares[:, :hdim]
        for k in range(1, pair):
            total = total + squares[:, k * hdim : (k + 1) * hdim]
        part[...] += total
        out_copy(c).start()

    def pass_on(r):
        c = theirs + r
        sl = chunk_cols(c)

        @pl.when(d >= 2)
        def _():
            s_copy(r).wait_recv()

        @pl.when(even)
        def _():
            lsend[r] = (own[c] + kown[:, sl] * srecv[r].astype(F32)).astype(BF16)
            f_copy(r).start()
            finish(c, srecv[r])

        @pl.when(odd)
        def _():
            @pl.when(d >= 2)
            def _():
                g_copy(r).start()

            finish(c, (arecv[r].astype(F32) + kin[:, sl] * srecv[r].astype(F32)).astype(BF16))

    lag = min(LAG, part_chunks)

    keep_msg.wait_recv()

    def main_body(i, _):
        @pl.when(i < part_chunks)
        def _():
            local_part(2 * i)
            relay(i)
            local_part(2 * i + 1)

        @pl.when(i >= lag)
        def _():
            pass_on(i - lag)

        return 0

    lax.fori_loop(0, part_chunks + lag, main_body, 0)

    def last_body(r, _):
        @pl.when(gets_late)
        def _():
            f_copy(r).wait_recv()

        finish(mine + r, lrecv[r])
        return 0

    lax.fori_loop(0, part_chunks, last_body, 0)

    ones = jnp.ones((8, hdim), F32)
    sq[...] = lax.dot_general(ones, part[...], (((1,), (1,)), ((), ())), precision=EXACT, preferred_element_type=F32)[:1]

    def sq_copy(k):
        return remote(
            sq, sqr.at[k - 1], sqsend.at[k - 1], sqrecv.at[k - 1], (d, lax.rem(hd + k, head_size))
        )

    for k in range(1, head_size):
        sq_copy(k).start()
    total = sq[...]
    for k in range(1, head_size):
        sq_copy(k).wait_recv()
        total = total + sqr[k - 1]
    scale = lax.rsqrt(total / (cols * head_size) + 1e-05)
    scale_ref[...] = jnp.broadcast_to(to_column(scale, rows), scale_ref.shape)

    for k in range(1, head_size):
        sq_copy(k).wait_send()

    @pl.when(d + 1 < ctx_size)
    def _():
        halo_p.wait_send()
        halo_f.wait_send()

    keep_msg.wait_send()

    def drain(r, _):
        out_copy(2 * r).wait()
        out_copy(2 * r + 1).wait()

        @pl.when(sends_early)
        def _():
            a_copy(r).wait_send()

        @pl.when(d + 2 < ctx_size)
        def _():
            s_copy(r).wait_send()

        @pl.when(sends_late)
        def _():
            f_copy(r).wait_send()

        return 0

    lax.fori_loop(0, part_chunks, drain, 0)


STRIPE = 32


def scale_kernel(gated_ref, scale_ref, gain_ref, out_hbm, staged, sems):
    rows, cols = staged.shape
    lanes = scale_ref.shape[1]
    stripe = min(STRIPE, rows)

    def out_copy(r):
        rs = pl.ds(r * stripe, stripe)
        return pltpu.make_async_copy(staged.at[rs, :], out_hbm.at[rs, :], sems.at[r])

    for r in range(rows // stripe):
        rs = slice(r * stripe, (r + 1) * stripe)
        scale = scale_ref[rs, :]
        for c in range(cols // lanes):
            cs = slice(c * lanes, (c + 1) * lanes)
            staged[rs, cs] = (gated_ref[rs, cs].astype(F32) * scale * gain_ref[:, cs]).astype(BF16)
        out_copy(r).start()
    for r in range(rows // stripe):
        out_copy(r).wait()


def finish_call(gated, scale, gain):
    rows, cols = gated.shape
    vm = pl.BlockSpec(memory_space=pltpu.VMEM)
    return pl.pallas_call(
        scale_kernel,
        out_shape=jax.ShapeDtypeStruct((rows, cols), BF16),
        in_specs=[vm, vm, vm],
        out_specs=pl.BlockSpec(memory_space=pltpu.HBM),
        scratch_shapes=[
            pltpu.VMEM((rows, cols), BF16), pltpu.SemaphoreType.DMA((rows // min(STRIPE, rows),)),
        ],
        compiler_params=pltpu.CompilerParams(vmem_limit_bytes=8 << 20),
        name="scale",
    )(gated, scale, gain)


def short_body(
    feat_in, gate_in, state_proj, step_raw, doc_offset, feat_taps, feat_bias,
    proj_taps, proj_bias, step_bias, decay_log, skip_gain, norm_gain,
):
    heads, rows = step_raw.shape
    cols = feat_in.shape[1]
    hdim = cols // heads
    state = state_proj.shape[1] // 2
    ctx_size = lax.axis_size("ctx")
    head_size = lax.axis_size("head")
    pair = PAIR
    chunks = heads // pair
    width = pair * hdim
    vm = pl.BlockSpec(memory_space=pltpu.VMEM)
    sm = pl.BlockSpec(memory_space=pltpu.SMEM)
    anywhere = pl.BlockSpec(memory_space=pl.ANY)
    hbm = pl.BlockSpec(memory_space=pltpu.HBM)
    V = pltpu.VMEM
    DMA = pltpu.SemaphoreType.DMA
    gated, scale = pl.pallas_call(
        functools.partial(mixer_kernel, ctx_size, head_size, pair),
        out_shape=(
            jax.ShapeDtypeStruct((rows, cols), GATED),
            jax.ShapeDtypeStruct((rows, hdim), F32),
        ),
        in_specs=[hbm, hbm, hbm, vm, vm, sm, vm, vm, vm, vm, vm, vm, sm],
        out_specs=(anywhere, vm),
        scratch_shapes=[
            V((rows, cols), BF16), V((rows, cols), BF16), V((rows, 2 * state), BF16),
            V((rows + 8, cols), F32), V((rows + 8, 2 * state), F32),
            V((8, cols), BF16), V((8, 2 * state), BF16), V((rows, cols), BF16),
            V((state, rows), F32), V((rows, 2 * state), BF16), V((rows, state), BF16), V((rows, rows), F32),
            V((heads, rows, hdim), F32), V((heads, rows), F32), V((heads, rows), F32),
            V((rows, hdim), F32), V((chunks, state, width), F32),
            V((chunks, state, width), BF16), V((chunks // 2, state, width), BF16),
            V((chunks // 2, state, width), BF16), V((chunks // 2, state, width), BF16),
            V((chunks // 2, state, width), BF16), V((chunks // 2, state, width), BF16),
            V((1, cols), F32), V((1, cols), F32), V((rows, cols), F32), V((rows, cols), F32),
            V((rows, cols), GATED), V((rows, hdim), F32),
            V((1, rows), F32), V((8, 1, rows), F32),
            DMA((chunks,)), DMA((chunks,)), DMA((chunks,)), DMA, DMA((2,)), DMA((2,)), DMA((2,)),
            *[DMA((chunks // 2,)) for _ in range(6)],
            DMA((head_size - 1,)), DMA((head_size - 1,)),
        ],
        compiler_params=pltpu.CompilerParams(
            collective_id=0, has_side_effects=True, vmem_limit_bytes=40 << 20
        ),
        name="mixer",
    )(*[
        pltpu.with_memory_space_constraint(operand, pltpu.HBM)
        for operand in (
            feat_in, gate_in, state_proj, step_raw, doc_offset[None, :], doc_offset, feat_taps,
            feat_bias[None, :], proj_taps, proj_bias[None, :], step_bias[None, :], decay_log[None, :], skip_gain,
        )
    ])
    return finish_call(gated, scale, norm_gain[None, :])


def solution(mesh):
    ctx_size = mesh.shape["ctx"]

    def chosen(*args):
        row_count = args[0].shape[0]
        longest_doc = row_count * ctx_size // 4
        span_back = (longest_doc + row_count - 2) // row_count
        if span_back == 2 and ctx_size % 2 == 0:
            return short_body(*args)
        return body(*args)

    return jax.shard_map(
        chosen,
        mesh=mesh,
        in_specs=(
            P("ctx", "head"),
            P("ctx", "head"),
            P("ctx", None),
            P("head", "ctx"),
            P("ctx"),
            P(None, "head"),
            P("head"),
            P(),
            P(),
            P("head"),
            P("head"),
            P("head"),
            P("head"),
        ),
        out_specs=P("ctx", "head"),
        check_vma=False,
    )
```

```python
import functools

import jax
import jax.numpy as jnp
from jax import lax
from jax.experimental import pallas as pl
from jax.experimental.pallas import tpu as pltpu
from jax.sharding import PartitionSpec as P


def passed_along(block, axis, distance):
    devices = range(lax.axis_size(axis))
    route = [(i - distance, i) for i in devices if i - distance in devices]
    return lax.ppermute(block, axis, route)


def causal_taps(values, rim_rows, kernel_taps, kernel_bias, offsets):
    row_count = values.shape[0]
    tap_count = kernel_taps.shape[0]
    joined = jnp.concatenate([rim_rows, values], axis=0).astype(jnp.float32)
    summed = jnp.broadcast_to(kernel_bias[None, :], values.shape)
    for tap_index in range(tap_count):
        tap_lag = tap_count - 1 - tap_index
        window_rows = lax.slice_in_dim(joined, tap_index, tap_index + row_count, axis=0)
        summed = summed + jnp.where(
            (offsets >= tap_lag)[:, None], kernel_taps[tap_index][None, :] * window_rows, 0.0
        )
    return jax.nn.silu(summed).astype(jnp.bfloat16)


def combine_states(earlier_part, later_part):
    return (
        earlier_part[0] * later_part[0],
        later_part[0][:, None, None] * earlier_part[1] + later_part[1],
    )


def body(
    feat_in,
    gate_in,
    state_proj,
    step_raw,
    doc_offset,
    feat_taps,
    feat_bias,
    proj_taps,
    proj_bias,
    step_bias,
    decay_log,
    skip_gain,
    norm_gain,
):
    head_count = step_raw.shape[0]
    row_count = feat_in.shape[0]
    head_dim = feat_in.shape[1] // head_count
    state_size = state_proj.shape[1] // 2
    tap_count = feat_taps.shape[0]
    rim_feat, rim_proj = passed_along(
        (feat_in[row_count - tap_count + 1 :], state_proj[row_count - tap_count + 1 :]), "ctx", 1
    )
    conv_feat = causal_taps(feat_in, rim_feat, feat_taps, feat_bias, doc_offset)
    conv_proj = causal_taps(state_proj, rim_proj, proj_taps, proj_bias, doc_offset)
    step_all = jax.nn.softplus(step_raw + step_bias[:, None])
    rate_all = step_all * (-jnp.exp(decay_log))[:, None]
    block_rows = min(512, row_count)
    position = jnp.arange(block_rows, dtype=jnp.int32)
    causal = position[None, :] <= position[:, None]
    final_row = block_rows - 1
    element_decay = jnp.ones((head_count,), jnp.float32)
    element_state = jnp.zeros((head_count, head_dim, state_size), jnp.float32)
    block_index = 0
    start = block_index * block_rows
    feat_block = conv_feat.reshape(block_rows, head_count, head_dim)
    in_block = conv_proj[start : start + block_rows, :state_size]
    out_block = conv_proj[start : start + block_rows, state_size:]
    cumulative = jnp.cumsum(rate_all, axis=1)
    same_doc = causal & (doc_offset[:, None] >= position[:, None] - position[None, :])
    scores = jnp.dot(out_block, in_block.T, preferred_element_type=jnp.float32)
    exponent_gap = jnp.where(
        same_doc[None], cumulative[:, :, None] - cumulative[:, None, :], -jnp.inf
    )
    weights = (scores[None] * jnp.exp(exponent_gap) * step_all[:, None, :]).astype(jnp.bfloat16)
    inner_out = jnp.einsum("hts,shp->thp", weights, feat_block, preferred_element_type=jnp.float32)
    reaches = doc_offset >= position + 1
    tail_mask = doc_offset[final_row] >= final_row - position
    tail_coef = jnp.where(
        tail_mask[None, :],
        jnp.exp(cumulative[:, final_row : final_row + 1] - cumulative) * step_all,
        0.0,
    )
    scaled = (in_block.astype(jnp.float32)[None] * tail_coef[:, :, None]).astype(jnp.bfloat16)
    contrib = jnp.einsum("shp,hsn->hpn", feat_block, scaled, preferred_element_type=jnp.float32)
    keep_factor = jnp.where(reaches[final_row], jnp.exp(cumulative[:, final_row]), 0.0)
    saved_blocks = [(feat_block, out_block, cumulative, reaches, inner_out, contrib, keep_factor)]
    element_state = keep_factor[:, None, None] * element_state + contrib
    element_decay = element_decay * keep_factor
    longest_doc = row_count * lax.axis_size("ctx") // 4
    span_back = (longest_doc + row_count - 2) // row_count
    distances = [1]
    window_size = 1
    while window_size < span_back:
        distances.append(window_size)
        window_size = window_size * 2
    current = (element_decay, element_state)
    for turn_index, distance in enumerate(distances):
        moved = passed_along((current[0], current[1]), "ctx", distance)
        if turn_index == 0:
            current = moved
        else:
            current = combine_states(moved, current)
    start_state = current[1]
    pieces_out = []
    for block_index, saved in enumerate(saved_blocks):
        feat_block, out_block, cumulative, reaches, inner_out, contrib, keep_factor = saved
        lift_factor = jnp.where(reaches[None, :], jnp.exp(cumulative), 0.0)
        from_state = (
            jnp.einsum(
                "tn,hpn->thp",
                out_block.astype(jnp.float32),
                start_state,
                precision=lax.Precision.HIGHEST,
            )
            * lift_factor.T[:, :, None]
        )
        pieces_out.append(
            inner_out + from_state + skip_gain[None, :, None] * feat_block.astype(jnp.float32)
        )
    mixed = pieces_out[0].reshape(row_count, head_count * head_dim)
    gated = mixed * jax.nn.silu(gate_in.astype(jnp.float32))
    squares = jnp.sum(gated * gated, axis=1)
    total_squares = lax.psum(squares, "head")
    scale = lax.rsqrt(total_squares / (head_count * head_dim * lax.axis_size("head")) + 1e-05)
    return (gated * scale[:, None] * norm_gain[None, :]).astype(jnp.bfloat16)


PAIR = 2
LAG = 4
STRIPE = 32

LOG2E = 1.4426950408889634
F32 = jnp.float32
BF16 = jnp.bfloat16


def to_column(row, size):
    rows = lax.broadcasted_iota(jnp.int32, (size, size), 0)
    cols = lax.broadcasted_iota(jnp.int32, (size, size), 1)
    return jnp.sum(jnp.where(rows == cols, row, 0.0), axis=1, keepdims=True)


def tap_sum(window_of, taps, bias, offsets, tap_count):
    summed = bias
    for tap_index in range(tap_count):
        tap_lag = tap_count - 1 - tap_index
        term = taps[tap_index : tap_index + 1, :] * window_of(tap_lag)
        if tap_lag:
            term = jnp.where(offsets >= float(tap_lag), term, 0.0)
        summed = summed + term
    return summed * (1.0 / (1.0 + jnp.exp(-summed)))


def running_sum(values, upper):
    first = values.astype(BF16)
    left = values - first.astype(F32)
    second = left.astype(BF16)
    third = (left - second.astype(F32)).astype(BF16)
    count = values.shape[0]
    sums = jnp.dot(jnp.concatenate([first, second, third], axis=0), upper, preferred_element_type=F32)
    return sums[:count] + sums[count : 2 * count] + sums[2 * count :]


def mixer_kernel(
    ctx_size, head_size, pair,
    feat_hbm, gate_hbm, proj_hbm, step_hbm, offset_hbm, taps_hbm, bias_hbm,
    ptaps_hbm, pbias_hbm, sbias_hbm, dlog_hbm, skip_hbm,
    gated, scale_ref,
    step_ref, offset_ref, taps_ref, bias_ref, ptaps_ref, pbias_ref, sbias_ref, dlog_ref, skip_ref,
    feat, gate, proj, xs, xp, rim, prim, conv, in_t, bc, out_b, masked, cb, a_rows, coef, coef_top,
    offs, skips, own, send, arecv, srecv, sout, lsend, lrecv, kown, kmate, kprev,
    top, tin, ext, xt, yv, g2, part, sq, sqr,
    small_sems, feat_sems, gate_sems, halo_send, halo_recv, keep_send, keep_recv, top_send, top_recv,
    asend, arecv_sem, ssend, srecv_sem, fsend, lrecv_sem, sqsend, sqrecv,
):
    d = lax.axis_index("ctx")
    hd = lax.axis_index("head")
    rows, cols = feat.shape
    heads = step_ref.shape[0]
    hdim = cols // heads
    state = in_t.shape[0]
    taps_n = taps_ref.shape[0]
    edge = taps_n - 1
    width = pair * hdim
    chunks = heads // pair
    half = rows // 2
    odd = d % 2 == 1
    even = d % 2 == 0
    parity = d % 2
    mate = d + 1 - 2 * parity
    part_heads = heads // 2
    part_chunks = chunks // 2
    mine = parity * part_heads
    theirs = part_heads - mine
    sends_early = even | (d + 1 < ctx_size)
    gets_early = odd | (d + 2 < ctx_size)
    sends_late = even | (d >= 2)
    gets_late = odd | (d >= 2)

    def cols_of(h, count):
        return pl.ds(pl.multiple_of(h * hdim, hdim), count * hdim)

    def chunk_cols(c):
        return pl.ds(pl.multiple_of(c * width, width), width)

    def feat_copy(c):
        return pltpu.make_async_copy(feat_hbm.at[:, chunk_cols(c)], feat.at[:, chunk_cols(c)], feat_sems.at[c])

    def gate_copy(c):
        return pltpu.make_async_copy(gate_hbm.at[:, chunk_cols(c)], gate.at[:, chunk_cols(c)], gate_sems.at[c])

    def remote(src, dst, ssem, rsem, where):
        return pltpu.make_async_remote_copy(
            src_ref=src, dst_ref=dst, send_sem=ssem, recv_sem=rsem,
            device_id=where, device_id_type=pl.DeviceIdType.MESH,
        )

    barrier = pltpu.get_barrier_semaphore()
    for shift in (-2, -1, 1, 2):
        @pl.when((d + shift >= 0) & (d + shift < ctx_size))
        def _():
            pl.semaphore_signal(barrier, inc=1, device_id=(d + shift, hd), device_id_type=pl.DeviceIdType.MESH)
    for k in range(1, head_size):
        pl.semaphore_signal(
            barrier, inc=1, device_id=(d, lax.rem(hd + k, head_size)), device_id_type=pl.DeviceIdType.MESH
        )

    def ordered(i):
        return lax.rem(mine // pair + i, chunks)

    small = [
        pltpu.make_async_copy(src, dst, small_sems.at[n])
        for n, (src, dst) in enumerate((
            (offset_hbm, offset_ref), (step_hbm, step_ref), (sbias_hbm, sbias_ref), (dlog_hbm, dlog_ref),
            (ptaps_hbm, ptaps_ref), (pbias_hbm, pbias_ref), (proj_hbm, proj), (taps_hbm, taps_ref),
            (bias_hbm, bias_ref), (skip_hbm, skip_ref),
        ))
    ]
    for copy in small:
        copy.start()
    for c in range(chunks):
        feat_copy(ordered(c)).start()
    for c in range(chunks):
        gate_copy(c).start()

    xs[:8, :] = jnp.zeros((8, cols), F32)
    xp[:8, :] = jnp.zeros((8, 2 * state), F32)
    part[...] = jnp.zeros_like(part)

    upper = (
        lax.broadcasted_iota(jnp.int32, (rows, rows), 0) <= lax.broadcasted_iota(jnp.int32, (rows, rows), 1)
    ).astype(F32).astype(BF16)
    for copy in small[:4]:
        copy.wait()
    offset_row = offset_ref[...].astype(F32)
    offs[...] = jnp.broadcast_to(to_column(offset_row, rows), offs.shape)
    step = jax.nn.softplus(step_ref[...] + to_column(sbias_ref[...], heads))
    rate = step * (-jnp.exp(to_column(dlog_ref[...], heads)) * LOG2E)
    cum = running_sum(rate, upper)
    shifted = cum - jnp.log(step) * LOG2E
    a_rows[...] = shifted
    last = offset_row[:, rows - 1 : rows]
    place = lax.broadcasted_iota(jnp.int32, (heads, rows), 1)
    reach = rows - 1 - place
    weight = jnp.where(last >= reach.astype(F32), jnp.exp2(cum[:, rows - 1 : rows] - shifted), 0.0)
    coef[...] = jnp.where(place >= edge, weight, 0.0)
    coef_top[...] = weight[:, :hdim]
    keep = jnp.where(last >= float(rows), jnp.exp2(cum[:, rows - 1 : rows]), 0.0)
    kown[...] = jnp.broadcast_to(keep, kown.shape)

    near = jnp.minimum(d, 2) + jnp.minimum(ctx_size - 1 - d, 2) + head_size - 1
    pl.semaphore_wait(barrier, near)
    halo_f = remote(feat_hbm.at[pl.ds(rows - 8, 8), :], rim, halo_send.at[0], halo_recv.at[0], (d + 1, hd))
    halo_p = remote(proj_hbm.at[pl.ds(rows - 8, 8), :], prim, halo_send.at[1], halo_recv.at[1], (d + 1, hd))
    keep_on = remote(kown, kprev, keep_send.at[0], keep_recv.at[0], (d + 1, hd))
    keep_back = remote(kown, kmate, keep_send.at[1], keep_recv.at[1], (d - 1, hd))
    top_one = remote(top, tin.at[0], top_send.at[0], top_recv.at[0], (d + 1, hd))
    top_two = remote(top, tin.at[1], top_send.at[1], top_recv.at[1], (d + 2, hd))

    @pl.when(d + 1 < ctx_size)
    def _():
        halo_p.start()
        halo_f.start()
        keep_on.start()

    @pl.when(odd)
    def _():
        keep_back.start()

    def conv_all(c):
        feat_copy(c).wait()
        sl = chunk_cols(c)
        xs[8:, sl] = feat[:, sl].astype(F32)
        conv[:, sl] = tap_sum(
            lambda lag: xs[8 - lag : 8 + rows - lag, sl], taps_ref[:, sl], bias_ref[:, sl], offs[:, :1], taps_n
        ).astype(BF16)

    def a_copy(r):
        return remote(send.at[r], arecv.at[r], asend.at[r], arecv_sem.at[r], (mate, hd))

    def s_copy(r):
        return remote(sout.at[r], srecv.at[r], ssend.at[r], srecv_sem.at[r], (d + 2, hd))

    def f_copy(r):
        return remote(lsend.at[r], lrecv.at[r], fsend.at[r], lrecv_sem.at[r], (mate, hd))

    def g_copy(r):
        return remote(srecv.at[r], lrecv.at[r], fsend.at[r], lrecv_sem.at[r], (mate, hd))

    def contrib(h):
        scaled = (in_t[...] * coef[pl.ds(h, 1), :]).astype(BF16)
        return jnp.dot(scaled, conv[:, cols_of(h, 1)], preferred_element_type=F32)

    def mine_body(i, _):
        conv_all(mine // pair + i)
        for k in range(pair):
            r = i * pair + k
            send[r] = contrib(mine + r).astype(BF16)

            @pl.when(sends_early)
            def _():
                a_copy(r).start()

        return 0

    def theirs_body(i, _):
        conv_all(theirs // pair + i)
        for k in range(pair):
            r = i * pair + k
            own[r] = contrib(theirs + r)
        return 0

    for copy in small[4:]:
        copy.wait()
    xp[8:, :] = proj[...].astype(F32)
    bc[...] = tap_sum(
        lambda lag: xp[8 - lag : 8 + rows - lag, :], ptaps_ref[...], pbias_ref[...], offs[:, :1], taps_n
    ).astype(BF16)
    in_t[...] = bc[:, :state].astype(F32).T
    lax.fori_loop(0, part_chunks, mine_body, 0)

    cum_t = cum.T
    for h in range(heads):
        cb[h] = jnp.broadcast_to(cum_t[:, h : h + 1], (rows, hdim))
    skips[...] = jnp.broadcast_to(to_column(skip_ref[...], heads), skips.shape)

    @pl.when(d == 0)
    def _():
        rim[...] = jnp.zeros_like(rim)
        prim[...] = jnp.zeros_like(prim)
        lrecv[...] = jnp.zeros_like(lrecv)
        kprev[...] = jnp.zeros_like(kprev)
        tin[0] = jnp.zeros(tin.shape[1:], BF16)

    @pl.when(d < 2)
    def _():
        srecv[...] = jnp.zeros_like(srecv)
        tin[1] = jnp.zeros(tin.shape[1:], BF16)

    lax.fori_loop(0, part_chunks, theirs_body, 0)

    @pl.when(d > 0)
    def _():
        keep_on.wait_recv()

    @pl.when(even)
    def _():
        keep_back.wait_recv()

    def relay(r):
        h = theirs + r

        @pl.when(gets_early)
        def _():
            a_copy(r).wait_recv()

        @pl.when((d + 2 < ctx_size) & even)
        def _():
            sout[r] = (arecv[r].astype(F32) + kmate[pl.ds(h, 1), :] * own[r]).astype(BF16)
            s_copy(r).start()

        @pl.when((d + 2 < ctx_size) & odd)
        def _():
            sout[r] = (own[r] + kown[pl.ds(h, 1), :] * arecv[r].astype(F32)).astype(BF16)
            s_copy(r).start()

    def pass_on(r):
        @pl.when(d >= 2)
        def _():
            s_copy(r).wait_recv()

        @pl.when(even)
        def _():
            lsend[r] = (own[r] + kown[pl.ds(theirs + r, 1), :] * srecv[r].astype(F32)).astype(BF16)
            f_copy(r).start()

        @pl.when(odd & (d >= 2))
        def _():
            g_copy(r).start()

    @pl.when(d > 0)
    def _():
        halo_p.wait_recv()
        halo_f.wait_recv()

    xp[:8, :] = prim[...].astype(F32)
    bc[:16, :] = tap_sum(
        lambda lag: xp[8 - lag : 24 - lag, :], ptaps_ref[...], pbias_ref[...], offs[:16, :1], taps_n
    ).astype(BF16)
    for c in range(cols // 512):
        sl = slice(c * 512, (c + 1) * 512)
        xs[:8, sl] = rim[:, sl].astype(F32)
        conv[:16, sl] = tap_sum(
            lambda lag: xs[8 - lag : 24 - lag, sl], taps_ref[:, sl], bias_ref[:, sl], offs[:16, :1], taps_n
        ).astype(BF16)
    weight_t = coef_top[...].T[:8, :]
    row_id = lax.broadcasted_iota(jnp.int32, weight_t.shape, 0)
    weight_t = jnp.where(row_id < edge, weight_t, 0.0)
    in_top = bc[:8, :state].astype(F32)
    top[:, :state] = jnp.concatenate([in_top[:4], in_top[:4]], axis=0).astype(BF16)
    for r in range(part_heads):
        rows_of = [
            (conv[:8, h * hdim : (h + 1) * hdim].astype(F32) * weight_t[:, h : h + 1])[:4] for h in (r, part_heads + r)
        ]
        top[:, state + r * hdim : state + (r + 1) * hdim] = jnp.concatenate(rows_of, axis=0).astype(BF16)

    @pl.when(d + 1 < ctx_size)
    def _():
        top_one.start()

    @pl.when(d + 2 < ctx_size)
    def _():
        top_two.start()

    in_b = bc[:, :state]
    out_b[...] = bc[:, state:]
    scores = lax.dot_general(out_b[...], in_b, (((1,), (1,)), ((), ())), preferred_element_type=F32)
    ti = lax.broadcasted_iota(jnp.int32, (rows, rows), 0)
    si = lax.broadcasted_iota(jnp.int32, (rows, rows), 1)
    gap = ti - si
    masked[...] = jnp.where((gap >= 0) & (offs[:, :1] >= gap.astype(F32)), scores, 0.0)

    def local_part(c):
        gate_copy(c).wait()
        for k in range(pair):
            h = c * pair + k
            fcols = cols_of(h, 1)
            arow = a_rows[pl.ds(h, 1), :]
            cbv = cb[h]
            w0 = (jnp.exp2(jnp.minimum(cbv - arow[:, :half], 126.0)) * masked[:, :half]).astype(BF16)
            w1 = (jnp.exp2(jnp.minimum(cbv[half:] - arow[:, half:], 126.0)) * masked[half:, half:]).astype(BF16)
            fv = conv[:, fcols]
            first = jnp.dot(w0, fv[:half], preferred_element_type=F32)
            second = jnp.dot(w1, fv[half:], preferred_element_type=F32)
            inner = jnp.concatenate([first[:half], first[half:] + second], axis=0)
            gv = gate[:, fcols].astype(F32)
            sg = gv * (1.0 / (1.0 + jnp.exp(-gv)))
            yv[:, fcols] = (inner + skips[pl.ds(h, 1), :] * fv.astype(F32)) * sg
            tpos = lax.broadcasted_iota(jnp.int32, (rows, hdim), 0)
            lift = jnp.where(offs[...] >= (tpos + 1).astype(F32), jnp.exp2(cbv), 0.0)
            g2[:, fcols] = lift * sg

    def early_terms():
        @pl.when(d > 0)
        def _():
            top_one.wait_recv()

        @pl.when(d > 1)
        def _():
            top_two.wait_recv()

        firsts = jnp.concatenate([tin[0, :, :state], tin[1, :, :state]], axis=0)
        marks = lax.dot_general(out_b[...], firsts, (((1,), (1,)), ((), ())), preferred_element_type=F32)
        lane = lax.broadcasted_iota(jnp.int32, marks.shape, 1) % 8
        ext[0] = jnp.where(lane < 4, marks, 0.0).astype(BF16)
        ext[1] = jnp.where(lane < 4, 0.0, marks).astype(BF16)
        near_rows = lax.broadcasted_iota(jnp.int32, (8, hdim), 0)
        for r in range(part_heads):
            cs = slice(state + r * hdim, state + (r + 1) * hdim)
            decay = jnp.where(near_rows < 4, kprev[r : r + 1, :], kprev[part_heads + r : part_heads + r + 1, :])
            xt[:, r * hdim : (r + 1) * hdim] = jnp.concatenate(
                [tin[0, :, cs].astype(F32), tin[1, :, cs].astype(F32) * decay], axis=0
            ).astype(BF16)

    def finish(side, r, st):
        sl = cols_of(side * part_heads + r, pair)
        fs = jnp.dot(out_b[...], st, preferred_element_type=F32)
        fs = fs + jnp.dot(ext[side], xt[:, cols_of(r, pair)], preferred_element_type=F32)
        gt = yv[:, sl] + fs * g2[:, sl]
        gated[:, sl] = gt.astype(gated.dtype)
        squares = gt * gt
        total = squares[:, :hdim]
        for k in range(1, pair):
            total = total + squares[:, k * hdim : (k + 1) * hdim]
        part[...] += total

    def finish_theirs(r):
        @pl.when(even)
        def _():
            finish(1, r, jnp.concatenate([srecv[r + k] for k in range(pair)], axis=1))

        @pl.when(odd)
        def _():
            finish(0, r, jnp.concatenate([
                (arecv[r + k].astype(F32) + kprev[pl.ds(r + k, 1), :] * srecv[r + k].astype(F32)).astype(BF16)
                for k in range(pair)
            ], axis=1))

    lag = min(LAG, part_heads)

    def first_body(i, _):
        relay(i)
        local_part(i)
        return 0

    def second_body(i, _):
        relay(i)
        local_part(i)
        pass_on(i - lag)
        return 0

    lax.fori_loop(0, lag, first_body, 0)
    lax.fori_loop(lag, part_heads, second_body, 0)
    early_terms()
    done = 0
    for r in range(part_heads - lag, part_heads):
        pass_on(r)
        if done + pair <= r + 1:
            finish_theirs(done)
            done += pair
    while done < part_heads:
        finish_theirs(done)
        done += pair

    def last_body(j, _):
        r = j * pair

        @pl.when(gets_late)
        def _():
            for k in range(pair):
                f_copy(r + k).wait_recv()

        finish(parity, r, jnp.concatenate([lrecv[r + k] for k in range(pair)], axis=1))
        return 0

    lax.fori_loop(0, part_chunks, last_body, 0)

    sq[...] = jnp.sum(part[...].T, axis=0, keepdims=True)

    def sq_copy(k):
        return remote(
            sq, sqr.at[k - 1], sqsend.at[k - 1], sqrecv.at[k - 1], (d, lax.rem(hd + k, head_size))
        )

    for k in range(1, head_size):
        sq_copy(k).start()

    @pl.when(d + 1 < ctx_size)
    def _():
        halo_p.wait_send()
        halo_f.wait_send()
        keep_on.wait_send()
        top_one.wait_send()

    @pl.when(d + 2 < ctx_size)
    def _():
        top_two.wait_send()

    @pl.when(odd)
    def _():
        keep_back.wait_send()

    def drain(r, _):
        @pl.when(sends_early)
        def _():
            a_copy(r).wait_send()

        @pl.when(d + 2 < ctx_size)
        def _():
            s_copy(r).wait_send()

        @pl.when(sends_late)
        def _():
            f_copy(r).wait_send()

        return 0

    lax.fori_loop(0, part_heads, drain, 0)
    total = sq[...]
    for k in range(1, head_size):
        sq_copy(k).wait_recv()
        total = total + sqr[k - 1]
    scale = lax.rsqrt(total / (cols * head_size) + 1e-05)
    scale_ref[...] = jnp.broadcast_to(scale, (hdim, rows)).T
    for k in range(1, head_size):
        sq_copy(k).wait_send()


def scale_kernel(gated_ref, scale_ref, gain_ref, out_hbm, staged, sems):
    rows, cols = staged.shape
    lanes = scale_ref.shape[1]
    stripe = min(STRIPE, rows)

    def out_copy(r):
        rs = pl.ds(r * stripe, stripe)
        return pltpu.make_async_copy(staged.at[rs, :], out_hbm.at[rs, :], sems.at[r])

    for r in range(rows // stripe):
        rs = slice(r * stripe, (r + 1) * stripe)
        scale = scale_ref[rs, :]
        for c in range(cols // lanes):
            cs = slice(c * lanes, (c + 1) * lanes)
            staged[rs, cs] = (gated_ref[rs, cs].astype(F32) * scale * gain_ref[:, cs]).astype(BF16)
        out_copy(r).start()
    for r in range(rows // stripe):
        out_copy(r).wait()


def finish_call(gated, scale, gain):
    rows, cols = gated.shape
    vm = pl.BlockSpec(memory_space=pltpu.VMEM)
    return pl.pallas_call(
        scale_kernel,
        out_shape=jax.ShapeDtypeStruct((rows, cols), BF16),
        in_specs=[vm, vm, vm],
        out_specs=pl.BlockSpec(memory_space=pltpu.HBM),
        scratch_shapes=[
            pltpu.VMEM((rows, cols), BF16), pltpu.SemaphoreType.DMA((rows // min(STRIPE, rows),)),
        ],
        compiler_params=pltpu.CompilerParams(vmem_limit_bytes=8 << 20),
        name="scale",
    )(gated, scale, gain)


def short_body(
    feat_in, gate_in, state_proj, step_raw, doc_offset, feat_taps, feat_bias,
    proj_taps, proj_bias, step_bias, decay_log, skip_gain, norm_gain,
):
    heads, rows = step_raw.shape
    cols = feat_in.shape[1]
    hdim = cols // heads
    state = state_proj.shape[1] // 2
    taps = feat_taps.shape[0]
    ctx_size = lax.axis_size("ctx")
    head_size = lax.axis_size("head")
    pair = PAIR
    chunks = heads // pair
    some = heads // 2
    vm = pl.BlockSpec(memory_space=pltpu.VMEM)
    hbm = pl.BlockSpec(memory_space=pltpu.HBM)
    V = pltpu.VMEM
    DMA = pltpu.SemaphoreType.DMA
    piece = (some, state, hdim)
    operands = (
        feat_in, gate_in, state_proj, step_raw, doc_offset[None, :], feat_taps,
        feat_bias[None, :], proj_taps, proj_bias[None, :], step_bias[None, :], decay_log[None, :], skip_gain[None, :],
    )
    gated, scale = pl.pallas_call(
        functools.partial(mixer_kernel, ctx_size, head_size, pair),
        out_shape=(
            jax.ShapeDtypeStruct((rows, cols), BF16),
            jax.ShapeDtypeStruct((rows, hdim), F32),
        ),
        in_specs=[hbm] * len(operands),
        out_specs=(vm, vm),
        scratch_shapes=[
            V((heads, rows), F32), V((1, rows), jnp.int32), V((taps, cols), F32), V((1, cols), F32),
            V((taps, 2 * state), F32), V((1, 2 * state), F32), V((1, heads), F32), V((1, heads), F32),
            V((1, heads), F32),
            V((rows, cols), BF16), V((rows, cols), BF16), V((rows, 2 * state), BF16),
            V((rows + 8, cols), F32), V((rows + 8, 2 * state), F32),
            V((8, cols), BF16), V((8, 2 * state), BF16), V((rows, cols), BF16),
            V((state, rows), F32), V((rows, 2 * state), BF16), V((rows, state), BF16), V((rows, rows), F32),
            V((heads, rows, hdim), F32), V((heads, rows), F32), V((heads, rows), F32), V((heads, hdim), F32),
            V((rows, hdim), F32), V((heads, hdim), F32),
            V(piece, F32), V(piece, BF16), V(piece, BF16), V(piece, BF16), V(piece, BF16), V(piece, BF16),
            V(piece, BF16),
            V((heads, hdim), F32), V((heads, hdim), F32), V((heads, hdim), F32),
            V((8, state + cols // 2), BF16), V((2, 8, state + cols // 2), BF16), V((2, rows, 16), BF16),
            V((16, cols // 2), BF16),
            V((rows, cols), F32), V((rows, cols), F32), V((rows, hdim), F32),
            V((1, rows), F32), V((head_size - 1, 1, rows), F32),
            DMA((10,)), DMA((chunks,)), DMA((chunks,)), *[DMA((2,)) for _ in range(6)],
            *[DMA((some,)) for _ in range(6)],
            DMA((head_size - 1,)), DMA((head_size - 1,)),
        ],
        compiler_params=pltpu.CompilerParams(collective_id=0, has_side_effects=True, vmem_limit_bytes=40 << 20),
        name="mixer",
    )(*[pltpu.with_memory_space_constraint(operand, pltpu.HBM) for operand in operands])
    return finish_call(gated, scale, norm_gain[None, :])


def solution(mesh):
    ctx_size = mesh.shape["ctx"]

    def chosen(*args):
        row_count = args[0].shape[0]
        longest_doc = row_count * ctx_size // 4
        span_back = (longest_doc + row_count - 2) // row_count
        if span_back == 2 and ctx_size % 2 == 0:
            return short_body(*args)
        return body(*args)

    return jax.shard_map(
        chosen,
        mesh=mesh,
        in_specs=(
            P("ctx", "head"),
            P("ctx", "head"),
            P("ctx", None),
            P("head", "ctx"),
            P("ctx"),
            P(None, "head"),
            P("head"),
            P(),
            P(),
            P("head"),
            P("head"),
            P("head"),
            P("head"),
        ),
        out_specs=P("ctx", "head"),
        check_vma=False,
    )
```

```python
import functools

import jax
import jax.numpy as jnp
from jax import lax
from jax.experimental import pallas as pl
from jax.experimental.pallas import tpu as pltpu
from jax.sharding import PartitionSpec as P


def passed_along(block, axis, distance):
    devices = range(lax.axis_size(axis))
    route = [(i - distance, i) for i in devices if i - distance in devices]
    return lax.ppermute(block, axis, route)


def causal_taps(values, rim_rows, kernel_taps, kernel_bias, offsets):
    row_count = values.shape[0]
    tap_count = kernel_taps.shape[0]
    joined = jnp.concatenate([rim_rows, values], axis=0).astype(jnp.float32)
    summed = jnp.broadcast_to(kernel_bias[None, :], values.shape)
    for tap_index in range(tap_count):
        tap_lag = tap_count - 1 - tap_index
        window_rows = lax.slice_in_dim(joined, tap_index, tap_index + row_count, axis=0)
        summed = summed + jnp.where(
            (offsets >= tap_lag)[:, None], kernel_taps[tap_index][None, :] * window_rows, 0.0
        )
    return jax.nn.silu(summed).astype(jnp.bfloat16)


def combine_states(earlier_part, later_part):
    return (
        earlier_part[0] * later_part[0],
        later_part[0][:, None, None] * earlier_part[1] + later_part[1],
    )


def body(
    feat_in,
    gate_in,
    state_proj,
    step_raw,
    doc_offset,
    feat_taps,
    feat_bias,
    proj_taps,
    proj_bias,
    step_bias,
    decay_log,
    skip_gain,
    norm_gain,
):
    head_count = step_raw.shape[0]
    row_count = feat_in.shape[0]
    head_dim = feat_in.shape[1] // head_count
    state_size = state_proj.shape[1] // 2
    tap_count = feat_taps.shape[0]
    rim_feat, rim_proj = passed_along(
        (feat_in[row_count - tap_count + 1 :], state_proj[row_count - tap_count + 1 :]), "ctx", 1
    )
    conv_feat = causal_taps(feat_in, rim_feat, feat_taps, feat_bias, doc_offset)
    conv_proj = causal_taps(state_proj, rim_proj, proj_taps, proj_bias, doc_offset)
    step_all = jax.nn.softplus(step_raw + step_bias[:, None])
    rate_all = step_all * (-jnp.exp(decay_log))[:, None]
    block_rows = min(512, row_count)
    position = jnp.arange(block_rows, dtype=jnp.int32)
    causal = position[None, :] <= position[:, None]
    final_row = block_rows - 1
    element_decay = jnp.ones((head_count,), jnp.float32)
    element_state = jnp.zeros((head_count, head_dim, state_size), jnp.float32)
    block_index = 0
    start = block_index * block_rows
    feat_block = conv_feat.reshape(block_rows, head_count, head_dim)
    in_block = conv_proj[start : start + block_rows, :state_size]
    out_block = conv_proj[start : start + block_rows, state_size:]
    cumulative = jnp.cumsum(rate_all, axis=1)
    same_doc = causal & (doc_offset[:, None] >= position[:, None] - position[None, :])
    scores = jnp.dot(out_block, in_block.T, preferred_element_type=jnp.float32)
    exponent_gap = jnp.where(
        same_doc[None], cumulative[:, :, None] - cumulative[:, None, :], -jnp.inf
    )
    weights = (scores[None] * jnp.exp(exponent_gap) * step_all[:, None, :]).astype(jnp.bfloat16)
    inner_out = jnp.einsum("hts,shp->thp", weights, feat_block, preferred_element_type=jnp.float32)
    reaches = doc_offset >= position + 1
    tail_mask = doc_offset[final_row] >= final_row - position
    tail_coef = jnp.where(
        tail_mask[None, :],
        jnp.exp(cumulative[:, final_row : final_row + 1] - cumulative) * step_all,
        0.0,
    )
    scaled = (in_block.astype(jnp.float32)[None] * tail_coef[:, :, None]).astype(jnp.bfloat16)
    contrib = jnp.einsum("shp,hsn->hpn", feat_block, scaled, preferred_element_type=jnp.float32)
    keep_factor = jnp.where(reaches[final_row], jnp.exp(cumulative[:, final_row]), 0.0)
    saved_blocks = [(feat_block, out_block, cumulative, reaches, inner_out, contrib, keep_factor)]
    element_state = keep_factor[:, None, None] * element_state + contrib
    element_decay = element_decay * keep_factor
    longest_doc = row_count * lax.axis_size("ctx") // 4
    span_back = (longest_doc + row_count - 2) // row_count
    distances = [1]
    window_size = 1
    while window_size < span_back:
        distances.append(window_size)
        window_size = window_size * 2
    current = (element_decay, element_state)
    for turn_index, distance in enumerate(distances):
        moved = passed_along((current[0], current[1]), "ctx", distance)
        if turn_index == 0:
            current = moved
        else:
            current = combine_states(moved, current)
    start_state = current[1]
    pieces_out = []
    for block_index, saved in enumerate(saved_blocks):
        feat_block, out_block, cumulative, reaches, inner_out, contrib, keep_factor = saved
        lift_factor = jnp.where(reaches[None, :], jnp.exp(cumulative), 0.0)
        from_state = (
            jnp.einsum(
                "tn,hpn->thp",
                out_block.astype(jnp.float32),
                start_state,
                precision=lax.Precision.HIGHEST,
            )
            * lift_factor.T[:, :, None]
        )
        pieces_out.append(
            inner_out + from_state + skip_gain[None, :, None] * feat_block.astype(jnp.float32)
        )
    mixed = pieces_out[0].reshape(row_count, head_count * head_dim)
    gated = mixed * jax.nn.silu(gate_in.astype(jnp.float32))
    squares = jnp.sum(gated * gated, axis=1)
    total_squares = lax.psum(squares, "head")
    scale = lax.rsqrt(total_squares / (head_count * head_dim * lax.axis_size("head")) + 1e-05)
    return (gated * scale[:, None] * norm_gain[None, :]).astype(jnp.bfloat16)


PAIR = 2
READY = 2
LAG = 5
STRIPE = 32

LOG2E = 1.4426950408889634
F32 = jnp.float32
BF16 = jnp.bfloat16


def to_column(row, size):
    rows = lax.broadcasted_iota(jnp.int32, (size, size), 0)
    cols = lax.broadcasted_iota(jnp.int32, (size, size), 1)
    return jnp.sum(jnp.where(rows == cols, row, 0.0), axis=1, keepdims=True)


def tap_sum(window_of, taps, bias, offsets, tap_count):
    summed = bias
    for tap_index in range(tap_count):
        tap_lag = tap_count - 1 - tap_index
        term = taps[tap_index : tap_index + 1, :] * window_of(tap_lag)
        if tap_lag:
            term = jnp.where(offsets >= float(tap_lag), term, 0.0)
        summed = summed + term
    return summed * (1.0 / (1.0 + jnp.exp(-summed)))


def running_sum(values, upper):
    first = values.astype(BF16)
    left = values - first.astype(F32)
    second = left.astype(BF16)
    third = (left - second.astype(F32)).astype(BF16)
    count = values.shape[0]
    sums = jnp.dot(jnp.concatenate([first, second, third], axis=0), upper, preferred_element_type=F32)
    return sums[:count] + sums[count : 2 * count] + sums[2 * count :]


def mixer_kernel(
    ctx_size, head_size, pair,
    feat_hbm, gate_hbm, proj_hbm, step_hbm, offset_hbm, taps_hbm, bias_hbm,
    ptaps_hbm, pbias_hbm, sbias_hbm, dlog_hbm, skip_hbm,
    gated, scale_ref,
    step_ref, offset_ref, taps_ref, bias_ref, ptaps_ref, pbias_ref, sbias_ref, dlog_ref, skip_ref,
    feat, gate, proj, xs, xp, rim, conv, in_t, bc, out_b, masked, cb, a_rows, coef, coef_top,
    offs, skips, own, send, arecv, srecv, sout, lsend, lrecv, kown, kmate, kprev,
    top, tin, ext, xt, yv, g2, part, sq, sqr, tail, tail_proj, tail_half, tail_sems,
    small_sems, feat_sems, gate_sem, halo_send, halo_recv, keep_send, keep_recv, top_send, top_recv,
    asend, arecv_sem, ssend, srecv_sem, fsend, lrecv_sem, sqsend, sqrecv,
):
    d = lax.axis_index("ctx")
    hd = lax.axis_index("head")
    rows, cols = feat.shape
    heads = step_ref.shape[0]
    hdim = cols // heads
    state = in_t.shape[0]
    taps_n = taps_ref.shape[0]
    edge = taps_n - 1
    width = pair * hdim
    chunks = heads // pair
    half = rows // 2
    odd = d % 2 == 1
    even = d % 2 == 0
    parity = d % 2
    mate = d + 1 - 2 * parity
    part_heads = heads // 2
    part_chunks = chunks // 2
    mine = parity * part_heads
    theirs = part_heads - mine
    sends_early = even | (d + 1 < ctx_size)
    gets_early = odd | (d + 2 < ctx_size)
    sends_late = even | (d >= 2)
    gets_late = odd | (d >= 2)

    def cols_of(h, count):
        return pl.ds(pl.multiple_of(h * hdim, hdim), count * hdim)

    def chunk_cols(c):
        return pl.ds(pl.multiple_of(c * width, width), width)

    def feat_copy(c):
        return pltpu.make_async_copy(feat_hbm.at[:, chunk_cols(c)], feat.at[:, chunk_cols(c)], feat_sems.at[c])

    gate_copy = pltpu.make_async_copy(gate_hbm, gate, gate_sem)

    def remote(src, dst, ssem, rsem, where):
        return pltpu.make_async_remote_copy(
            src_ref=src, dst_ref=dst, send_sem=ssem, recv_sem=rsem,
            device_id=where, device_id_type=pl.DeviceIdType.MESH,
        )

    barrier = pltpu.get_barrier_semaphore()
    for shift in (-2, -1, 1, 2):
        @pl.when((d + shift >= 0) & (d + shift < ctx_size))
        def _():
            pl.semaphore_signal(barrier, inc=1, device_id=(d + shift, hd), device_id_type=pl.DeviceIdType.MESH)
    for k in range(1, head_size):
        pl.semaphore_signal(
            barrier, inc=1, device_id=(d, lax.rem(hd + k, head_size)), device_id_type=pl.DeviceIdType.MESH
        )

    def ordered(i):
        return lax.rem(mine // pair + i, chunks)

    tail_copies = [
        pltpu.make_async_copy(feat_hbm.at[pl.ds(rows - 8, 8), :], tail, tail_sems.at[0]),
        pltpu.make_async_copy(proj_hbm.at[pl.ds(rows - 8, 8), :], tail_proj, tail_sems.at[1]),
    ]
    for copy in tail_copies:
        copy.start()
    small = [
        pltpu.make_async_copy(src, dst, small_sems.at[n])
        for n, (src, dst) in enumerate((
            (offset_hbm, offset_ref), (step_hbm, step_ref), (sbias_hbm, sbias_ref), (dlog_hbm, dlog_ref),
            (ptaps_hbm, ptaps_ref), (pbias_hbm, pbias_ref), (proj_hbm, proj), (taps_hbm, taps_ref),
            (bias_hbm, bias_ref), (skip_hbm, skip_ref),
        ))
    ]
    for copy in small:
        copy.start()
    for c in range(chunks):
        feat_copy(ordered(c)).start()
    gate_copy.start()

    xs[:8, :] = jnp.zeros((8, cols), F32)
    xp[:8, :] = jnp.zeros((8, 2 * state), F32)
    part[...] = jnp.zeros_like(part)

    upper = (
        lax.broadcasted_iota(jnp.int32, (rows, rows), 0) <= lax.broadcasted_iota(jnp.int32, (rows, rows), 1)
    ).astype(F32).astype(BF16)
    for copy in small[:4]:
        copy.wait()
    offset_row = offset_ref[...].astype(F32)
    offs[...] = jnp.broadcast_to(to_column(offset_row, rows), offs.shape)
    step = jax.nn.softplus(step_ref[...] + to_column(sbias_ref[...], heads))
    rate = step * (-jnp.exp(to_column(dlog_ref[...], heads)) * LOG2E)
    cum = running_sum(rate, upper)
    shifted = cum - jnp.log(step) * LOG2E
    a_rows[...] = shifted
    last = offset_row[:, rows - 1 : rows]
    place = lax.broadcasted_iota(jnp.int32, (heads, rows), 1)
    reach = rows - 1 - place
    weight = jnp.where(last >= reach.astype(F32), jnp.exp2(cum[:, rows - 1 : rows] - shifted), 0.0)
    coef[...] = jnp.where(place >= edge, weight, 0.0)
    coef_top[...] = weight[:, :hdim]
    keep = jnp.where(last >= float(rows), jnp.exp2(cum[:, rows - 1 : rows]), 0.0)
    kown[...] = jnp.broadcast_to(keep, kown.shape)

    for copy in tail_copies:
        copy.wait()
    tail_half[:, cols // 2 :] = tail_proj[...]
    tail_half[:, : cols // 2] = jnp.concatenate(
        [tail[:, : cols // 2].astype(F32)[4:], tail[:, cols // 2 :].astype(F32)[4:]], axis=0
    ).astype(BF16)
    near = jnp.minimum(d, 2) + jnp.minimum(ctx_size - 1 - d, 2) + head_size - 1
    pl.semaphore_wait(barrier, near)
    halo = remote(tail_half, rim, halo_send, halo_recv, (d + 1, hd))
    keep_on = remote(kown, kprev, keep_send.at[0], keep_recv.at[0], (d + 1, hd))
    keep_back = remote(kown, kmate, keep_send.at[1], keep_recv.at[1], (d - 1, hd))
    top_one = remote(top, tin.at[0], top_send.at[0], top_recv.at[0], (d + 1, hd))
    top_two = remote(top, tin.at[1], top_send.at[1], top_recv.at[1], (d + 2, hd))

    @pl.when(d + 1 < ctx_size)
    def _():
        halo.start()
        keep_on.start()

    @pl.when(odd)
    def _():
        keep_back.start()

    def conv_all(c):
        feat_copy(c).wait()
        sl = chunk_cols(c)
        xs[8:, sl] = feat[:, sl].astype(F32)
        conv[:, sl] = tap_sum(
            lambda lag: xs[8 - lag : 8 + rows - lag, sl], taps_ref[:, sl], bias_ref[:, sl], offs[:, :1], taps_n
        ).astype(BF16)

    def a_copy(r):
        return remote(send.at[r], arecv.at[r], asend, arecv_sem.at[r], (mate, hd))

    def s_copy(r):
        return remote(sout.at[r], srecv.at[r], ssend, srecv_sem.at[r], (d + 2, hd))

    def f_copy(r):
        return remote(lsend.at[r], lrecv.at[r], fsend, lrecv_sem.at[r // pair], (mate, hd))

    def g_copy(r):
        return remote(srecv.at[r], lrecv.at[r], fsend, lrecv_sem.at[r // pair], (mate, hd))

    def contrib(h):
        scaled = (in_t[...] * coef[pl.ds(h, 1), :]).astype(BF16)
        return jnp.dot(scaled, conv[:, cols_of(h, 1)], preferred_element_type=F32)

    def mine_body(i, _):
        conv_all(mine // pair + i)
        for k in range(pair):
            r = i * pair + k
            send[r] = contrib(mine + r).astype(BF16)

            @pl.when(sends_early)
            def _():
                a_copy(r).start()

        return 0

    def theirs_body(i, _):
        conv_all(theirs // pair + i)
        for k in range(pair):
            r = i * pair + k
            own[r] = contrib(theirs + r)
        return 0

    for copy in small[4:]:
        copy.wait()
    xp[8:, :] = proj[...].astype(F32)
    bc[...] = tap_sum(
        lambda lag: xp[8 - lag : 8 + rows - lag, :], ptaps_ref[...], pbias_ref[...], offs[:, :1], taps_n
    ).astype(BF16)
    in_t[...] = bc[:, :state].astype(F32).T
    lax.fori_loop(0, part_chunks, mine_body, 0)

    @pl.when(d == 0)
    def _():
        rim[...] = jnp.zeros_like(rim)
        lrecv[...] = jnp.zeros_like(lrecv)
        kprev[...] = jnp.zeros_like(kprev)
        tin[0] = jnp.zeros(tin.shape[1:], BF16)

    @pl.when(d < 2)
    def _():
        srecv[...] = jnp.zeros_like(srecv)
        tin[1] = jnp.zeros(tin.shape[1:], BF16)

    lax.fori_loop(0, part_chunks, theirs_body, 0)

    @pl.when(d > 0)
    def _():
        keep_on.wait_recv()

    @pl.when(even)
    def _():
        keep_back.wait_recv()

    def relay(r):
        h = theirs + r

        @pl.when(gets_early)
        def _():
            a_copy(r).wait_recv()

        @pl.when((d + 2 < ctx_size) & even)
        def _():
            sout[r] = (arecv[r].astype(F32) + kmate[pl.ds(h, 1), :] * own[r]).astype(BF16)
            s_copy(r).start()

        @pl.when((d + 2 < ctx_size) & odd)
        def _():
            sout[r] = (own[r] + kown[pl.ds(h, 1), :] * arecv[r].astype(F32)).astype(BF16)
            s_copy(r).start()

    def pass_on(r):
        @pl.when(d >= 2)
        def _():
            s_copy(r).wait_recv()

        @pl.when(even)
        def _():
            lsend[r] = (own[r] + kown[pl.ds(theirs + r, 1), :] * srecv[r].astype(F32)).astype(BF16)
            f_copy(r).start()

        @pl.when(odd & (d >= 2))
        def _():
            g_copy(r).start()

    ready = min(READY, part_heads)
    for r in range(ready):
        relay(r)
    cum_t = cum.T
    for h in range(heads):
        cb[h] = jnp.broadcast_to(cum_t[:, h : h + 1], (rows, hdim))
    skips[...] = jnp.broadcast_to(to_column(skip_ref[...], heads), skips.shape)

    @pl.when(d > 0)
    def _():
        halo.wait_recv()

    xp[:8, :] = rim[:, cols // 2 :].astype(F32)
    bc[:16, :] = tap_sum(
        lambda lag: xp[8 - lag : 24 - lag, :], ptaps_ref[...], pbias_ref[...], offs[:16, :1], taps_n
    ).astype(BF16)
    for c in range(cols // 512):
        sl = slice(c * 512, (c + 1) * 512)
        first = c * 512 < cols // 2
        arrived = rim[:, (c * 512) % (cols // 2) : (c * 512) % (cols // 2) + 512].astype(F32)
        xs[:8, sl] = jnp.concatenate([arrived[:4], arrived[:4]], axis=0) if first else arrived
        conv[:16, sl] = tap_sum(
            lambda lag: xs[8 - lag : 24 - lag, sl], taps_ref[:, sl], bias_ref[:, sl], offs[:16, :1], taps_n
        ).astype(BF16)
    weight_t = coef_top[...].T[:8, :]
    row_id = lax.broadcasted_iota(jnp.int32, weight_t.shape, 0)
    weight_t = jnp.where(row_id < edge, weight_t, 0.0)
    in_top = bc[:8, :state].astype(F32)
    top[:, :state] = jnp.concatenate([in_top[:4], in_top[:4]], axis=0).astype(BF16)
    for r in range(part_heads):
        rows_of = [
            (conv[:8, h * hdim : (h + 1) * hdim].astype(F32) * weight_t[:, h : h + 1])[:4] for h in (r, part_heads + r)
        ]
        top[:, state + r * hdim : state + (r + 1) * hdim] = jnp.concatenate(rows_of, axis=0).astype(BF16)

    @pl.when(d + 1 < ctx_size)
    def _():
        top_one.start()

    @pl.when(d + 2 < ctx_size)
    def _():
        top_two.start()

    in_b = bc[:, :state]
    out_b[...] = bc[:, state:]
    scores = lax.dot_general(out_b[...], in_b, (((1,), (1,)), ((), ())), preferred_element_type=F32)
    ti = lax.broadcasted_iota(jnp.int32, (rows, rows), 0)
    si = lax.broadcasted_iota(jnp.int32, (rows, rows), 1)
    gap = ti - si
    masked[...] = jnp.where((gap >= 0) & (offs[:, :1] >= gap.astype(F32)), scores, 0.0)

    def local_part(h):
        for _ in range(1):
            fcols = cols_of(h, 1)
            arow = a_rows[pl.ds(h, 1), :]
            cbv = cb[h]
            w0 = (jnp.exp2(jnp.minimum(cbv - arow[:, :half], 126.0)) * masked[:, :half]).astype(BF16)
            w1 = (jnp.exp2(jnp.minimum(cbv[half:] - arow[:, half:], 126.0)) * masked[half:, half:]).astype(BF16)
            fv = conv[:, fcols]
            first = jnp.dot(w0, fv[:half], preferred_element_type=F32)
            second = jnp.dot(w1, fv[half:], preferred_element_type=F32)
            inner = jnp.concatenate([first[:half], first[half:] + second], axis=0)
            gv = gate[:, fcols].astype(F32)
            sg = gv * (1.0 / (1.0 + jnp.exp(-gv)))
            yv[:, fcols] = (inner + skips[pl.ds(h, 1), :] * fv.astype(F32)) * sg
            tpos = lax.broadcasted_iota(jnp.int32, (rows, hdim), 0)
            lift = jnp.where(offs[...] >= (tpos + 1).astype(F32), jnp.exp2(cbv), 0.0)
            g2[:, fcols] = lift * sg

    def early_terms():
        @pl.when(d > 0)
        def _():
            top_one.wait_recv()

        @pl.when(d > 1)
        def _():
            top_two.wait_recv()

        firsts = jnp.concatenate([tin[0, :, :state], tin[1, :, :state]], axis=0)
        marks = lax.dot_general(out_b[...], firsts, (((1,), (1,)), ((), ())), preferred_element_type=F32)
        lane = lax.broadcasted_iota(jnp.int32, marks.shape, 1) % 8
        ext[0] = jnp.where(lane < 4, marks, 0.0).astype(BF16)
        ext[1] = jnp.where(lane < 4, 0.0, marks).astype(BF16)
        near_rows = lax.broadcasted_iota(jnp.int32, (8, hdim), 0)
        for r in range(part_heads):
            cs = slice(state + r * hdim, state + (r + 1) * hdim)
            decay = jnp.where(near_rows < 4, kprev[r : r + 1, :], kprev[part_heads + r : part_heads + r + 1, :])
            xt[:, r * hdim : (r + 1) * hdim] = jnp.concatenate(
                [tin[0, :, cs].astype(F32), tin[1, :, cs].astype(F32) * decay], axis=0
            ).astype(BF16)

    def finish(side, r, st):
        sl = cols_of(side * part_heads + r, pair)
        fs = jnp.dot(out_b[...], st, preferred_element_type=F32)
        fs = fs + jnp.dot(ext[side], xt[:, cols_of(r, pair)], preferred_element_type=F32)
        gt = yv[:, sl] + fs * g2[:, sl]
        gated[:, sl] = gt.astype(gated.dtype)
        squares = gt * gt
        total = squares[:, :hdim]
        for k in range(1, pair):
            total = total + squares[:, k * hdim : (k + 1) * hdim]
        part[...] += total

    def finish_theirs(r):
        @pl.when(even)
        def _():
            finish(1, r, jnp.concatenate([srecv[r + k] for k in range(pair)], axis=1))

        @pl.when(odd)
        def _():
            finish(0, r, jnp.concatenate([
                (arecv[r + k].astype(F32) + kprev[pl.ds(r + k, 1), :] * srecv[r + k].astype(F32)).astype(BF16)
                for k in range(pair)
            ], axis=1))

    lag = min(LAG, part_heads)

    def first_body(i, _):
        relay(i)
        local_part(i)
        return 0

    def second_body(i, _):
        pass_on(i - lag)
        local_part(part_heads + i - lag)
        return 0

    def both_body(i, _):
        first_body(i, 0)
        second_body(i, 0)
        return 0

    gate_copy.wait()
    for r in range(ready):
        local_part(r)
    lax.fori_loop(ready, lag, first_body, 0)
    lax.fori_loop(lag, part_heads, both_body, 0)
    lax.fori_loop(part_heads, part_heads + lag, second_body, 0)
    early_terms()
    for r in range(0, part_heads, pair):
        finish_theirs(r)

    def last_body(j, _):
        r = j * pair

        @pl.when(gets_late)
        def _():
            some = pl.ds(r, pair)
            remote(lsend.at[some], lrecv.at[some], fsend, lrecv_sem.at[j], (mate, hd)).wait_recv()

        finish(parity, r, jnp.concatenate([lrecv[r + k] for k in range(pair)], axis=1))
        return 0

    lax.fori_loop(0, part_chunks, last_body, 0)

    sq[...] = jnp.sum(part[...].T, axis=0, keepdims=True)

    def sq_copy(k):
        return remote(
            sq, sqr.at[k - 1], sqsend, sqrecv.at[k - 1], (d, lax.rem(hd + k, head_size))
        )

    for k in range(1, head_size):
        sq_copy(k).start()

    @pl.when(d + 1 < ctx_size)
    def _():
        halo.wait_send()
        keep_on.wait_send()
        top_one.wait_send()

    @pl.when(d + 2 < ctx_size)
    def _():
        top_two.wait_send()

    @pl.when(odd)
    def _():
        keep_back.wait_send()

    @pl.when(sends_early)
    def _():
        remote(send, arecv, asend, arecv_sem.at[0], (mate, hd)).wait_send()

    @pl.when(d + 2 < ctx_size)
    def _():
        remote(sout, srecv, ssend, srecv_sem.at[0], (d + 2, hd)).wait_send()

    @pl.when(sends_late)
    def _():
        remote(lsend, lrecv, fsend, lrecv_sem.at[0], (mate, hd)).wait_send()

    total = sq[...]
    for k in range(1, head_size):
        sq_copy(k).wait_recv()
        total = total + sqr[k - 1]
    scale = lax.rsqrt(total / (cols * head_size) + 1e-05)
    scale_ref[...] = jnp.broadcast_to(scale, (hdim, rows)).T
    remote(sqr, sqr, sqsend, sqrecv.at[0], (d, lax.rem(hd + 1, head_size))).wait_send()


def scale_kernel(gated_ref, scale_ref, gain_ref, out_hbm, staged, sems):
    rows, cols = staged.shape
    lanes = scale_ref.shape[1]
    stripe = min(STRIPE, rows)

    def out_copy(r):
        rs = pl.ds(r * stripe, stripe)
        return pltpu.make_async_copy(staged.at[rs, :], out_hbm.at[rs, :], sems.at[r])

    for r in range(rows // stripe):
        rs = slice(r * stripe, (r + 1) * stripe)
        scale = scale_ref[rs, :]
        for c in range(cols // lanes):
            cs = slice(c * lanes, (c + 1) * lanes)
            staged[rs, cs] = (gated_ref[rs, cs].astype(F32) * scale * gain_ref[:, cs]).astype(BF16)
        out_copy(r).start()
    for r in range(rows // stripe):
        out_copy(r).wait()


def finish_call(gated, scale, gain):
    rows, cols = gated.shape
    vm = pl.BlockSpec(memory_space=pltpu.VMEM)
    return pl.pallas_call(
        scale_kernel,
        out_shape=jax.ShapeDtypeStruct((rows, cols), BF16),
        in_specs=[vm, vm, vm],
        out_specs=pl.BlockSpec(memory_space=pltpu.HBM),
        scratch_shapes=[
            pltpu.VMEM((rows, cols), BF16), pltpu.SemaphoreType.DMA((rows // min(STRIPE, rows),)),
        ],
        compiler_params=pltpu.CompilerParams(vmem_limit_bytes=8 << 20),
        name="scale",
    )(gated, scale, gain)


def short_body(
    feat_in, gate_in, state_proj, step_raw, doc_offset, feat_taps, feat_bias,
    proj_taps, proj_bias, step_bias, decay_log, skip_gain, norm_gain,
):
    heads, rows = step_raw.shape
    cols = feat_in.shape[1]
    hdim = cols // heads
    state = state_proj.shape[1] // 2
    taps = feat_taps.shape[0]
    ctx_size = lax.axis_size("ctx")
    head_size = lax.axis_size("head")
    pair = PAIR
    chunks = heads // pair
    some = heads // 2
    vm = pl.BlockSpec(memory_space=pltpu.VMEM)
    hbm = pl.BlockSpec(memory_space=pltpu.HBM)
    V = pltpu.VMEM
    DMA = pltpu.SemaphoreType.DMA
    piece = (some, state, hdim)
    operands = (
        feat_in, gate_in, state_proj, step_raw, doc_offset[None, :], feat_taps,
        feat_bias[None, :], proj_taps, proj_bias[None, :], step_bias[None, :], decay_log[None, :], skip_gain[None, :],
    )
    gated, scale = pl.pallas_call(
        functools.partial(mixer_kernel, ctx_size, head_size, pair),
        out_shape=(
            jax.ShapeDtypeStruct((rows, cols), BF16),
            jax.ShapeDtypeStruct((rows, hdim), F32),
        ),
        in_specs=[hbm] * len(operands),
        out_specs=(vm, vm),
        scratch_shapes=[
            V((heads, rows), F32), V((1, rows), jnp.int32), V((taps, cols), F32), V((1, cols), F32),
            V((taps, 2 * state), F32), V((1, 2 * state), F32), V((1, heads), F32), V((1, heads), F32),
            V((1, heads), F32),
            V((rows, cols), BF16), V((rows, cols), BF16), V((rows, 2 * state), BF16),
            V((rows + 8, cols), F32), V((rows + 8, 2 * state), F32),
            V((8, cols // 2 + 2 * state), BF16), V((rows, cols), BF16),
            V((state, rows), F32), V((rows, 2 * state), BF16), V((rows, state), BF16), V((rows, rows), F32),
            V((heads, rows, hdim), F32), V((heads, rows), F32), V((heads, rows), F32), V((heads, hdim), F32),
            V((rows, hdim), F32), V((heads, hdim), F32),
            V(piece, F32), V(piece, BF16), V(piece, BF16), V(piece, BF16), V(piece, BF16), V(piece, BF16),
            V(piece, BF16),
            V((heads, hdim), F32), V((heads, hdim), F32), V((heads, hdim), F32),
            V((8, state + cols // 2), BF16), V((2, 8, state + cols // 2), BF16), V((2, rows, 16), BF16),
            V((16, cols // 2), BF16),
            V((rows, cols), F32), V((rows, cols), F32), V((rows, hdim), F32),
            V((1, rows), F32), V((head_size - 1, 1, rows), F32), V((8, cols), BF16), V((8, 2 * state), BF16),
            V((8, cols // 2 + 2 * state), BF16), DMA((2,)),
            DMA((10,)), DMA((chunks,)), DMA, DMA, DMA, *[DMA((2,)) for _ in range(4)],
            DMA, DMA((some,)), DMA, DMA((some,)), DMA, DMA((chunks // 2,)),
            DMA, DMA((head_size - 1,)),
        ],
        compiler_params=pltpu.CompilerParams(collective_id=0, has_side_effects=True, vmem_limit_bytes=40 << 20),
        name="mixer",
    )(*[pltpu.with_memory_space_constraint(operand, pltpu.HBM) for operand in operands])
    return finish_call(gated, scale, norm_gain[None, :])


def solution(mesh):
    ctx_size = mesh.shape["ctx"]

    def chosen(*args):
        row_count = args[0].shape[0]
        longest_doc = row_count * ctx_size // 4
        span_back = (longest_doc + row_count - 2) // row_count
        if span_back == 2 and ctx_size % 2 == 0:
            return short_body(*args)
        return body(*args)

    return jax.shard_map(
        chosen,
        mesh=mesh,
        in_specs=(
            P("ctx", "head"),
            P("ctx", "head"),
            P("ctx", None),
            P("head", "ctx"),
            P("ctx"),
            P(None, "head"),
            P("head"),
            P(),
            P(),
            P("head"),
            P("head"),
            P("head"),
            P("head"),
        ),
        out_specs=P("ctx", "head"),
        check_vma=False,
    )
```

```python
import functools

import jax
import jax.numpy as jnp
from jax import lax
from jax.experimental import pallas as pl
from jax.experimental.pallas import tpu as pltpu
from jax.sharding import PartitionSpec as P


def passed_along(block, axis, distance):
    devices = range(lax.axis_size(axis))
    route = [(i - distance, i) for i in devices if i - distance in devices]
    return lax.ppermute(block, axis, route)


def causal_taps(values, rim_rows, kernel_taps, kernel_bias, offsets):
    row_count = values.shape[0]
    tap_count = kernel_taps.shape[0]
    joined = jnp.concatenate([rim_rows, values], axis=0).astype(jnp.float32)
    summed = jnp.broadcast_to(kernel_bias[None, :], values.shape)
    for tap_index in range(tap_count):
        tap_lag = tap_count - 1 - tap_index
        window_rows = lax.slice_in_dim(joined, tap_index, tap_index + row_count, axis=0)
        summed = summed + jnp.where(
            (offsets >= tap_lag)[:, None], kernel_taps[tap_index][None, :] * window_rows, 0.0
        )
    return jax.nn.silu(summed).astype(jnp.bfloat16)


def combine_states(earlier_part, later_part):
    return (
        earlier_part[0] * later_part[0],
        later_part[0][:, None, None] * earlier_part[1] + later_part[1],
    )


def body(
    feat_in,
    gate_in,
    state_proj,
    step_raw,
    doc_offset,
    feat_taps,
    feat_bias,
    proj_taps,
    proj_bias,
    step_bias,
    decay_log,
    skip_gain,
    norm_gain,
):
    head_count = step_raw.shape[0]
    row_count = feat_in.shape[0]
    head_dim = feat_in.shape[1] // head_count
    state_size = state_proj.shape[1] // 2
    tap_count = feat_taps.shape[0]
    rim_feat, rim_proj = passed_along(
        (feat_in[row_count - tap_count + 1 :], state_proj[row_count - tap_count + 1 :]), "ctx", 1
    )
    conv_feat = causal_taps(feat_in, rim_feat, feat_taps, feat_bias, doc_offset)
    conv_proj = causal_taps(state_proj, rim_proj, proj_taps, proj_bias, doc_offset)
    step_all = jax.nn.softplus(step_raw + step_bias[:, None])
    rate_all = step_all * (-jnp.exp(decay_log))[:, None]
    block_rows = min(512, row_count)
    position = jnp.arange(block_rows, dtype=jnp.int32)
    causal = position[None, :] <= position[:, None]
    final_row = block_rows - 1
    element_decay = jnp.ones((head_count,), jnp.float32)
    element_state = jnp.zeros((head_count, head_dim, state_size), jnp.float32)
    block_index = 0
    start = block_index * block_rows
    feat_block = conv_feat.reshape(block_rows, head_count, head_dim)
    in_block = conv_proj[start : start + block_rows, :state_size]
    out_block = conv_proj[start : start + block_rows, state_size:]
    cumulative = jnp.cumsum(rate_all, axis=1)
    same_doc = causal & (doc_offset[:, None] >= position[:, None] - position[None, :])
    scores = jnp.dot(out_block, in_block.T, preferred_element_type=jnp.float32)
    exponent_gap = jnp.where(
        same_doc[None], cumulative[:, :, None] - cumulative[:, None, :], -jnp.inf
    )
    weights = (scores[None] * jnp.exp(exponent_gap) * step_all[:, None, :]).astype(jnp.bfloat16)
    inner_out = jnp.einsum("hts,shp->thp", weights, feat_block, preferred_element_type=jnp.float32)
    reaches = doc_offset >= position + 1
    tail_mask = doc_offset[final_row] >= final_row - position
    tail_coef = jnp.where(
        tail_mask[None, :],
        jnp.exp(cumulative[:, final_row : final_row + 1] - cumulative) * step_all,
        0.0,
    )
    scaled = (in_block.astype(jnp.float32)[None] * tail_coef[:, :, None]).astype(jnp.bfloat16)
    contrib = jnp.einsum("shp,hsn->hpn", feat_block, scaled, preferred_element_type=jnp.float32)
    keep_factor = jnp.where(reaches[final_row], jnp.exp(cumulative[:, final_row]), 0.0)
    saved_blocks = [(feat_block, out_block, cumulative, reaches, inner_out, contrib, keep_factor)]
    element_state = keep_factor[:, None, None] * element_state + contrib
    element_decay = element_decay * keep_factor
    longest_doc = row_count * lax.axis_size("ctx") // 4
    span_back = (longest_doc + row_count - 2) // row_count
    distances = [1]
    window_size = 1
    while window_size < span_back:
        distances.append(window_size)
        window_size = window_size * 2
    current = (element_decay, element_state)
    for turn_index, distance in enumerate(distances):
        moved = passed_along((current[0], current[1]), "ctx", distance)
        if turn_index == 0:
            current = moved
        else:
            current = combine_states(moved, current)
    start_state = current[1]
    pieces_out = []
    for block_index, saved in enumerate(saved_blocks):
        feat_block, out_block, cumulative, reaches, inner_out, contrib, keep_factor = saved
        lift_factor = jnp.where(reaches[None, :], jnp.exp(cumulative), 0.0)
        from_state = (
            jnp.einsum(
                "tn,hpn->thp",
                out_block.astype(jnp.float32),
                start_state,
                precision=lax.Precision.HIGHEST,
            )
            * lift_factor.T[:, :, None]
        )
        pieces_out.append(
            inner_out + from_state + skip_gain[None, :, None] * feat_block.astype(jnp.float32)
        )
    mixed = pieces_out[0].reshape(row_count, head_count * head_dim)
    gated = mixed * jax.nn.silu(gate_in.astype(jnp.float32))
    squares = jnp.sum(gated * gated, axis=1)
    total_squares = lax.psum(squares, "head")
    scale = lax.rsqrt(total_squares / (head_count * head_dim * lax.axis_size("head")) + 1e-05)
    return (gated * scale[:, None] * norm_gain[None, :]).astype(jnp.bfloat16)


PAIR = 2
HOLD = 1
AHEAD = 2
EARLY = 4
STRIPE = 32

LOG2E = 1.4426950408889634
F32 = jnp.float32
BF16 = jnp.bfloat16


def to_column(row, size):
    rows = lax.broadcasted_iota(jnp.int32, (size, size), 0)
    cols = lax.broadcasted_iota(jnp.int32, (size, size), 1)
    return jnp.sum(jnp.where(rows == cols, row, 0.0), axis=1, keepdims=True)


def tap_sum(window_of, taps, bias, offsets, tap_count):
    summed = bias
    for tap_index in range(tap_count):
        tap_lag = tap_count - 1 - tap_index
        term = taps[tap_index : tap_index + 1, :] * window_of(tap_lag)
        if tap_lag:
            term = jnp.where(offsets >= float(tap_lag), term, 0.0)
        summed = summed + term
    return summed * (1.0 / (1.0 + jnp.exp(-summed)))


def running_sum(values, upper):
    first = values.astype(BF16)
    left = values - first.astype(F32)
    second = left.astype(BF16)
    third = (left - second.astype(F32)).astype(BF16)
    count = values.shape[0]
    sums = jnp.dot(jnp.concatenate([first, second, third], axis=0), upper, preferred_element_type=F32)
    return sums[:count] + sums[count : 2 * count] + sums[2 * count :]


def mixer_kernel(
    ctx_size, head_size, pair,
    feat_hbm, gate_hbm, proj_hbm, step_hbm, offset_hbm, taps_hbm, bias_hbm,
    ptaps_hbm, pbias_hbm, sbias_hbm, dlog_hbm, skip_hbm,
    gated, scale_ref,
    step_ref, offset_ref, taps_ref, bias_ref, ptaps_ref, pbias_ref, sbias_ref, dlog_ref, skip_ref,
    feat, gate, proj, xs, xp, rim, conv, in_t, bc, out_b, masked, cb, a_rows, coef, coef_top,
    offs, skips, own, send, arecv, srecv, sout, lsend, lrecv, kown, kmate, kprev,
    top, tin, ext, xt, yv, g2, part, sq, sqr, tail, tail_proj, tail_half, tail_sems,
    small_sems, feat_sems, gate_sem, halo_send, halo_recv, keep_send, keep_recv, top_send, top_recv,
    asend, arecv_sem, ssend, srecv_sem, fsend, lrecv_sem, sqsend, sqrecv,
):
    d = lax.axis_index("ctx")
    hd = lax.axis_index("head")
    rows, cols = feat.shape
    heads = step_ref.shape[0]
    hdim = cols // heads
    state = in_t.shape[0]
    taps_n = taps_ref.shape[0]
    edge = taps_n - 1
    width = pair * hdim
    chunks = heads // pair
    half = rows // 2
    odd = d % 2 == 1
    even = d % 2 == 0
    parity = d % 2
    first_core = hd % 2 == 0
    mate = d + 1 - 2 * parity
    part_heads = heads // 2
    part_chunks = chunks // 2
    mine = parity * part_heads
    theirs = part_heads - mine
    cross = pair if part_heads > 2 * pair else 0
    single = part_heads - cross
    single_chunks = single // pair
    moved = single + 2 * cross
    moved_chunks = moved // pair
    sends_early = even | (d + 1 < ctx_size)
    gets_early = odd | (d + 2 < ctx_size)
    sends_late = even | (d >= 2)
    gets_late = odd | (d >= 2)

    def cols_of(h, count):
        return pl.ds(pl.multiple_of(h * hdim, hdim), count * hdim)

    def chunk_cols(c):
        return pl.ds(pl.multiple_of(c * width, width), width)

    def feat_copy(c):
        return pltpu.make_async_copy(feat_hbm.at[:, chunk_cols(c)], feat.at[:, chunk_cols(c)], feat_sems.at[c])

    gate_copy = pltpu.make_async_copy(gate_hbm, gate, gate_sem)

    def remote(src, dst, ssem, rsem, where):
        return pltpu.make_async_remote_copy(
            src_ref=src, dst_ref=dst, send_sem=ssem, recv_sem=rsem,
            device_id=where, device_id_type=pl.DeviceIdType.MESH,
        )

    barrier = pltpu.get_barrier_semaphore()
    for shift in (-2, -1, 1, 2):
        @pl.when((d + shift >= 0) & (d + shift < ctx_size))
        def _():
            pl.semaphore_signal(barrier, inc=1, device_id=(d + shift, hd), device_id_type=pl.DeviceIdType.MESH)
    for k in range(1, head_size):
        pl.semaphore_signal(
            barrier, inc=1, device_id=(d, lax.rem(hd + k, head_size)), device_id_type=pl.DeviceIdType.MESH
        )

    def cross_chunk(j):
        return j * part_chunks + single_chunks

    def ordered(i):
        if i < single_chunks:
            return mine // pair + i
        if i < moved_chunks:
            return cross_chunk(i - single_chunks)
        return theirs // pair + i - moved_chunks

    tail_copies = [
        pltpu.make_async_copy(feat_hbm.at[pl.ds(rows - 8, 8), :], tail, tail_sems.at[0]),
        pltpu.make_async_copy(proj_hbm.at[pl.ds(rows - 8, 8), :], tail_proj, tail_sems.at[1]),
    ]
    for copy in tail_copies:
        copy.start()
    small = [
        pltpu.make_async_copy(src, dst, small_sems.at[n])
        for n, (src, dst) in enumerate((
            (offset_hbm, offset_ref), (step_hbm, step_ref), (sbias_hbm, sbias_ref), (dlog_hbm, dlog_ref),
            (ptaps_hbm, ptaps_ref), (pbias_hbm, pbias_ref), (proj_hbm, proj), (taps_hbm, taps_ref),
            (bias_hbm, bias_ref), (skip_hbm, skip_ref),
        ))
    ]
    for copy in small:
        copy.start()
    for c in range(chunks):
        feat_copy(ordered(c)).start()
    gate_copy.start()

    xs[:8, :] = jnp.zeros((8, cols), F32)
    xp[:8, :] = jnp.zeros((8, 2 * state), F32)
    part[...] = jnp.zeros_like(part)

    upper = (
        lax.broadcasted_iota(jnp.int32, (rows, rows), 0) <= lax.broadcasted_iota(jnp.int32, (rows, rows), 1)
    ).astype(F32).astype(BF16)
    for copy in small[:4]:
        copy.wait()
    offset_row = offset_ref[...].astype(F32)
    offs[...] = jnp.broadcast_to(to_column(offset_row, rows), offs.shape)
    step = jax.nn.softplus(step_ref[...] + to_column(sbias_ref[...], heads))
    rate = step * (-jnp.exp(to_column(dlog_ref[...], heads)) * LOG2E)
    cum = running_sum(rate, upper)
    shifted = cum - jnp.log(step) * LOG2E
    a_rows[...] = shifted
    last = offset_row[:, rows - 1 : rows]
    place = lax.broadcasted_iota(jnp.int32, (heads, rows), 1)
    reach = rows - 1 - place
    weight = jnp.where(last >= reach.astype(F32), jnp.exp2(cum[:, rows - 1 : rows] - shifted), 0.0)
    coef[...] = jnp.where(place >= edge, weight, 0.0)
    coef_top[...] = weight[:, :hdim]
    keep = jnp.where(last >= float(rows), jnp.exp2(cum[:, rows - 1 : rows]), 0.0)
    kown[...] = jnp.broadcast_to(keep, kown.shape)

    for copy in tail_copies:
        copy.wait()
    tail_half[:, cols // 2 :] = tail_proj[...]
    tail_half[:, : cols // 2] = jnp.concatenate(
        [tail[:, : cols // 2].astype(F32)[4:], tail[:, cols // 2 :].astype(F32)[4:]], axis=0
    ).astype(BF16)
    def proj_taps(rows_from, rows_to, cs):
        return tap_sum(
            lambda lag: xp[8 + rows_from - lag : 8 + rows_to - lag, cs], ptaps_ref[:, cs], pbias_ref[:, cs],
            offs[rows_from:rows_to, :1], taps_n,
        ).astype(BF16)

    in_cols, out_cols = slice(0, state), slice(state, 2 * state)
    for copy in small[4:]:
        copy.wait()
    xp[8:, :] = proj[...].astype(F32)
    bc[:, in_cols] = proj_taps(0, rows, in_cols)
    in_t[...] = bc[:, in_cols].astype(F32).T
    near = jnp.minimum(d, 2) + jnp.minimum(ctx_size - 1 - d, 2) + head_size - 1
    pl.semaphore_wait(barrier, near)
    halo = remote(tail_half, rim, halo_send, halo_recv, (d + 1, hd))
    keep_on = remote(kown, kprev, keep_send.at[0], keep_recv.at[0], (d + 1, hd))
    keep_back = remote(kown, kmate, keep_send.at[1], keep_recv.at[1], (d - 1, hd))
    top_one = remote(top, tin.at[0], top_send.at[0], top_recv.at[0], (d + 1, hd))
    top_two = remote(top, tin.at[1], top_send.at[1], top_recv.at[1], (d + 2, hd))

    @pl.when(d + 1 < ctx_size)
    def _():
        halo.start()
        keep_on.start()

    @pl.when(odd)
    def _():
        keep_back.start()

    def conv_all(c):
        feat_copy(c).wait()
        sl = chunk_cols(c)
        xs[8:, sl] = feat[:, sl].astype(F32)
        conv[:, sl] = tap_sum(
            lambda lag: xs[8 - lag : 8 + rows - lag, sl], taps_ref[:, sl], bias_ref[:, sl], offs[:, :1], taps_n
        ).astype(BF16)

    def a_copy(r):
        return remote(send.at[r], arecv.at[r], asend, arecv_sem.at[r], (mate, hd))

    def direct_copy(r):
        return remote(send.at[r], srecv.at[r], ssend, srecv_sem.at[r], (d + 2, hd))

    def s_copy(r):
        return remote(sout.at[r], srecv.at[r], ssend, srecv_sem.at[r], (d + 2, hd))

    def f_copy(r):
        return remote(lsend.at[r], lrecv.at[r], fsend, lrecv_sem.at[r // pair], (mate, hd))

    def g_copy(r):
        return remote(srecv.at[r], lrecv.at[r], fsend, lrecv_sem.at[r // pair], (mate, hd))

    def contrib(h):
        scaled = (in_t[...] * coef[pl.ds(h, 1), :]).astype(BF16)
        return jnp.dot(scaled, conv[:, cols_of(h, 1)], preferred_element_type=F32)

    def held_back(i):
        @pl.when((i >= 0) & (i < moved_chunks) & sends_early & jnp.logical_not(first_core))
        def _():
            for k in range(pair):
                a_copy(i * pair + k).start()

    def sent(c, slot, keeps):
        conv_all(c)
        for k in range(pair):
            r = slot * pair + k
            got = contrib(c * pair + k)
            send[r] = got.astype(BF16)
            if keeps:
                own[r] = got

            @pl.when(sends_early & first_core)
            def _():
                a_copy(r).start()

            if keeps:
                @pl.when(odd & (d + 2 < ctx_size))
                def _():
                    direct_copy(r).start()

        held_back(slot - HOLD)

    def mine_body(i, _):
        sent(mine // pair + i, i, False)
        return 0

    def cross_body(i, _):
        sent(cross_chunk(i), single_chunks + i, True)
        return 0

    def theirs_body(i, _):
        held_back(moved_chunks + i - HOLD)
        conv_all(theirs // pair + i)
        for k in range(pair):
            r = i * pair + k
            own[r] = contrib(theirs + r)

        @pl.when(odd & (i >= 1) & (i <= AHEAD))
        def _():
            relay(i - 1)

        return 0

    lax.fori_loop(0, single_chunks, mine_body, 0)
    lax.fori_loop(0, moved_chunks - single_chunks, cross_body, 0)

    @pl.when(d == 0)
    def _():
        rim[...] = jnp.zeros_like(rim)
        lrecv[...] = jnp.zeros_like(lrecv)
        kprev[...] = jnp.zeros_like(kprev)
        tin[0] = jnp.zeros(tin.shape[1:], BF16)

    @pl.when(d < 2)
    def _():
        srecv[...] = jnp.zeros_like(srecv)
        tin[1] = jnp.zeros(tin.shape[1:], BF16)


    @pl.when(d > 0)
    def _():
        keep_on.wait_recv()

    @pl.when(even)
    def _():
        keep_back.wait_recv()

    def relay(r):
        h = theirs + r

        @pl.when(gets_early)
        def _():
            a_copy(r).wait_recv()

        @pl.when((d + 2 < ctx_size) & even)
        def _():
            sout[r] = (arecv[r].astype(F32) + kmate[pl.ds(h, 1), :] * own[r]).astype(BF16)
            s_copy(r).start()

        @pl.when((d + 2 < ctx_size) & odd)
        def _():
            sout[r] = (own[r] + kown[pl.ds(h, 1), :] * arecv[r].astype(F32)).astype(BF16)
            s_copy(r).start()

    def pass_on(r):
        @pl.when(d >= 2)
        def _():
            s_copy(r).wait_recv()

        @pl.when(even)
        def _():
            lsend[r] = (own[r] + kown[pl.ds(theirs + r, 1), :] * srecv[r].astype(F32)).astype(BF16)
            f_copy(r).start()

        @pl.when(odd & (d >= 2))
        def _():
            g_copy(r).start()

    ahead = jnp.where(odd, min(AHEAD, single_chunks - 1), 0)
    lax.fori_loop(0, single_chunks, theirs_body, 0)
    cum_t = cum.T

    def spread(some):
        for h in some:
            cb[h] = jnp.broadcast_to(cum_t[:, h : h + 1], (rows, hdim))

    fill = [lambda: spread(range(part_heads)), lambda: spread(range(part_heads, heads))]
    ready = len(fill)
    for r in range(ready):
        relay(ahead + r)
        fill[r]()
    skips[...] = jnp.broadcast_to(to_column(skip_ref[...], heads), skips.shape)

    @pl.when(d > 0)
    def _():
        halo.wait_recv()

    xp[:8, :] = rim[:, cols // 2 :].astype(F32)
    bc[:16, in_cols] = proj_taps(0, 16, in_cols)
    out_b[...] = proj_taps(0, rows, out_cols)
    for c in range(cols // 512):
        sl = slice(c * 512, (c + 1) * 512)
        first = c * 512 < cols // 2
        arrived = rim[:, (c * 512) % (cols // 2) : (c * 512) % (cols // 2) + 512].astype(F32)
        xs[:8, sl] = jnp.concatenate([arrived[:4], arrived[:4]], axis=0) if first else arrived
        conv[:16, sl] = tap_sum(
            lambda lag: xs[8 - lag : 24 - lag, sl], taps_ref[:, sl], bias_ref[:, sl], offs[:16, :1], taps_n
        ).astype(BF16)
    weight_t = coef_top[...].T[:8, :]
    row_id = lax.broadcasted_iota(jnp.int32, weight_t.shape, 0)
    weight_t = jnp.where(row_id < edge, weight_t, 0.0)
    in_top = bc[:8, :state].astype(F32)
    top[:, :state] = jnp.concatenate([in_top[:4], in_top[:4]], axis=0).astype(BF16)
    for r in range(part_heads):
        rows_of = [
            (conv[:8, h * hdim : (h + 1) * hdim].astype(F32) * weight_t[:, h : h + 1])[:4] for h in (r, part_heads + r)
        ]
        top[:, state + r * hdim : state + (r + 1) * hdim] = jnp.concatenate(rows_of, axis=0).astype(BF16)

    @pl.when(d + 1 < ctx_size)
    def _():
        top_one.start()

    @pl.when(d + 2 < ctx_size)
    def _():
        top_two.start()

    in_b = bc[...]
    scores = lax.dot_general(out_b[...], in_b, (((1,), (1,)), ((), ())), preferred_element_type=F32)
    ti = lax.broadcasted_iota(jnp.int32, (rows, rows), 0)
    si = lax.broadcasted_iota(jnp.int32, (rows, rows), 1)
    gap = ti - si
    masked[...] = jnp.where((gap >= 0) & (offs[:, :1] >= gap.astype(F32)), scores, 0.0)

    def local_part(h):
        for _ in range(1):
            fcols = cols_of(h, 1)
            arow = a_rows[pl.ds(h, 1), :]
            cbv = cb[h]
            w0 = (jnp.exp2(jnp.minimum(cbv - arow[:, :half], 126.0)) * masked[:, :half]).astype(BF16)
            w1 = (jnp.exp2(jnp.minimum(cbv[half:] - arow[:, half:], 126.0)) * masked[half:, half:]).astype(BF16)
            fv = conv[:, fcols]
            first = jnp.dot(w0, fv[:half], preferred_element_type=F32)
            second = jnp.dot(w1, fv[half:], preferred_element_type=F32)
            inner = jnp.concatenate([first[:half], first[half:] + second], axis=0)
            gv = gate[:, fcols].astype(F32)
            sg = gv * (1.0 / (1.0 + jnp.exp(-gv)))
            yv[:, fcols] = (inner + skips[pl.ds(h, 1), :] * fv.astype(F32)) * sg
            tpos = lax.broadcasted_iota(jnp.int32, (rows, hdim), 0)
            lift = jnp.where(offs[...] >= (tpos + 1).astype(F32), jnp.exp2(cbv), 0.0)
            g2[:, fcols] = lift * sg

    def early_terms():
        @pl.when(d > 0)
        def _():
            top_one.wait_recv()

        @pl.when(d > 1)
        def _():
            top_two.wait_recv()

        firsts = jnp.concatenate([tin[0, :, :state], tin[1, :, :state]], axis=0)
        marks = lax.dot_general(out_b[...], firsts, (((1,), (1,)), ((), ())), preferred_element_type=F32)
        lane = lax.broadcasted_iota(jnp.int32, marks.shape, 1) % 8
        ext[0] = jnp.where(lane < 4, marks, 0.0).astype(BF16)
        ext[1] = jnp.where(lane < 4, 0.0, marks).astype(BF16)
        near_rows = lax.broadcasted_iota(jnp.int32, (8, hdim), 0)
        for r in range(part_heads):
            cs = slice(state + r * hdim, state + (r + 1) * hdim)
            decay = jnp.where(near_rows < 4, kprev[r : r + 1, :], kprev[part_heads + r : part_heads + r + 1, :])
            xt[:, r * hdim : (r + 1) * hdim] = jnp.concatenate(
                [tin[0, :, cs].astype(F32), tin[1, :, cs].astype(F32) * decay], axis=0
            ).astype(BF16)

    def finish(side, r, st):
        sl = cols_of(side * part_heads + r, pair)
        fs = jnp.dot(out_b[...], st, preferred_element_type=F32)
        fs = fs + jnp.dot(ext[side], xt[:, cols_of(r, pair)], preferred_element_type=F32)
        gt = yv[:, sl] + fs * g2[:, sl]
        gated[:, sl] = gt.astype(gated.dtype)
        squares = gt * gt
        total = squares[:, :hdim]
        for k in range(1, pair):
            total = total + squares[:, k * hdim : (k + 1) * hdim]
        part[...] += total

    def finish_received(r, side_even, side_odd, row):
        @pl.when(even)
        def _():
            finish(side_even, row, jnp.concatenate([srecv[r + k] for k in range(pair)], axis=1))

        @pl.when(odd)
        def _():
            finish(side_odd, row, jnp.concatenate([
                (
                    arecv[r + k].astype(F32)
                    + kprev[side_odd * part_heads + row + k : side_odd * part_heads + row + k + 1, :]
                    * srecv[r + k].astype(F32)
                ).astype(BF16)
                for k in range(pair)
            ], axis=1))

    begun = ahead + ready
    early = min(EARLY, single)

    def first_body(i, _):
        relay(i)
        local_part(i - begun)
        return 0

    def both_body(i, _):
        local_part(i - begun)
        pass_on(i - early)
        relay(i)
        return 0

    def cross_relay(x):
        r = single + x

        @pl.when(gets_early)
        def _():
            a_copy(r).wait_recv()

        @pl.when((d + 2 < ctx_size) & even)
        def _():
            h = x // pair * part_heads + single + x % pair
            sout[r] = (arecv[r].astype(F32) + kmate[pl.ds(h, 1), :] * own[r]).astype(BF16)
            s_copy(r).start()

    def second_body(i, _):
        for k in range(2):
            h = single - begun + 2 * (i - single + early) + k

            @pl.when(h < heads)
            def _():
                local_part(h)

            if k == 0:
                pass_on(i)

        x = i - single + early

        @pl.when(x < moved - single)
        def _():
            cross_relay(x)

        return 0

    def left_body(h, _):
        local_part(h)
        return 0

    gate_copy.wait()
    lax.fori_loop(begun, early, first_body, 0)
    lax.fori_loop(early, single, both_body, 0)
    lax.fori_loop(single - early, single, second_body, 0)
    lax.fori_loop(single - begun + 2 * early, heads, left_body, 0)
    for x in range(early, moved - single):
        cross_relay(x)
    early_terms()
    for r in range(0, single, pair):
        finish_received(r, 1, 0, r)

    for j in range(single_chunks):
        r = j * pair

        if j == single_chunks - 1:
            for x in range((moved - single) // pair):
                at = single + x * pair

                @pl.when(d >= 2)
                def _():
                    for k in range(pair):
                        s_copy(at + k).wait_recv()

                finish_received(at, x, x, single)

        @pl.when(gets_late)
        def _():
            some = pl.ds(r, pair)
            remote(lsend.at[some], lrecv.at[some], fsend, lrecv_sem.at[j], (mate, hd)).wait_recv()

        finish(parity, r, jnp.concatenate([lrecv[r + k] for k in range(pair)], axis=1))

    sq[...] = jnp.sum(part[...].T, axis=0, keepdims=True)

    def sq_copy(k):
        return remote(
            sq, sqr.at[k - 1], sqsend, sqrecv.at[k - 1], (d, lax.rem(hd + k, head_size))
        )

    for k in range(1, head_size):
        sq_copy(k).start()

    @pl.when(d + 1 < ctx_size)
    def _():
        halo.wait_send()
        keep_on.wait_send()
        top_one.wait_send()

    @pl.when(d + 2 < ctx_size)
    def _():
        top_two.wait_send()

    @pl.when(odd)
    def _():
        keep_back.wait_send()

    @pl.when(sends_early)
    def _():
        remote(send, arecv, asend, arecv_sem.at[0], (mate, hd)).wait_send()

    @pl.when(d + 2 < ctx_size)
    def _():
        remote(send, srecv, ssend, srecv_sem.at[0], (d + 2, hd)).wait_send()

    @pl.when(sends_late)
    def _():
        remote(lsend, lrecv, fsend, lrecv_sem.at[0], (mate, hd)).wait_send()

    total = sq[...]
    for k in range(1, head_size):
        sq_copy(k).wait_recv()
        total = total + sqr[k - 1]
    scale = lax.rsqrt(total / (cols * head_size) + 1e-05)
    scale_ref[...] = jnp.broadcast_to(scale, (hdim, rows)).T
    remote(sqr, sqr, sqsend, sqrecv.at[0], (d, lax.rem(hd + 1, head_size))).wait_send()


def scale_kernel(gated_ref, scale_ref, gain_ref, out_hbm, staged, sems):
    rows, cols = staged.shape
    lanes = scale_ref.shape[1]
    stripe = min(STRIPE, rows)

    def out_copy(r):
        rs = pl.ds(r * stripe, stripe)
        return pltpu.make_async_copy(staged.at[rs, :], out_hbm.at[rs, :], sems.at[r])

    for r in range(rows // stripe):
        rs = slice(r * stripe, (r + 1) * stripe)
        scale = scale_ref[rs, :]
        for c in range(cols // lanes):
            cs = slice(c * lanes, (c + 1) * lanes)
            staged[rs, cs] = (gated_ref[rs, cs].astype(F32) * scale * gain_ref[:, cs]).astype(BF16)
        out_copy(r).start()
    for r in range(rows // stripe):
        out_copy(r).wait()


def finish_call(gated, scale, gain):
    rows, cols = gated.shape
    vm = pl.BlockSpec(memory_space=pltpu.VMEM)
    return pl.pallas_call(
        scale_kernel,
        out_shape=jax.ShapeDtypeStruct((rows, cols), BF16),
        in_specs=[vm, vm, vm],
        out_specs=pl.BlockSpec(memory_space=pltpu.HBM),
        scratch_shapes=[
            pltpu.VMEM((rows, cols), BF16), pltpu.SemaphoreType.DMA((rows // min(STRIPE, rows),)),
        ],
        compiler_params=pltpu.CompilerParams(vmem_limit_bytes=8 << 20),
        name="scale",
    )(gated, scale, gain)


def short_body(
    feat_in, gate_in, state_proj, step_raw, doc_offset, feat_taps, feat_bias,
    proj_taps, proj_bias, step_bias, decay_log, skip_gain, norm_gain,
):
    heads, rows = step_raw.shape
    cols = feat_in.shape[1]
    hdim = cols // heads
    state = state_proj.shape[1] // 2
    taps = feat_taps.shape[0]
    ctx_size = lax.axis_size("ctx")
    head_size = lax.axis_size("head")
    pair = PAIR
    chunks = heads // pair
    some = heads // 2
    vm = pl.BlockSpec(memory_space=pltpu.VMEM)
    hbm = pl.BlockSpec(memory_space=pltpu.HBM)
    V = pltpu.VMEM
    DMA = pltpu.SemaphoreType.DMA
    cross = pair if some > 2 * pair else 0
    single = some - cross
    moved = single + 2 * cross
    late_piece = (single, state, hdim)
    piece = (moved, state, hdim)
    operands = (
        feat_in, gate_in, state_proj, step_raw, doc_offset[None, :], feat_taps,
        feat_bias[None, :], proj_taps, proj_bias[None, :], step_bias[None, :], decay_log[None, :], skip_gain[None, :],
    )
    gated, scale = pl.pallas_call(
        functools.partial(mixer_kernel, ctx_size, head_size, pair),
        out_shape=(
            jax.ShapeDtypeStruct((rows, cols), BF16),
            jax.ShapeDtypeStruct((rows, hdim), F32),
        ),
        in_specs=[hbm] * len(operands),
        out_specs=(vm, vm),
        scratch_shapes=[
            V((heads, rows), F32), V((1, rows), jnp.int32), V((taps, cols), F32), V((1, cols), F32),
            V((taps, 2 * state), F32), V((1, 2 * state), F32), V((1, heads), F32), V((1, heads), F32),
            V((1, heads), F32),
            V((rows, cols), BF16), V((rows, cols), BF16), V((rows, 2 * state), BF16),
            V((rows + 8, cols), F32), V((rows + 8, 2 * state), F32),
            V((8, cols // 2 + 2 * state), BF16), V((rows, cols), BF16),
            V((state, rows), F32), V((rows, state), BF16), V((rows, state), BF16), V((rows, rows), F32),
            V((heads, rows, hdim), F32), V((heads, rows), F32), V((heads, rows), F32), V((heads, hdim), F32),
            V((rows, hdim), F32), V((heads, hdim), F32),
            V(piece, F32), V(piece, BF16), V(piece, BF16), V(piece, BF16), V(piece, BF16), V(late_piece, BF16),
            V(late_piece, BF16),
            V((heads, hdim), F32), V((heads, hdim), F32), V((heads, hdim), F32),
            V((8, state + cols // 2), BF16), V((2, 8, state + cols // 2), BF16), V((2, rows, 16), BF16),
            V((16, cols // 2), BF16),
            V((rows, cols), F32), V((rows, cols), F32), V((rows, hdim), F32),
            V((1, rows), F32), V((head_size - 1, 1, rows), F32), V((8, cols), BF16), V((8, 2 * state), BF16),
            V((8, cols // 2 + 2 * state), BF16), DMA((2,)),
            DMA((10,)), DMA((chunks,)), DMA, DMA, DMA, *[DMA((2,)) for _ in range(4)],
            DMA, DMA((moved,)), DMA, DMA((moved,)), DMA, DMA((single // pair,)),
            DMA, DMA((head_size - 1,)),
        ],
        compiler_params=pltpu.CompilerParams(collective_id=0, has_side_effects=True, vmem_limit_bytes=40 << 20),
        name="mixer",
    )(*[pltpu.with_memory_space_constraint(operand, pltpu.HBM) for operand in operands])
    return finish_call(gated, scale, norm_gain[None, :])


def solution(mesh):
    ctx_size = mesh.shape["ctx"]

    def chosen(*args):
        row_count = args[0].shape[0]
        longest_doc = row_count * ctx_size // 4
        span_back = (longest_doc + row_count - 2) // row_count
        if span_back == 2 and ctx_size % 2 == 0:
            return short_body(*args)
        return body(*args)

    return jax.shard_map(
        chosen,
        mesh=mesh,
        in_specs=(
            P("ctx", "head"),
            P("ctx", "head"),
            P("ctx", None),
            P("head", "ctx"),
            P("ctx"),
            P(None, "head"),
            P("head"),
            P(),
            P(),
            P("head"),
            P("head"),
            P("head"),
            P("head"),
        ),
        out_specs=P("ctx", "head"),
        check_vma=False,
    )
```

```python
import functools

import jax
import jax.numpy as jnp
from jax import lax
from jax.experimental import pallas as pl
from jax.experimental.pallas import tpu as pltpu
from jax.sharding import PartitionSpec as P


def passed_along(block, axis, distance):
    devices = range(lax.axis_size(axis))
    route = [(i - distance, i) for i in devices if i - distance in devices]
    return lax.ppermute(block, axis, route)


def causal_taps(values, rim_rows, kernel_taps, kernel_bias, offsets):
    row_count = values.shape[0]
    tap_count = kernel_taps.shape[0]
    joined = jnp.concatenate([rim_rows, values], axis=0).astype(jnp.float32)
    summed = jnp.broadcast_to(kernel_bias[None, :], values.shape)
    for tap_index in range(tap_count):
        tap_lag = tap_count - 1 - tap_index
        window_rows = lax.slice_in_dim(joined, tap_index, tap_index + row_count, axis=0)
        summed = summed + jnp.where(
            (offsets >= tap_lag)[:, None], kernel_taps[tap_index][None, :] * window_rows, 0.0
        )
    return jax.nn.silu(summed).astype(jnp.bfloat16)


def combine_states(earlier_part, later_part):
    return (
        earlier_part[0] * later_part[0],
        later_part[0][:, None, None] * earlier_part[1] + later_part[1],
    )


def body(
    feat_in,
    gate_in,
    state_proj,
    step_raw,
    doc_offset,
    feat_taps,
    feat_bias,
    proj_taps,
    proj_bias,
    step_bias,
    decay_log,
    skip_gain,
    norm_gain,
):
    head_count = step_raw.shape[0]
    row_count = feat_in.shape[0]
    head_dim = feat_in.shape[1] // head_count
    state_size = state_proj.shape[1] // 2
    tap_count = feat_taps.shape[0]
    rim_feat, rim_proj = passed_along(
        (feat_in[row_count - tap_count + 1 :], state_proj[row_count - tap_count + 1 :]), "ctx", 1
    )
    conv_feat = causal_taps(feat_in, rim_feat, feat_taps, feat_bias, doc_offset)
    conv_proj = causal_taps(state_proj, rim_proj, proj_taps, proj_bias, doc_offset)
    step_all = jax.nn.softplus(step_raw + step_bias[:, None])
    rate_all = step_all * (-jnp.exp(decay_log))[:, None]
    block_rows = min(512, row_count)
    position = jnp.arange(block_rows, dtype=jnp.int32)
    causal = position[None, :] <= position[:, None]
    final_row = block_rows - 1
    element_decay = jnp.ones((head_count,), jnp.float32)
    element_state = jnp.zeros((head_count, head_dim, state_size), jnp.float32)
    block_index = 0
    start = block_index * block_rows
    feat_block = conv_feat.reshape(block_rows, head_count, head_dim)
    in_block = conv_proj[start : start + block_rows, :state_size]
    out_block = conv_proj[start : start + block_rows, state_size:]
    cumulative = jnp.cumsum(rate_all, axis=1)
    same_doc = causal & (doc_offset[:, None] >= position[:, None] - position[None, :])
    scores = jnp.dot(out_block, in_block.T, preferred_element_type=jnp.float32)
    exponent_gap = jnp.where(
        same_doc[None], cumulative[:, :, None] - cumulative[:, None, :], -jnp.inf
    )
    weights = (scores[None] * jnp.exp(exponent_gap) * step_all[:, None, :]).astype(jnp.bfloat16)
    inner_out = jnp.einsum("hts,shp->thp", weights, feat_block, preferred_element_type=jnp.float32)
    reaches = doc_offset >= position + 1
    tail_mask = doc_offset[final_row] >= final_row - position
    tail_coef = jnp.where(
        tail_mask[None, :],
        jnp.exp(cumulative[:, final_row : final_row + 1] - cumulative) * step_all,
        0.0,
    )
    scaled = (in_block.astype(jnp.float32)[None] * tail_coef[:, :, None]).astype(jnp.bfloat16)
    contrib = jnp.einsum("shp,hsn->hpn", feat_block, scaled, preferred_element_type=jnp.float32)
    keep_factor = jnp.where(reaches[final_row], jnp.exp(cumulative[:, final_row]), 0.0)
    saved_blocks = [(feat_block, out_block, cumulative, reaches, inner_out, contrib, keep_factor)]
    element_state = keep_factor[:, None, None] * element_state + contrib
    element_decay = element_decay * keep_factor
    longest_doc = row_count * lax.axis_size("ctx") // 4
    span_back = (longest_doc + row_count - 2) // row_count
    distances = [1]
    window_size = 1
    while window_size < span_back:
        distances.append(window_size)
        window_size = window_size * 2
    current = (element_decay, element_state)
    for turn_index, distance in enumerate(distances):
        moved = passed_along((current[0], current[1]), "ctx", distance)
        if turn_index == 0:
            current = moved
        else:
            current = combine_states(moved, current)
    start_state = current[1]
    pieces_out = []
    for block_index, saved in enumerate(saved_blocks):
        feat_block, out_block, cumulative, reaches, inner_out, contrib, keep_factor = saved
        lift_factor = jnp.where(reaches[None, :], jnp.exp(cumulative), 0.0)
        from_state = (
            jnp.einsum(
                "tn,hpn->thp",
                out_block.astype(jnp.float32),
                start_state,
                precision=lax.Precision.HIGHEST,
            )
            * lift_factor.T[:, :, None]
        )
        pieces_out.append(
            inner_out + from_state + skip_gain[None, :, None] * feat_block.astype(jnp.float32)
        )
    mixed = pieces_out[0].reshape(row_count, head_count * head_dim)
    gated = mixed * jax.nn.silu(gate_in.astype(jnp.float32))
    squares = jnp.sum(gated * gated, axis=1)
    total_squares = lax.psum(squares, "head")
    scale = lax.rsqrt(total_squares / (head_count * head_dim * lax.axis_size("head")) + 1e-05)
    return (gated * scale[:, None] * norm_gain[None, :]).astype(jnp.bfloat16)


PAIR = 2
HOLD = 1
AHEAD = 2
EARLY = 4
STRIPE = 32

LOG2E = 1.4426950408889634
F32 = jnp.float32
BF16 = jnp.bfloat16


def to_column(row, size):
    rows = lax.broadcasted_iota(jnp.int32, (size, size), 0)
    cols = lax.broadcasted_iota(jnp.int32, (size, size), 1)
    return jnp.sum(jnp.where(rows == cols, row, 0.0), axis=1, keepdims=True)


def tap_sum(window_of, taps, bias, offsets, tap_count):
    summed = bias
    for tap_index in range(tap_count):
        tap_lag = tap_count - 1 - tap_index
        term = taps[tap_index : tap_index + 1, :] * window_of(tap_lag)
        if tap_lag:
            term = jnp.where(offsets >= float(tap_lag), term, 0.0)
        summed = summed + term
    return summed * (1.0 / (1.0 + jnp.exp(-summed)))


def running_sum(values, upper):
    first = values.astype(BF16)
    left = values - first.astype(F32)
    second = left.astype(BF16)
    third = (left - second.astype(F32)).astype(BF16)
    count = values.shape[0]
    sums = jnp.dot(jnp.concatenate([first, second, third], axis=0), upper, preferred_element_type=F32)
    return sums[:count] + sums[count : 2 * count] + sums[2 * count :]


def mixer_kernel(
    ctx_size, head_size, pair,
    feat_hbm, gate_hbm, proj_hbm, step_hbm, offset_hbm, taps_hbm, bias_hbm,
    ptaps_hbm, pbias_hbm, sbias_hbm, dlog_hbm, skip_hbm,
    gated, scale_ref,
    step_ref, offset_ref, taps_ref, bias_ref, ptaps_ref, pbias_ref, sbias_ref, dlog_ref, skip_ref,
    feat, gate, proj, xs, xp, rim, conv, in_t, bc, out_b, masked, cb, a_rows, coef, coef_top,
    offs, skips, own, send, arecv, srecv, sout, lsend, lrecv, kown, kmate, kprev,
    top, tin, ext, xt, yv, g2, part, sq, sqr, tail, tail_proj, tail_half, tail_sems,
    small_sems, feat_sems, halo_recv, keep_recv, top_recv, arecv_sem, srecv_sem, lrecv_sem, sqrecv,
):
    d = lax.axis_index("ctx")
    hd = lax.axis_index("head")
    rows, cols = feat.shape
    heads = step_ref.shape[0]
    hdim = cols // heads
    state = in_t.shape[0]
    taps_n = taps_ref.shape[0]
    edge = taps_n - 1
    width = pair * hdim
    chunks = heads // pair
    half = rows // 2
    odd = d % 2 == 1
    even = d % 2 == 0
    parity = d % 2
    first_core = hd % 2 == 0
    mate = d + 1 - 2 * parity
    part_heads = heads // 2
    part_chunks = chunks // 2
    mine = parity * part_heads
    theirs = part_heads - mine
    cross = pair if part_heads > 2 * pair else 0
    single = part_heads - cross
    single_chunks = single // pair
    moved = single + 2 * cross
    moved_chunks = moved // pair
    sends_early = even | (d + 1 < ctx_size)
    gets_early = odd | (d + 2 < ctx_size)
    sends_late = even | (d >= 2)
    gets_late = odd | (d >= 2)

    halo_send, keep_send, top_send = small_sems.at[0], small_sems.at[pl.ds(1, 2)], small_sems.at[pl.ds(3, 2)]
    asend, ssend, fsend, sqsend = (small_sems.at[n] for n in range(5, 9))
    gate_sem = small_sems.at[9]

    def cols_of(h, count):
        return pl.ds(pl.multiple_of(h * hdim, hdim), count * hdim)

    def chunk_cols(c):
        return pl.ds(pl.multiple_of(c * width, width), width)

    def feat_copy(c):
        return pltpu.make_async_copy(feat_hbm.at[:, chunk_cols(c)], feat.at[:, chunk_cols(c)], feat_sems.at[c])

    gate_copy = pltpu.make_async_copy(gate_hbm, gate, gate_sem)

    def remote(src, dst, ssem, rsem, where):
        return pltpu.make_async_remote_copy(
            src_ref=src, dst_ref=dst, send_sem=ssem, recv_sem=rsem,
            device_id=where, device_id_type=pl.DeviceIdType.MESH,
        )

    barrier = pltpu.get_barrier_semaphore()
    for shift in (-2, -1, 1, 2):
        @pl.when((d + shift >= 0) & (d + shift < ctx_size))
        def _():
            pl.semaphore_signal(barrier, inc=1, device_id=(d + shift, hd), device_id_type=pl.DeviceIdType.MESH)
    for k in range(1, head_size):
        pl.semaphore_signal(
            barrier, inc=1, device_id=(d, lax.rem(hd + k, head_size)), device_id_type=pl.DeviceIdType.MESH
        )

    def cross_chunk(j):
        return j * part_chunks + single_chunks

    def ordered(i):
        if i < single_chunks:
            return mine // pair + i
        if i < moved_chunks:
            return cross_chunk(i - single_chunks)
        return theirs // pair + i - moved_chunks

    tail_copies = [
        pltpu.make_async_copy(feat_hbm.at[pl.ds(rows - 8, 8), :], tail, tail_sems.at[0]),
        pltpu.make_async_copy(proj_hbm.at[pl.ds(rows - 8, 8), :], tail_proj, tail_sems.at[1]),
    ]
    for copy in tail_copies:
        copy.start()
    small = [
        pltpu.make_async_copy(src, dst, small_sems.at[n])
        for n, (src, dst) in enumerate((
            (offset_hbm, offset_ref), (step_hbm, step_ref), (sbias_hbm, sbias_ref), (dlog_hbm, dlog_ref),
            (ptaps_hbm, ptaps_ref), (pbias_hbm, pbias_ref), (proj_hbm, proj), (taps_hbm, taps_ref),
            (bias_hbm, bias_ref), (skip_hbm, skip_ref),
        ))
    ]
    for copy in small:
        copy.start()
    for c in range(chunks):
        feat_copy(ordered(c)).start()

    xs[:8, :] = jnp.zeros((8, cols), F32)
    xp[:8, :] = jnp.zeros((8, 2 * state), F32)
    part[...] = jnp.zeros_like(part)

    upper = (
        lax.broadcasted_iota(jnp.int32, (rows, rows), 0) <= lax.broadcasted_iota(jnp.int32, (rows, rows), 1)
    ).astype(F32).astype(BF16)
    for copy in small[:4]:
        copy.wait()
    offset_row = offset_ref[...].astype(F32)
    offs[...] = jnp.broadcast_to(to_column(offset_row, rows), offs.shape)
    step = jax.nn.softplus(step_ref[...] + to_column(sbias_ref[...], heads))
    rate = step * (-jnp.exp(to_column(dlog_ref[...], heads)) * LOG2E)
    cum = running_sum(rate, upper)
    shifted = cum - jnp.log(step) * LOG2E
    a_rows[...] = shifted
    last = offset_row[:, rows - 1 : rows]
    place = lax.broadcasted_iota(jnp.int32, (heads, rows), 1)
    reach = rows - 1 - place
    weight = jnp.where(last >= reach.astype(F32), jnp.exp2(cum[:, rows - 1 : rows] - shifted), 0.0)
    coef[...] = jnp.where(place >= edge, weight, 0.0)
    coef_top[...] = weight[:, :hdim]
    keep = jnp.where(last >= float(rows), jnp.exp2(cum[:, rows - 1 : rows]), 0.0)
    kown[...] = jnp.broadcast_to(keep, kown.shape)

    for copy in tail_copies:
        copy.wait()
    tail_half[:, cols // 2 :] = tail_proj[...]
    tail_half[:, : cols // 2] = jnp.concatenate(
        [tail[:, : cols // 2].astype(F32)[4:], tail[:, cols // 2 :].astype(F32)[4:]], axis=0
    ).astype(BF16)
    def proj_taps(rows_from, rows_to, cs):
        return tap_sum(
            lambda lag: xp[8 + rows_from - lag : 8 + rows_to - lag, cs], ptaps_ref[:, cs], pbias_ref[:, cs],
            offs[rows_from:rows_to, :1], taps_n,
        ).astype(BF16)

    in_cols, out_cols = slice(0, state), slice(state, 2 * state)
    for copy in small[4:]:
        copy.wait()
    xp[8:, :] = proj[...].astype(F32)
    bc[:, in_cols] = proj_taps(0, rows, in_cols)
    in_t[...] = bc[:, in_cols].astype(F32).T
    near = jnp.minimum(d, 2) + jnp.minimum(ctx_size - 1 - d, 2) + head_size - 1
    pl.semaphore_wait(barrier, near)
    gate_copy.start()
    halo = remote(tail_half, rim, halo_send, halo_recv, (d + 1, hd))
    keep_on = remote(kown, kprev, keep_send.at[0], keep_recv.at[0], (d + 1, hd))
    keep_back = remote(kown, kmate, keep_send.at[1], keep_recv.at[1], (d - 1, hd))
    top_one = remote(top, tin.at[0], top_send.at[0], top_recv.at[0], (d + 1, hd))
    top_two = remote(top, tin.at[1], top_send.at[1], top_recv.at[1], (d + 2, hd))

    @pl.when(d + 1 < ctx_size)
    def _():
        halo.start()
        keep_on.start()

    @pl.when(odd)
    def _():
        keep_back.start()

    def conv_all(c):
        feat_copy(c).wait()
        sl = chunk_cols(c)
        xs[8:, sl] = feat[:, sl].astype(F32)
        conv[:, sl] = tap_sum(
            lambda lag: xs[8 - lag : 8 + rows - lag, sl], taps_ref[:, sl], bias_ref[:, sl], offs[:, :1], taps_n
        ).astype(BF16)

    def conv_head(h):
        sl = cols_of(h, 1)
        xs[8:, sl] = feat[:, sl].astype(F32)
        conv[:, sl] = tap_sum(
            lambda lag: xs[8 - lag : 8 + rows - lag, sl], taps_ref[:, sl], bias_ref[:, sl], offs[...], taps_n
        ).astype(BF16)

    def a_copy(r):
        return remote(send.at[r], arecv.at[r], asend, arecv_sem.at[r], (mate, hd))

    def direct_copy(r):
        return remote(send.at[r], srecv.at[r], ssend, srecv_sem.at[r], (d + 2, hd))

    def s_copy(r):
        return remote(sout.at[r], srecv.at[r], ssend, srecv_sem.at[r], (d + 2, hd))

    def late_sem(r):
        whole = single - pair
        return lrecv_sem.at[jnp.where(r < whole, r // pair, whole // pair + r - whole)]

    def f_copy(r):
        return remote(lsend.at[r], lrecv.at[r], fsend, late_sem(r), (mate, hd))

    def g_copy(r):
        return remote(srecv.at[r], lrecv.at[r], fsend, late_sem(r), (mate, hd))

    def contrib(h):
        scaled = (in_t[...] * coef[pl.ds(h, 1), :]).astype(BF16)
        return jnp.dot(scaled, conv[:, cols_of(h, 1)], preferred_element_type=F32)

    def held_back(i):
        @pl.when((i >= 0) & (i < moved_chunks) & sends_early & jnp.logical_not(first_core))
        def _():
            for k in range(pair):
                a_copy(i * pair + k).start()

    def sent(c, slot, keeps):
        feat_copy(c).wait()
        for k in range(pair):
            r = slot * pair + k
            conv_head(c * pair + k)
            got = contrib(c * pair + k)
            send[r] = got.astype(BF16)
            if keeps:
                own[r] = got

            @pl.when(sends_early & first_core)
            def _():
                a_copy(r).start()

            if keeps:
                @pl.when(odd & (d + 2 < ctx_size))
                def _():
                    direct_copy(r).start()

        held_back(slot - HOLD)

    def mine_body(i, _):
        sent(mine // pair + i, i, False)
        return 0

    def cross_body(i, _):
        sent(cross_chunk(i), single_chunks + i, True)
        return 0

    def theirs_body(i, _):
        held_back(moved_chunks + i - HOLD)
        conv_all(theirs // pair + i)
        for k in range(pair):
            r = i * pair + k
            own[r] = contrib(theirs + r)

        @pl.when(odd & (i >= 1) & (i <= AHEAD))
        def _():
            relay(i - 1)

        return 0

    lax.fori_loop(0, single_chunks, mine_body, 0)
    lax.fori_loop(0, moved_chunks - single_chunks, cross_body, 0)

    @pl.when(d == 0)
    def _():
        rim[...] = jnp.zeros_like(rim)
        lrecv[...] = jnp.zeros_like(lrecv)
        kprev[...] = jnp.zeros_like(kprev)
        tin[0] = jnp.zeros(tin.shape[1:], BF16)

    @pl.when(d < 2)
    def _():
        srecv[...] = jnp.zeros_like(srecv)
        tin[1] = jnp.zeros(tin.shape[1:], BF16)


    @pl.when(d > 0)
    def _():
        keep_on.wait_recv()

    @pl.when(even)
    def _():
        keep_back.wait_recv()

    def relay(r):
        h = theirs + r

        @pl.when(gets_early)
        def _():
            a_copy(r).wait_recv()

        @pl.when((d + 2 < ctx_size) & even)
        def _():
            sout[r] = (arecv[r].astype(F32) + kmate[pl.ds(h, 1), :] * own[r]).astype(BF16)
            s_copy(r).start()

        @pl.when((d + 2 < ctx_size) & odd)
        def _():
            sout[r] = (own[r] + kown[pl.ds(h, 1), :] * arecv[r].astype(F32)).astype(BF16)
            s_copy(r).start()

    def pass_on(r):
        @pl.when(d >= 2)
        def _():
            s_copy(r).wait_recv()

        @pl.when(even)
        def _():
            lsend[r] = (own[r] + kown[pl.ds(theirs + r, 1), :] * srecv[r].astype(F32)).astype(BF16)
            f_copy(r).start()

        @pl.when(odd & (d >= 2))
        def _():
            g_copy(r).start()

    ahead = jnp.where(odd, min(AHEAD, single_chunks - 1), 0)
    lax.fori_loop(0, single_chunks, theirs_body, 0)
    cum_t = cum.T

    def spread(some):
        for h in some:
            cb[h] = jnp.broadcast_to(cum_t[:, h : h + 1], (rows, hdim))

    fill = [lambda: spread(range(part_heads)), lambda: spread(range(part_heads, heads))]
    ready = len(fill)
    for r in range(ready):
        relay(ahead + r)
        fill[r]()
    skips[...] = jnp.broadcast_to(to_column(skip_ref[...], heads), skips.shape)

    @pl.when(d > 0)
    def _():
        halo.wait_recv()

    xp[:8, :] = rim[:, cols // 2 :].astype(F32)
    bc[:16, in_cols] = proj_taps(0, 16, in_cols)
    out_b[...] = proj_taps(0, rows, out_cols)
    for c in range(cols // 512):
        sl = slice(c * 512, (c + 1) * 512)
        first = c * 512 < cols // 2
        arrived = rim[:, (c * 512) % (cols // 2) : (c * 512) % (cols // 2) + 512].astype(F32)
        xs[:8, sl] = jnp.concatenate([arrived[:4], arrived[:4]], axis=0) if first else arrived
        conv[:16, sl] = tap_sum(
            lambda lag: xs[8 - lag : 24 - lag, sl], taps_ref[:, sl], bias_ref[:, sl], offs[:16, :1], taps_n
        ).astype(BF16)
    weight_t = coef_top[...].T[:8, :]
    row_id = lax.broadcasted_iota(jnp.int32, weight_t.shape, 0)
    weight_t = jnp.where(row_id < edge, weight_t, 0.0)
    in_top = bc[:8, :state].astype(F32)
    top[:, :state] = jnp.concatenate([in_top[:4], in_top[:4]], axis=0).astype(BF16)
    for r in range(part_heads):
        rows_of = [
            (conv[:8, h * hdim : (h + 1) * hdim].astype(F32) * weight_t[:, h : h + 1])[:4] for h in (r, part_heads + r)
        ]
        top[:, state + r * hdim : state + (r + 1) * hdim] = jnp.concatenate(rows_of, axis=0).astype(BF16)

    @pl.when(d + 1 < ctx_size)
    def _():
        top_one.start()

    @pl.when(d + 2 < ctx_size)
    def _():
        top_two.start()

    in_b = bc[...]
    scores = lax.dot_general(out_b[...], in_b, (((1,), (1,)), ((), ())), preferred_element_type=F32)
    ti = lax.broadcasted_iota(jnp.int32, (rows, rows), 0)
    si = lax.broadcasted_iota(jnp.int32, (rows, rows), 1)
    gap = ti - si
    masked[...] = jnp.where((gap >= 0) & (offs[:, :1] >= gap.astype(F32)), scores, 0.0)

    def local_part(h):
        for _ in range(1):
            fcols = cols_of(h, 1)
            arow = a_rows[pl.ds(h, 1), :]
            cbv = cb[h]
            w0 = (jnp.exp2(jnp.minimum(cbv - arow[:, :half], 126.0)) * masked[:, :half]).astype(BF16)
            w1 = (jnp.exp2(jnp.minimum(cbv[half:] - arow[:, half:], 126.0)) * masked[half:, half:]).astype(BF16)
            fv = conv[:, fcols]
            first = jnp.dot(w0, fv[:half], preferred_element_type=F32)
            second = jnp.dot(w1, fv[half:], preferred_element_type=F32)
            inner = jnp.concatenate([first[:half], first[half:] + second], axis=0)
            gv = gate[:, fcols].astype(F32)
            sg = gv * (1.0 / (1.0 + jnp.exp(-gv)))
            yv[:, fcols] = (inner + skips[pl.ds(h, 1), :] * fv.astype(F32)) * sg
            tpos = lax.broadcasted_iota(jnp.int32, (rows, hdim), 0)
            lift = jnp.where(offs[...] >= (tpos + 1).astype(F32), jnp.exp2(cbv), 0.0)
            g2[:, fcols] = lift * sg

    def early_terms():
        @pl.when(d > 0)
        def _():
            top_one.wait_recv()

        @pl.when(d > 1)
        def _():
            top_two.wait_recv()

        firsts = jnp.concatenate([tin[0, :, :state], tin[1, :, :state]], axis=0)
        marks = lax.dot_general(out_b[...], firsts, (((1,), (1,)), ((), ())), preferred_element_type=F32)
        lane = lax.broadcasted_iota(jnp.int32, marks.shape, 1) % 8
        ext[0] = jnp.where(lane < 4, marks, 0.0).astype(BF16)
        ext[1] = jnp.where(lane < 4, 0.0, marks).astype(BF16)
        near_rows = lax.broadcasted_iota(jnp.int32, (8, hdim), 0)
        for r in range(part_heads):
            cs = slice(state + r * hdim, state + (r + 1) * hdim)
            decay = jnp.where(near_rows < 4, kprev[r : r + 1, :], kprev[part_heads + r : part_heads + r + 1, :])
            xt[:, r * hdim : (r + 1) * hdim] = jnp.concatenate(
                [tin[0, :, cs].astype(F32), tin[1, :, cs].astype(F32) * decay], axis=0
            ).astype(BF16)

    def finish(side, r, st, count=pair):
        sl = cols_of(side * part_heads + r, count)
        fs = jnp.dot(out_b[...], st, preferred_element_type=F32)
        fs = fs + jnp.dot(ext[side], xt[:, cols_of(r, count)], preferred_element_type=F32)
        gt = yv[:, sl] + fs * g2[:, sl]
        gated[:, sl] = gt.astype(gated.dtype)
        squares = gt * gt
        total = squares[:, :hdim]
        for k in range(1, count):
            total = total + squares[:, k * hdim : (k + 1) * hdim]
        part[...] += total

    def finish_received(r, side_even, side_odd, row):
        @pl.when(even)
        def _():
            finish(side_even, row, jnp.concatenate([srecv[r + k] for k in range(pair)], axis=1))

        @pl.when(odd)
        def _():
            finish(side_odd, row, jnp.concatenate([
                (
                    arecv[r + k].astype(F32)
                    + kprev[side_odd * part_heads + row + k : side_odd * part_heads + row + k + 1, :]
                    * srecv[r + k].astype(F32)
                ).astype(BF16)
                for k in range(pair)
            ], axis=1))

    begun = ahead + ready
    early = min(EARLY, single)

    def first_body(i, _):
        relay(i)
        local_part(i - begun)
        return 0

    def both_body(i, _):
        local_part(i - begun)
        pass_on(i - early)
        relay(i)
        return 0

    def cross_relay(x):
        r = single + x

        @pl.when(gets_early)
        def _():
            a_copy(r).wait_recv()

        @pl.when((d + 2 < ctx_size) & even)
        def _():
            h = x // pair * part_heads + single + x % pair
            sout[r] = (arecv[r].astype(F32) + kmate[pl.ds(h, 1), :] * own[r]).astype(BF16)
            s_copy(r).start()

    def second_body(i, _):
        for k in range(2):
            h = single - begun + 2 * (i - single + early) + k

            @pl.when(h < heads)
            def _():
                local_part(h)

            if k == 0:
                pass_on(i)

        x = i - single + early

        @pl.when(x < moved - single)
        def _():
            cross_relay(x)

        return 0

    def left_body(h, _):
        local_part(h)
        return 0

    gate_copy.wait()
    lax.fori_loop(begun, early, first_body, 0)
    lax.fori_loop(early, single, both_body, 0)
    lax.fori_loop(single - early, single, second_body, 0)
    lax.fori_loop(single - begun + 2 * early, heads, left_body, 0)
    for x in range(early, moved - single):
        cross_relay(x)
    early_terms()
    for r in range(0, single, pair):
        finish_received(r, 1, 0, r)

    for j in range(single_chunks):
        r = j * pair

        if j == single_chunks - 1:
            for x in range((moved - single) // pair):
                at = single + x * pair

                @pl.when(d >= 2)
                def _():
                    for k in range(pair):
                        s_copy(at + k).wait_recv()

                finish_received(at, x, x, single)

            for k in range(pair):
                @pl.when(gets_late)
                def _():
                    f_copy(r + k).wait_recv()

                finish(parity, r + k, lrecv[r + k], 1)
        else:
            @pl.when(gets_late)
            def _():
                some = pl.ds(r, pair)
                remote(lsend.at[some], lrecv.at[some], fsend, lrecv_sem.at[j], (mate, hd)).wait_recv()

            finish(parity, r, jnp.concatenate([lrecv[r + k] for k in range(pair)], axis=1))

    sq[...] = jnp.sum(part[...].T, axis=0, keepdims=True)

    def sq_copy(k):
        return remote(
            sq, sqr.at[k - 1], sqsend, sqrecv.at[k - 1], (d, lax.rem(hd + k, head_size))
        )

    far_first = sorted(range(1, head_size), key=lambda k: (k != head_size // 2, k))
    for k in far_first:
        sq_copy(k).start()

    @pl.when(d + 1 < ctx_size)
    def _():
        halo.wait_send()
        keep_on.wait_send()
        top_one.wait_send()

    @pl.when(d + 2 < ctx_size)
    def _():
        top_two.wait_send()

    @pl.when(odd)
    def _():
        keep_back.wait_send()

    @pl.when(sends_early)
    def _():
        remote(send, arecv, asend, arecv_sem.at[0], (mate, hd)).wait_send()

    @pl.when(d + 2 < ctx_size)
    def _():
        remote(send, srecv, ssend, srecv_sem.at[0], (d + 2, hd)).wait_send()

    @pl.when(sends_late)
    def _():
        remote(lsend, lrecv, fsend, lrecv_sem.at[0], (mate, hd)).wait_send()

    total = sq[...]
    for k in range(1, head_size):
        sq_copy(k).wait_recv()
        total = total + sqr[k - 1]
    scale = lax.rsqrt(total / (cols * head_size) + 1e-05)
    scale_ref[...] = jnp.broadcast_to(scale, (hdim, rows)).T
    remote(sqr, sqr, sqsend, sqrecv.at[0], (d, lax.rem(hd + 1, head_size))).wait_send()


def scale_kernel(gated_ref, scale_ref, gain_ref, out_hbm, staged, sems):
    rows, cols = staged.shape
    lanes = scale_ref.shape[1]
    stripe = min(STRIPE, rows)

    def out_copy(r):
        rs = pl.ds(r * stripe, stripe)
        return pltpu.make_async_copy(staged.at[rs, :], out_hbm.at[rs, :], sems.at[r])

    for r in range(rows // stripe):
        rs = slice(r * stripe, (r + 1) * stripe)
        scale = scale_ref[rs, :]
        for c in range(cols // lanes):
            cs = slice(c * lanes, (c + 1) * lanes)
            staged[rs, cs] = (gated_ref[rs, cs].astype(F32) * scale * gain_ref[:, cs]).astype(BF16)
        out_copy(r).start()
    for r in range(rows // stripe):
        out_copy(r).wait()


def finish_call(gated, scale, gain):
    rows, cols = gated.shape
    vm = pl.BlockSpec(memory_space=pltpu.VMEM)
    return pl.pallas_call(
        scale_kernel,
        out_shape=jax.ShapeDtypeStruct((rows, cols), BF16),
        in_specs=[vm, vm, vm],
        out_specs=pl.BlockSpec(memory_space=pltpu.HBM),
        scratch_shapes=[
            pltpu.VMEM((rows, cols), BF16), pltpu.SemaphoreType.DMA((rows // min(STRIPE, rows),)),
        ],
        compiler_params=pltpu.CompilerParams(vmem_limit_bytes=8 << 20),
        name="scale",
    )(gated, scale, gain)


def short_body(
    feat_in, gate_in, state_proj, step_raw, doc_offset, feat_taps, feat_bias,
    proj_taps, proj_bias, step_bias, decay_log, skip_gain, norm_gain,
):
    heads, rows = step_raw.shape
    cols = feat_in.shape[1]
    hdim = cols // heads
    state = state_proj.shape[1] // 2
    taps = feat_taps.shape[0]
    ctx_size = lax.axis_size("ctx")
    head_size = lax.axis_size("head")
    pair = PAIR
    chunks = heads // pair
    some = heads // 2
    vm = pl.BlockSpec(memory_space=pltpu.VMEM)
    hbm = pl.BlockSpec(memory_space=pltpu.HBM)
    V = pltpu.VMEM
    DMA = pltpu.SemaphoreType.DMA
    cross = pair if some > 2 * pair else 0
    single = some - cross
    moved = single + 2 * cross
    late_piece = (single, state, hdim)
    piece = (moved, state, hdim)
    operands = (
        feat_in, gate_in, state_proj, step_raw, doc_offset[None, :], feat_taps,
        feat_bias[None, :], proj_taps, proj_bias[None, :], step_bias[None, :], decay_log[None, :], skip_gain[None, :],
    )
    gated, scale = pl.pallas_call(
        functools.partial(mixer_kernel, ctx_size, head_size, pair),
        out_shape=(
            jax.ShapeDtypeStruct((rows, cols), BF16),
            jax.ShapeDtypeStruct((rows, hdim), F32),
        ),
        in_specs=[hbm] * len(operands),
        out_specs=(vm, vm),
        scratch_shapes=[
            V((heads, rows), F32), V((1, rows), jnp.int32), V((taps, cols), F32), V((1, cols), F32),
            V((taps, 2 * state), F32), V((1, 2 * state), F32), V((1, heads), F32), V((1, heads), F32),
            V((1, heads), F32),
            V((rows, cols), BF16), V((rows, cols), BF16), V((rows, 2 * state), BF16),
            V((rows + 8, cols), F32), V((rows + 8, 2 * state), F32),
            V((8, cols // 2 + 2 * state), BF16), V((rows, cols), BF16),
            V((state, rows), F32), V((rows, state), BF16), V((rows, state), BF16), V((rows, rows), F32),
            V((heads, rows, hdim), F32), V((heads, rows), F32), V((heads, rows), F32), V((heads, hdim), F32),
            V((rows, hdim), F32), V((heads, hdim), F32),
            V(piece, F32), V(piece, BF16), V(piece, BF16), V(piece, BF16), V(piece, BF16), V(late_piece, BF16),
            V(late_piece, BF16),
            V((heads, hdim), F32), V((heads, hdim), F32), V((heads, hdim), F32),
            V((8, state + cols // 2), BF16), V((2, 8, state + cols // 2), BF16), V((2, rows, 16), BF16),
            V((16, cols // 2), BF16),
            V((rows, cols), F32), V((rows, cols), F32), V((rows, hdim), F32),
            V((1, rows), F32), V((head_size - 1, 1, rows), F32), V((8, cols), BF16), V((8, 2 * state), BF16),
            V((8, cols // 2 + 2 * state), BF16), DMA((2,)),
            DMA((10,)), DMA((chunks,)), DMA, DMA((2,)), DMA((2,)),
            DMA((moved,)), DMA((moved,)), DMA((single // pair + pair - 1,)), DMA((head_size - 1,)),
        ],
        compiler_params=pltpu.CompilerParams(collective_id=0, has_side_effects=True, vmem_limit_bytes=40 << 20),
        name="mixer",
    )(*[pltpu.with_memory_space_constraint(operand, pltpu.HBM) for operand in operands])
    return finish_call(gated, scale, norm_gain[None, :])


def solution(mesh):
    ctx_size = mesh.shape["ctx"]

    def chosen(*args):
        row_count = args[0].shape[0]
        longest_doc = row_count * ctx_size // 4
        span_back = (longest_doc + row_count - 2) // row_count
        if span_back == 2 and ctx_size % 2 == 0:
            return short_body(*args)
        return body(*args)

    return jax.shard_map(
        chosen,
        mesh=mesh,
        in_specs=(
            P("ctx", "head"),
            P("ctx", "head"),
            P("ctx", None),
            P("head", "ctx"),
            P("ctx"),
            P(None, "head"),
            P("head"),
            P(),
            P(),
            P("head"),
            P("head"),
            P("head"),
            P("head"),
        ),
        out_specs=P("ctx", "head"),
        check_vma=False,
    )
```

```python
import functools

import jax
import jax.numpy as jnp
from jax import lax
from jax.experimental import pallas as pl
from jax.experimental.pallas import tpu as pltpu
from jax.sharding import PartitionSpec as P


def passed_along(block, axis, distance):
    devices = range(lax.axis_size(axis))
    route = [(i - distance, i) for i in devices if i - distance in devices]
    return lax.ppermute(block, axis, route)


def causal_taps(values, rim_rows, kernel_taps, kernel_bias, offsets):
    row_count = values.shape[0]
    tap_count = kernel_taps.shape[0]
    joined = jnp.concatenate([rim_rows, values], axis=0).astype(jnp.float32)
    summed = jnp.broadcast_to(kernel_bias[None, :], values.shape)
    for tap_index in range(tap_count):
        tap_lag = tap_count - 1 - tap_index
        window_rows = lax.slice_in_dim(joined, tap_index, tap_index + row_count, axis=0)
        summed = summed + jnp.where(
            (offsets >= tap_lag)[:, None], kernel_taps[tap_index][None, :] * window_rows, 0.0
        )
    return jax.nn.silu(summed).astype(jnp.bfloat16)


def combine_states(earlier_part, later_part):
    return (
        earlier_part[0] * later_part[0],
        later_part[0][:, None, None] * earlier_part[1] + later_part[1],
    )


def body(
    feat_in,
    gate_in,
    state_proj,
    step_raw,
    doc_offset,
    feat_taps,
    feat_bias,
    proj_taps,
    proj_bias,
    step_bias,
    decay_log,
    skip_gain,
    norm_gain,
):
    head_count = step_raw.shape[0]
    row_count = feat_in.shape[0]
    head_dim = feat_in.shape[1] // head_count
    state_size = state_proj.shape[1] // 2
    tap_count = feat_taps.shape[0]
    rim_feat, rim_proj = passed_along(
        (feat_in[row_count - tap_count + 1 :], state_proj[row_count - tap_count + 1 :]), "ctx", 1
    )
    conv_feat = causal_taps(feat_in, rim_feat, feat_taps, feat_bias, doc_offset)
    conv_proj = causal_taps(state_proj, rim_proj, proj_taps, proj_bias, doc_offset)
    step_all = jax.nn.softplus(step_raw + step_bias[:, None])
    rate_all = step_all * (-jnp.exp(decay_log))[:, None]
    block_rows = min(512, row_count)
    position = jnp.arange(block_rows, dtype=jnp.int32)
    causal = position[None, :] <= position[:, None]
    final_row = block_rows - 1
    element_decay = jnp.ones((head_count,), jnp.float32)
    element_state = jnp.zeros((head_count, head_dim, state_size), jnp.float32)
    block_index = 0
    start = block_index * block_rows
    feat_block = conv_feat.reshape(block_rows, head_count, head_dim)
    in_block = conv_proj[start : start + block_rows, :state_size]
    out_block = conv_proj[start : start + block_rows, state_size:]
    cumulative = jnp.cumsum(rate_all, axis=1)
    same_doc = causal & (doc_offset[:, None] >= position[:, None] - position[None, :])
    scores = jnp.dot(out_block, in_block.T, preferred_element_type=jnp.float32)
    exponent_gap = jnp.where(
        same_doc[None], cumulative[:, :, None] - cumulative[:, None, :], -jnp.inf
    )
    weights = (scores[None] * jnp.exp(exponent_gap) * step_all[:, None, :]).astype(jnp.bfloat16)
    inner_out = jnp.einsum("hts,shp->thp", weights, feat_block, preferred_element_type=jnp.float32)
    reaches = doc_offset >= position + 1
    tail_mask = doc_offset[final_row] >= final_row - position
    tail_coef = jnp.where(
        tail_mask[None, :],
        jnp.exp(cumulative[:, final_row : final_row + 1] - cumulative) * step_all,
        0.0,
    )
    scaled = (in_block.astype(jnp.float32)[None] * tail_coef[:, :, None]).astype(jnp.bfloat16)
    contrib = jnp.einsum("shp,hsn->hpn", feat_block, scaled, preferred_element_type=jnp.float32)
    keep_factor = jnp.where(reaches[final_row], jnp.exp(cumulative[:, final_row]), 0.0)
    saved_blocks = [(feat_block, out_block, cumulative, reaches, inner_out, contrib, keep_factor)]
    element_state = keep_factor[:, None, None] * element_state + contrib
    element_decay = element_decay * keep_factor
    longest_doc = row_count * lax.axis_size("ctx") // 4
    span_back = (longest_doc + row_count - 2) // row_count
    distances = [1]
    window_size = 1
    while window_size < span_back:
        distances.append(window_size)
        window_size = window_size * 2
    current = (element_decay, element_state)
    for turn_index, distance in enumerate(distances):
        moved = passed_along((current[0], current[1]), "ctx", distance)
        if turn_index == 0:
            current = moved
        else:
            current = combine_states(moved, current)
    start_state = current[1]
    pieces_out = []
    for block_index, saved in enumerate(saved_blocks):
        feat_block, out_block, cumulative, reaches, inner_out, contrib, keep_factor = saved
        lift_factor = jnp.where(reaches[None, :], jnp.exp(cumulative), 0.0)
        from_state = (
            jnp.einsum(
                "tn,hpn->thp",
                out_block.astype(jnp.float32),
                start_state,
                precision=lax.Precision.HIGHEST,
            )
            * lift_factor.T[:, :, None]
        )
        pieces_out.append(
            inner_out + from_state + skip_gain[None, :, None] * feat_block.astype(jnp.float32)
        )
    mixed = pieces_out[0].reshape(row_count, head_count * head_dim)
    gated = mixed * jax.nn.silu(gate_in.astype(jnp.float32))
    squares = jnp.sum(gated * gated, axis=1)
    total_squares = lax.psum(squares, "head")
    scale = lax.rsqrt(total_squares / (head_count * head_dim * lax.axis_size("head")) + 1e-05)
    return (gated * scale[:, None] * norm_gain[None, :]).astype(jnp.bfloat16)


PAIR = 2
HOLD = 0
AHEAD = 2
EARLY = 4
STRIPE = 32

LOG2E = 1.4426950408889634
F32 = jnp.float32
BF16 = jnp.bfloat16


def to_column(row, size):
    rows = lax.broadcasted_iota(jnp.int32, (size, size), 0)
    cols = lax.broadcasted_iota(jnp.int32, (size, size), 1)
    return jnp.sum(jnp.where(rows == cols, row, 0.0), axis=1, keepdims=True)


def tap_sum(window_of, taps, bias, offsets, tap_count):
    summed = bias
    for tap_index in range(tap_count):
        tap_lag = tap_count - 1 - tap_index
        term = taps[tap_index : tap_index + 1, :] * window_of(tap_lag)
        if tap_lag:
            term = jnp.where(offsets >= float(tap_lag), term, 0.0)
        summed = summed + term
    return summed * (1.0 / (1.0 + jnp.exp(-summed)))


def running_sum(values, upper):
    first = values.astype(BF16)
    left = values - first.astype(F32)
    second = left.astype(BF16)
    third = (left - second.astype(F32)).astype(BF16)
    count = values.shape[0]
    sums = jnp.dot(jnp.concatenate([first, second, third], axis=0), upper, preferred_element_type=F32)
    return sums[:count] + sums[count : 2 * count] + sums[2 * count :]


def mixer_kernel(
    ctx_size, head_size, pair,
    feat_hbm, gate_hbm, proj_hbm, step_hbm, offset_hbm, taps_hbm, bias_hbm,
    ptaps_hbm, pbias_hbm, sbias_hbm, dlog_hbm, skip_hbm,
    gated, scale_ref,
    step_ref, offset_ref, taps_ref, bias_ref, ptaps_ref, pbias_ref, sbias_ref, dlog_ref, skip_ref,
    feat, gate, proj, xs, xp, rim, conv, in_t, bc, out_b, masked, cb, a_rows, coef, coef_top,
    offs, skips, own, send, arecv, srecv, sout, lsend, lrecv, kown, kmate, kprev,
    top, tin, ext, xt, yv, g2, part, sq, sqr, tail, tail_proj, tail_half, tail_sems,
    small_sems, feat_sems, halo_recv, keep_recv, top_recv, arecv_sem, srecv_sem, lrecv_sem, sqrecv,
):
    d = lax.axis_index("ctx")
    hd = lax.axis_index("head")
    rows, cols = feat.shape
    heads = step_ref.shape[0]
    hdim = cols // heads
    state = in_t.shape[0]
    taps_n = taps_ref.shape[0]
    edge = taps_n - 1
    width = pair * hdim
    chunks = heads // pair
    half = rows // 2
    odd = d % 2 == 1
    even = d % 2 == 0
    parity = d % 2
    first_core = hd % 2 == 0
    mate = d + 1 - 2 * parity
    part_heads = heads // 2
    part_chunks = chunks // 2
    mine = parity * part_heads
    theirs = part_heads - mine
    cross = pair if part_heads > 2 * pair else 0
    single = part_heads - cross
    single_chunks = single // pair
    moved = single + 2 * cross
    moved_chunks = moved // pair
    sends_early = even | (d + 1 < ctx_size)
    gets_early = odd | (d + 2 < ctx_size)
    sends_late = even | (d >= 2)
    gets_late = odd | (d >= 2)

    halo_send, keep_send, top_send = small_sems.at[0], small_sems.at[pl.ds(1, 2)], small_sems.at[pl.ds(3, 2)]
    asend, ssend, fsend, sqsend = (small_sems.at[n] for n in range(5, 9))
    gate_sem = small_sems.at[9]

    def cols_of(h, count):
        return pl.ds(pl.multiple_of(h * hdim, hdim), count * hdim)

    def chunk_cols(c):
        return pl.ds(pl.multiple_of(c * width, width), width)

    def feat_copy(c):
        return pltpu.make_async_copy(feat_hbm.at[:, chunk_cols(c)], feat.at[:, chunk_cols(c)], feat_sems.at[c])

    gate_copy = pltpu.make_async_copy(gate_hbm, gate, gate_sem)

    def remote(src, dst, ssem, rsem, where):
        return pltpu.make_async_remote_copy(
            src_ref=src, dst_ref=dst, send_sem=ssem, recv_sem=rsem,
            device_id=where, device_id_type=pl.DeviceIdType.MESH,
        )

    barrier = pltpu.get_barrier_semaphore()
    for shift in (-2, -1, 1, 2):
        @pl.when((d + shift >= 0) & (d + shift < ctx_size))
        def _():
            pl.semaphore_signal(barrier, inc=1, device_id=(d + shift, hd), device_id_type=pl.DeviceIdType.MESH)
    for k in range(1, head_size):
        pl.semaphore_signal(
            barrier, inc=1, device_id=(d, lax.rem(hd + k, head_size)), device_id_type=pl.DeviceIdType.MESH
        )

    def cross_chunk(j):
        return j * part_chunks + single_chunks

    def ordered(i):
        if i < single_chunks:
            return mine // pair + i
        if i < moved_chunks:
            return cross_chunk(i - single_chunks)
        return theirs // pair + i - moved_chunks

    tail_copies = [
        pltpu.make_async_copy(feat_hbm.at[pl.ds(rows - 8, 8), :], tail, tail_sems.at[0]),
        pltpu.make_async_copy(proj_hbm.at[pl.ds(rows - 8, 8), :], tail_proj, tail_sems.at[1]),
    ]
    for copy in tail_copies:
        copy.start()
    small = [
        pltpu.make_async_copy(src, dst, small_sems.at[n])
        for n, (src, dst) in enumerate((
            (offset_hbm, offset_ref), (step_hbm, step_ref), (sbias_hbm, sbias_ref), (dlog_hbm, dlog_ref),
            (ptaps_hbm, ptaps_ref), (pbias_hbm, pbias_ref), (proj_hbm, proj), (taps_hbm, taps_ref),
            (bias_hbm, bias_ref), (skip_hbm, skip_ref),
        ))
    ]
    for copy in small:
        copy.start()
    for c in range(chunks):
        feat_copy(ordered(c)).start()

    xs[:8, :] = jnp.zeros((8, cols), F32)
    xp[:8, :] = jnp.zeros((8, 2 * state), F32)
    part[...] = jnp.zeros_like(part)

    upper = (
        lax.broadcasted_iota(jnp.int32, (rows, rows), 0) <= lax.broadcasted_iota(jnp.int32, (rows, rows), 1)
    ).astype(F32).astype(BF16)
    for copy in small[:4]:
        copy.wait()
    offset_row = offset_ref[...].astype(F32)
    offs[...] = jnp.broadcast_to(to_column(offset_row, rows), offs.shape)
    step = jax.nn.softplus(step_ref[...] + to_column(sbias_ref[...], heads))
    rate = step * (-jnp.exp(to_column(dlog_ref[...], heads)) * LOG2E)
    cum = running_sum(rate, upper)
    shifted = cum - jnp.log(step) * LOG2E
    a_rows[...] = shifted
    last = offset_row[:, rows - 1 : rows]
    place = lax.broadcasted_iota(jnp.int32, (heads, rows), 1)
    reach = rows - 1 - place
    weight = jnp.where(last >= reach.astype(F32), jnp.exp2(cum[:, rows - 1 : rows] - shifted), 0.0)
    coef[...] = jnp.where(place >= edge, weight, 0.0)
    coef_top[...] = weight[:, :hdim]
    keep = jnp.where(last >= float(rows), jnp.exp2(cum[:, rows - 1 : rows]), 0.0)
    kown[...] = jnp.broadcast_to(keep, kown.shape)

    for copy in tail_copies:
        copy.wait()
    tail_half[:, cols // 2 :] = tail_proj[...]
    tail_half[:, : cols // 2] = jnp.concatenate(
        [tail[:, : cols // 2].astype(F32)[4:], tail[:, cols // 2 :].astype(F32)[4:]], axis=0
    ).astype(BF16)
    def proj_taps(rows_from, rows_to, cs):
        return tap_sum(
            lambda lag: xp[8 + rows_from - lag : 8 + rows_to - lag, cs], ptaps_ref[:, cs], pbias_ref[:, cs],
            offs[rows_from:rows_to, :1], taps_n,
        ).astype(BF16)

    in_cols, out_cols = slice(0, state), slice(state, 2 * state)
    for copy in small[4:]:
        copy.wait()
    xp[8:, :] = proj[...].astype(F32)
    bc[:, in_cols] = proj_taps(0, rows, in_cols)
    in_t[...] = bc[:, in_cols].astype(F32).T
    near = jnp.minimum(d, 2) + jnp.minimum(ctx_size - 1 - d, 2) + head_size - 1
    pl.semaphore_wait(barrier, near)
    gate_copy.start()
    halo = remote(tail_half, rim, halo_send, halo_recv, (d + 1, hd))
    keep_on = remote(kown, kprev, keep_send.at[0], keep_recv.at[0], (d + 1, hd))
    keep_back = remote(kown, kmate, keep_send.at[1], keep_recv.at[1], (d - 1, hd))
    top_one = remote(top, tin.at[0], top_send.at[0], top_recv.at[0], (d + 1, hd))
    top_two = remote(top, tin.at[1], top_send.at[1], top_recv.at[1], (d + 2, hd))

    @pl.when(d + 1 < ctx_size)
    def _():
        halo.start()
        keep_on.start()

    @pl.when(odd)
    def _():
        keep_back.start()

    def conv_all(c):
        feat_copy(c).wait()
        sl = chunk_cols(c)
        xs[8:, sl] = feat[:, sl].astype(F32)
        conv[:, sl] = tap_sum(
            lambda lag: xs[8 - lag : 8 + rows - lag, sl], taps_ref[:, sl], bias_ref[:, sl], offs[:, :1], taps_n
        ).astype(BF16)

    def conv_head(h):
        sl = cols_of(h, 1)
        xs[8:, sl] = feat[:, sl].astype(F32)
        conv[:, sl] = tap_sum(
            lambda lag: xs[8 - lag : 8 + rows - lag, sl], taps_ref[:, sl], bias_ref[:, sl], offs[...], taps_n
        ).astype(BF16)

    def a_copy(r):
        return remote(send.at[r], arecv.at[r], asend, arecv_sem.at[r], (mate, hd))

    def direct_copy(r):
        return remote(send.at[r], srecv.at[r], ssend, srecv_sem.at[r], (d + 2, hd))

    def s_copy(r):
        return remote(sout.at[r], srecv.at[r], ssend, srecv_sem.at[r], (d + 2, hd))

    def late_sem(r):
        whole = single - pair
        return lrecv_sem.at[jnp.where(r < whole, r // pair, whole // pair + r - whole)]

    def f_copy(r):
        return remote(lsend.at[r], lrecv.at[r], fsend, late_sem(r), (mate, hd))

    def g_copy(r):
        return remote(srecv.at[r], lrecv.at[r], fsend, late_sem(r), (mate, hd))

    def contrib(h):
        scaled = (in_t[...] * coef[pl.ds(h, 1), :]).astype(BF16)
        return jnp.dot(scaled, conv[:, cols_of(h, 1)], preferred_element_type=F32)

    def held_back(i):
        @pl.when((i >= 0) & (i < moved_chunks) & sends_early & jnp.logical_not(first_core))
        def _():
            for k in range(pair):
                a_copy(i * pair + k).start()

    def sent(c, slot, keeps):
        feat_copy(c).wait()
        for k in range(pair):
            r = slot * pair + k
            conv_head(c * pair + k)
            got = contrib(c * pair + k)
            send[r] = got.astype(BF16)
            if keeps:
                own[r] = got

            @pl.when(sends_early & first_core)
            def _():
                a_copy(r).start()

            if keeps:
                @pl.when(odd & (d + 2 < ctx_size))
                def _():
                    direct_copy(r).start()

        held_back(slot - HOLD)

    def mine_body(i, _):
        sent(mine // pair + i, i, False)
        return 0

    def cross_body(i, _):
        sent(cross_chunk(i), single_chunks + i, True)
        return 0

    def theirs_body(i, _):
        held_back(moved_chunks + i - HOLD)
        conv_all(theirs // pair + i)
        for k in range(pair):
            r = i * pair + k
            own[r] = contrib(theirs + r)

        @pl.when(odd & (i >= 1) & (i <= AHEAD))
        def _():
            relay(i - 1)

        return 0

    lax.fori_loop(0, single_chunks, mine_body, 0)
    lax.fori_loop(0, moved_chunks - single_chunks, cross_body, 0)

    @pl.when(d == 0)
    def _():
        rim[...] = jnp.zeros_like(rim)
        lrecv[...] = jnp.zeros_like(lrecv)
        kprev[...] = jnp.zeros_like(kprev)
        tin[0] = jnp.zeros(tin.shape[1:], BF16)

    @pl.when(d < 2)
    def _():
        srecv[...] = jnp.zeros_like(srecv)
        tin[1] = jnp.zeros(tin.shape[1:], BF16)


    @pl.when(d > 0)
    def _():
        keep_on.wait_recv()

    @pl.when(even)
    def _():
        keep_back.wait_recv()

    def relay(r):
        h = theirs + r

        @pl.when(gets_early)
        def _():
            a_copy(r).wait_recv()

        @pl.when((d + 2 < ctx_size) & even)
        def _():
            sout[r] = (arecv[r].astype(F32) + kmate[pl.ds(h, 1), :] * own[r]).astype(BF16)
            s_copy(r).start()

        @pl.when((d + 2 < ctx_size) & odd)
        def _():
            sout[r] = (own[r] + kown[pl.ds(h, 1), :] * arecv[r].astype(F32)).astype(BF16)
            s_copy(r).start()

    def pass_on(r):
        @pl.when(d >= 2)
        def _():
            s_copy(r).wait_recv()

        @pl.when(even)
        def _():
            lsend[r] = (own[r] + kown[pl.ds(theirs + r, 1), :] * srecv[r].astype(F32)).astype(BF16)
            f_copy(r).start()

        @pl.when(odd & (d >= 2))
        def _():
            g_copy(r).start()

    ahead = jnp.where(odd, min(AHEAD, single_chunks - 1), 0)
    lax.fori_loop(0, single_chunks, theirs_body, 0)
    cum_t = cum.T

    def spread(some):
        for h in some:
            cb[h] = jnp.broadcast_to(cum_t[:, h : h + 1], (rows, hdim))

    fill = [lambda: spread(range(part_heads)), lambda: spread(range(part_heads, heads))]
    ready = len(fill)
    for r in range(ready):
        relay(ahead + r)
        fill[r]()
    skips[...] = jnp.broadcast_to(to_column(skip_ref[...], heads), skips.shape)

    @pl.when(d > 0)
    def _():
        halo.wait_recv()

    xp[:8, :] = rim[:, cols // 2 :].astype(F32)
    bc[:16, in_cols] = proj_taps(0, 16, in_cols)
    out_b[...] = proj_taps(0, rows, out_cols)
    for c in range(cols // 512):
        sl = slice(c * 512, (c + 1) * 512)
        first = c * 512 < cols // 2
        arrived = rim[:, (c * 512) % (cols // 2) : (c * 512) % (cols // 2) + 512].astype(F32)
        xs[:8, sl] = jnp.concatenate([arrived[:4], arrived[:4]], axis=0) if first else arrived
        conv[:16, sl] = tap_sum(
            lambda lag: xs[8 - lag : 24 - lag, sl], taps_ref[:, sl], bias_ref[:, sl], offs[:16, :1], taps_n
        ).astype(BF16)
    weight_t = coef_top[...].T[:8, :]
    row_id = lax.broadcasted_iota(jnp.int32, weight_t.shape, 0)
    weight_t = jnp.where(row_id < edge, weight_t, 0.0)
    in_top = bc[:8, :state].astype(F32)
    top[:, :state] = jnp.concatenate([in_top[:4], in_top[:4]], axis=0).astype(BF16)
    for r in range(part_heads):
        rows_of = [
            (conv[:8, h * hdim : (h + 1) * hdim].astype(F32) * weight_t[:, h : h + 1])[:4] for h in (r, part_heads + r)
        ]
        top[:, state + r * hdim : state + (r + 1) * hdim] = jnp.concatenate(rows_of, axis=0).astype(BF16)

    @pl.when(d + 1 < ctx_size)
    def _():
        top_one.start()

    @pl.when(d + 2 < ctx_size)
    def _():
        top_two.start()

    in_b = bc[...]
    scores = lax.dot_general(out_b[...], in_b, (((1,), (1,)), ((), ())), preferred_element_type=F32)
    ti = lax.broadcasted_iota(jnp.int32, (rows, rows), 0)
    si = lax.broadcasted_iota(jnp.int32, (rows, rows), 1)
    gap = ti - si
    masked[...] = jnp.where((gap >= 0) & (offs[:, :1] >= gap.astype(F32)), scores, 0.0)

    def local_part(h):
        for _ in range(1):
            fcols = cols_of(h, 1)
            arow = a_rows[pl.ds(h, 1), :]
            cbv = cb[h]
            w0 = (jnp.exp2(jnp.minimum(cbv - arow[:, :half], 126.0)) * masked[:, :half]).astype(BF16)
            w1 = (jnp.exp2(jnp.minimum(cbv[half:] - arow[:, half:], 126.0)) * masked[half:, half:]).astype(BF16)
            fv = conv[:, fcols]
            first = jnp.dot(w0, fv[:half], preferred_element_type=F32)
            second = jnp.dot(w1, fv[half:], preferred_element_type=F32)
            inner = jnp.concatenate([first[:half], first[half:] + second], axis=0)
            gv = gate[:, fcols].astype(F32)
            sg = gv * (1.0 / (1.0 + jnp.exp(-gv)))
            yv[:, fcols] = (inner + skips[pl.ds(h, 1), :] * fv.astype(F32)) * sg
            tpos = lax.broadcasted_iota(jnp.int32, (rows, hdim), 0)
            lift = jnp.where(offs[...] >= (tpos + 1).astype(F32), jnp.exp2(cbv), 0.0)
            g2[:, fcols] = lift * sg

    def early_terms():
        @pl.when(d > 0)
        def _():
            top_one.wait_recv()

        @pl.when(d > 1)
        def _():
            top_two.wait_recv()

        firsts = jnp.concatenate([tin[0, :, :state], tin[1, :, :state]], axis=0)
        marks = lax.dot_general(out_b[...], firsts, (((1,), (1,)), ((), ())), preferred_element_type=F32)
        lane = lax.broadcasted_iota(jnp.int32, marks.shape, 1) % 8
        ext[0] = jnp.where(lane < 4, marks, 0.0).astype(BF16)
        ext[1] = jnp.where(lane < 4, 0.0, marks).astype(BF16)
        near_rows = lax.broadcasted_iota(jnp.int32, (8, hdim), 0)
        for r in range(part_heads):
            cs = slice(state + r * hdim, state + (r + 1) * hdim)
            decay = jnp.where(near_rows < 4, kprev[r : r + 1, :], kprev[part_heads + r : part_heads + r + 1, :])
            xt[:, r * hdim : (r + 1) * hdim] = jnp.concatenate(
                [tin[0, :, cs].astype(F32), tin[1, :, cs].astype(F32) * decay], axis=0
            ).astype(BF16)

    def finish(side, r, st, count=pair):
        sl = cols_of(side * part_heads + r, count)
        fs = jnp.dot(out_b[...], st, preferred_element_type=F32)
        fs = fs + jnp.dot(ext[side], xt[:, cols_of(r, count)], preferred_element_type=F32)
        gt = yv[:, sl] + fs * g2[:, sl]
        gated[:, sl] = gt.astype(gated.dtype)
        squares = gt * gt
        total = squares[:, :hdim]
        for k in range(1, count):
            total = total + squares[:, k * hdim : (k + 1) * hdim]
        part[...] += total

    def finish_received(r, side_even, side_odd, row):
        @pl.when(even)
        def _():
            finish(side_even, row, jnp.concatenate([srecv[r + k] for k in range(pair)], axis=1))

        @pl.when(odd)
        def _():
            finish(side_odd, row, jnp.concatenate([
                (
                    arecv[r + k].astype(F32)
                    + kprev[side_odd * part_heads + row + k : side_odd * part_heads + row + k + 1, :]
                    * srecv[r + k].astype(F32)
                ).astype(BF16)
                for k in range(pair)
            ], axis=1))

    begun = ahead + ready
    early = min(EARLY, single)

    def first_body(i, _):
        relay(i)
        local_part(i - begun)
        return 0

    def both_body(i, _):
        local_part(i - begun)
        pass_on(i - early)
        relay(i)
        return 0

    def cross_relay(x):
        r = single + x

        @pl.when(gets_early)
        def _():
            a_copy(r).wait_recv()

        @pl.when((d + 2 < ctx_size) & even)
        def _():
            h = x // pair * part_heads + single + x % pair
            sout[r] = (arecv[r].astype(F32) + kmate[pl.ds(h, 1), :] * own[r]).astype(BF16)
            s_copy(r).start()

    def second_body(i, _):
        for k in range(2):
            h = single - begun + 2 * (i - single + early) + k

            @pl.when(h < heads)
            def _():
                local_part(h)

            if k == 0:
                pass_on(i)

        x = i - single + early

        @pl.when(x < moved - single)
        def _():
            cross_relay(x)

        return 0

    def left_body(h, _):
        local_part(h)
        return 0

    gate_copy.wait()
    lax.fori_loop(begun, early, first_body, 0)
    lax.fori_loop(early, single, both_body, 0)
    lax.fori_loop(single - early, single, second_body, 0)
    lax.fori_loop(single - begun + 2 * early, heads, left_body, 0)
    for x in range(early, moved - single):
        cross_relay(x)
    early_terms()
    for r in range(0, single, pair):
        finish_received(r, 1, 0, r)

    for j in range(single_chunks):
        r = j * pair

        if j == single_chunks - 1:
            for x in range((moved - single) // pair):
                at = single + x * pair

                @pl.when(d >= 2)
                def _():
                    for k in range(pair):
                        s_copy(at + k).wait_recv()

                finish_received(at, x, x, single)

            for k in range(pair):
                @pl.when(gets_late)
                def _():
                    f_copy(r + k).wait_recv()

                finish(parity, r + k, lrecv[r + k], 1)
        else:
            @pl.when(gets_late)
            def _():
                some = pl.ds(r, pair)
                remote(lsend.at[some], lrecv.at[some], fsend, lrecv_sem.at[j], (mate, hd)).wait_recv()

            finish(parity, r, jnp.concatenate([lrecv[r + k] for k in range(pair)], axis=1))

    sq[...] = jnp.sum(part[...].T, axis=0, keepdims=True)

    def sq_copy(k):
        return remote(
            sq, sqr.at[k - 1], sqsend, sqrecv.at[k - 1], (d, lax.rem(hd + k, head_size))
        )

    far_first = sorted(range(1, head_size), key=lambda k: (k != head_size // 2, k))
    for k in far_first:
        sq_copy(k).start()

    @pl.when(d + 1 < ctx_size)
    def _():
        halo.wait_send()
        keep_on.wait_send()
        top_one.wait_send()

    @pl.when(d + 2 < ctx_size)
    def _():
        top_two.wait_send()

    @pl.when(odd)
    def _():
        keep_back.wait_send()

    @pl.when(sends_early)
    def _():
        remote(send, arecv, asend, arecv_sem.at[0], (mate, hd)).wait_send()

    @pl.when(d + 2 < ctx_size)
    def _():
        remote(send, srecv, ssend, srecv_sem.at[0], (d + 2, hd)).wait_send()

    @pl.when(sends_late)
    def _():
        remote(lsend, lrecv, fsend, lrecv_sem.at[0], (mate, hd)).wait_send()

    total = sq[...]
    for k in range(1, head_size):
        sq_copy(k).wait_recv()
        total = total + sqr[k - 1]
    scale = lax.rsqrt(total / (cols * head_size) + 1e-05)
    scale_ref[...] = jnp.broadcast_to(scale, (hdim, rows)).T
    remote(sqr, sqr, sqsend, sqrecv.at[0], (d, lax.rem(hd + 1, head_size))).wait_send()


def scale_kernel(gated_ref, scale_ref, gain_ref, out_hbm, staged, sems):
    rows, cols = staged.shape
    lanes = scale_ref.shape[1]
    stripe = min(STRIPE, rows)

    def out_copy(r):
        rs = pl.ds(r * stripe, stripe)
        return pltpu.make_async_copy(staged.at[rs, :], out_hbm.at[rs, :], sems.at[r])

    for r in range(rows // stripe):
        rs = slice(r * stripe, (r + 1) * stripe)
        scale = scale_ref[rs, :]
        for c in range(cols // lanes):
            cs = slice(c * lanes, (c + 1) * lanes)
            staged[rs, cs] = (gated_ref[rs, cs].astype(F32) * scale * gain_ref[:, cs]).astype(BF16)
        out_copy(r).start()
    for r in range(rows // stripe):
        out_copy(r).wait()


def finish_call(gated, scale, gain):
    rows, cols = gated.shape
    vm = pl.BlockSpec(memory_space=pltpu.VMEM)
    return pl.pallas_call(
        scale_kernel,
        out_shape=jax.ShapeDtypeStruct((rows, cols), BF16),
        in_specs=[vm, vm, vm],
        out_specs=pl.BlockSpec(memory_space=pltpu.HBM),
        scratch_shapes=[
            pltpu.VMEM((rows, cols), BF16), pltpu.SemaphoreType.DMA((rows // min(STRIPE, rows),)),
        ],
        compiler_params=pltpu.CompilerParams(vmem_limit_bytes=8 << 20),
        name="scale",
    )(gated, scale, gain)


def short_body(
    feat_in, gate_in, state_proj, step_raw, doc_offset, feat_taps, feat_bias,
    proj_taps, proj_bias, step_bias, decay_log, skip_gain, norm_gain,
):
    heads, rows = step_raw.shape
    cols = feat_in.shape[1]
    hdim = cols // heads
    state = state_proj.shape[1] // 2
    taps = feat_taps.shape[0]
    ctx_size = lax.axis_size("ctx")
    head_size = lax.axis_size("head")
    pair = PAIR
    chunks = heads // pair
    some = heads // 2
    vm = pl.BlockSpec(memory_space=pltpu.VMEM)
    hbm = pl.BlockSpec(memory_space=pltpu.HBM)
    V = pltpu.VMEM
    DMA = pltpu.SemaphoreType.DMA
    cross = pair if some > 2 * pair else 0
    single = some - cross
    moved = single + 2 * cross
    late_piece = (single, state, hdim)
    piece = (moved, state, hdim)
    operands = (
        feat_in, gate_in, state_proj, step_raw, doc_offset[None, :], feat_taps,
        feat_bias[None, :], proj_taps, proj_bias[None, :], step_bias[None, :], decay_log[None, :], skip_gain[None, :],
    )
    gated, scale = pl.pallas_call(
        functools.partial(mixer_kernel, ctx_size, head_size, pair),
        out_shape=(
            jax.ShapeDtypeStruct((rows, cols), BF16),
            jax.ShapeDtypeStruct((rows, hdim), F32),
        ),
        in_specs=[hbm] * len(operands),
        out_specs=(vm, vm),
        scratch_shapes=[
            V((heads, rows), F32), V((1, rows), jnp.int32), V((taps, cols), F32), V((1, cols), F32),
            V((taps, 2 * state), F32), V((1, 2 * state), F32), V((1, heads), F32), V((1, heads), F32),
            V((1, heads), F32),
            V((rows, cols), BF16), V((rows, cols), BF16), V((rows, 2 * state), BF16),
            V((rows + 8, cols), F32), V((rows + 8, 2 * state), F32),
            V((8, cols // 2 + 2 * state), BF16), V((rows, cols), BF16),
            V((state, rows), F32), V((rows, state), BF16), V((rows, state), BF16), V((rows, rows), F32),
            V((heads, rows, hdim), F32), V((heads, rows), F32), V((heads, rows), F32), V((heads, hdim), F32),
            V((rows, hdim), F32), V((heads, hdim), F32),
            V(piece, F32), V(piece, BF16), V(piece, BF16), V(piece, BF16), V(piece, BF16), V(late_piece, BF16),
            V(late_piece, BF16),
            V((heads, hdim), F32), V((heads, hdim), F32), V((heads, hdim), F32),
            V((8, state + cols // 2), BF16), V((2, 8, state + cols // 2), BF16), V((2, rows, 16), BF16),
            V((16, cols // 2), BF16),
            V((rows, cols), F32), V((rows, cols), F32), V((rows, hdim), F32),
            V((1, rows), F32), V((head_size - 1, 1, rows), F32), V((8, cols), BF16), V((8, 2 * state), BF16),
            V((8, cols // 2 + 2 * state), BF16), DMA((2,)),
            DMA((10,)), DMA((chunks,)), DMA, DMA((2,)), DMA((2,)),
            DMA((moved,)), DMA((moved,)), DMA((single // pair + pair - 1,)), DMA((head_size - 1,)),
        ],
        compiler_params=pltpu.CompilerParams(collective_id=0, has_side_effects=True, vmem_limit_bytes=40 << 20),
        name="mixer",
    )(*[pltpu.with_memory_space_constraint(operand, pltpu.HBM) for operand in operands])
    return finish_call(gated, scale, norm_gain[None, :])


def solution(mesh):
    ctx_size = mesh.shape["ctx"]

    def chosen(*args):
        row_count = args[0].shape[0]
        longest_doc = row_count * ctx_size // 4
        span_back = (longest_doc + row_count - 2) // row_count
        if span_back == 2 and ctx_size % 2 == 0:
            return short_body(*args)
        return body(*args)

    return jax.shard_map(
        chosen,
        mesh=mesh,
        in_specs=(
            P("ctx", "head"),
            P("ctx", "head"),
            P("ctx", None),
            P("head", "ctx"),
            P("ctx"),
            P(None, "head"),
            P("head"),
            P(),
            P(),
            P("head"),
            P("head"),
            P("head"),
            P("head"),
        ),
        out_specs=P("ctx", "head"),
        check_vma=False,
    )
```
